256 devices in a mesh: tm: 16 (over z_hi, y), space: 16 (over x, z_lo, core).
Axes of the slice: x: 4, y: 4, z: 8 (z_hi: 4, z_lo: 2; z = z_hi * 2 + z_lo), core: 2. Of those that a mesh axis runs over, the one named last changes fastest.
Arguments:
- snapshots: bfloat16 [3, 4096, 16384], P(None, 'tm', 'space'), may hold values from -6 to 6
- tile_table: int32 [16, 20, 2], P('tm'), may hold values from -1 to 15, as said below
Outputs:
- gram_tiles: float32 [16, 20, 256, 256], P('tm', None, 'space')
The draws below stay inside these ranges and needn't reach their ends.
Inputs may be any that keep to these rules, and one draw needn't show every extreme that they name: `tile_table`: every pair a <= b of block numbers below 16 stands in exactly one slot of the table, with a as row block and b as column block. In each owner's row the filled slots come first and the empty slots, -1 in both entries, last. Some owner has all 20 slots filled; owners may have no tiles.
All inputs are finite; a program needn't handle non-finite values.
Results may differ from the reference program's by a relative error of at most 0.0003.
Values may be sent and summed in bfloat16 or wider, within the bound.
A program may use at most 128 MiB of HBM per device.

```python
import math
import jax
import jax.numpy as jnp
from jax import lax

COMP = 3
SNAP_DEV = 256
MAXT = 20
SNAPS = 4096
CELLS = 16384
N_TM = 16


def draw_tile_table(key, part):
    blocks_count = N_TM
    slot_count = MAXT
    upper_rows, upper_cols = jnp.triu_indices(blocks_count)
    upper_rows = upper_rows.astype(jnp.int32)
    upper_cols = upper_cols.astype(jnp.int32)
    pair_count = blocks_count * (blocks_count + 1) // 2
    key_order = jax.random.fold_in(key, 11)
    key_owner = jax.random.fold_in(key, 12)
    key_moves = jax.random.fold_in(key, 13)
    order = jax.random.permutation(key_order, pair_count).astype(jnp.int32)
    owners = jax.random.permutation(key_owner, blocks_count).astype(jnp.int32)
    remain = pair_count - slot_count
    quota = remain // (blocks_count - 1)
    extra = remain % (blocks_count - 1)
    others_count = (jnp.arange(blocks_count - 1, dtype=jnp.int32) < extra).astype(jnp.int32) + quota
    pair_moves = (blocks_count - 1) // 2
    moves = jax.random.randint(key_moves, (pair_moves,), 0, quota + 1).astype(jnp.int32)
    others_count = others_count.at[0:2 * pair_moves:2].add(-moves)
    others_count = others_count.at[1:2 * pair_moves:2].add(moves)
    counts = jnp.zeros((blocks_count,), jnp.int32)
    counts = counts.at[owners[0]].set(slot_count)
    counts = counts.at[owners[1:]].set(others_count)
    starts = jnp.cumsum(counts) - counts
    slot_index = jnp.arange(slot_count, dtype=jnp.int32)
    position = starts[:, None] + slot_index[None, :]
    valid = slot_index[None, :] < counts[:, None]
    chosen = order[jnp.clip(position, 0, pair_count - 1)]
    row_block = jnp.where(valid, upper_rows[chosen], -1)
    col_block = jnp.where(valid, upper_cols[chosen], -1)
    return jnp.stack([row_block, col_block], axis=-1).astype(jnp.int32)


def shard_levels(own_key, shape, split, least, top_value):
    level, own = 1.0, jax.random.fold_in(own_key, 6)
    for dim, blocks in split:
        steps = jnp.exp(jax.random.uniform(jax.random.fold_in(own, dim), (blocks,), jnp.float32, least / len(split), top_value / len(split)))
        level = level * jnp.repeat(steps, shape[dim] // blocks).reshape([-1 if axis == dim else 1 for axis in range(len(shape))])
    return level


def centred(key, shape, scale, bound, split=(), held_as=jnp.bfloat16):
    drawn = jax.random.normal(key, shape, jnp.float32) * scale
    if len(split) > 0:
        drawn = shard_levels(key, shape, split, -0.22, 0.18) * drawn
    return jnp.clip(drawn, min=-bound, max=bound).astype(held_as)


def setup_inputs(seed: int = 0) -> dict:
    splits = jax.random.split(jax.random.key(seed), 3)
    snapshots = centred(splits[0], (COMP, SNAPS, CELLS), 1.0, 6.0, ((1, 16), (2, 16)))
    tile_table = draw_tile_table(jax.random.fold_in(splits[2], 71), 0)
    return dict(snapshots=snapshots, tile_table=tile_table)


def reference(snapshots, tile_table):
    scale_factor = 1.0 / math.sqrt(COMP * CELLS)
    values = snapshots.astype(jnp.float32)
    flat = jnp.transpose(values, (1, 0, 2)).reshape(SNAPS, COMP * CELLS)
    gram = jnp.dot(flat, flat.T, precision=lax.Precision.HIGHEST, preferred_element_type=jnp.float32)
    gram = gram * scale_factor
    blocked = gram.reshape(N_TM, SNAP_DEV, N_TM, SNAP_DEV)
    row_block = tile_table[:, :, 0]
    col_block = tile_table[:, :, 1]
    valid = row_block >= 0
    row_safe = jnp.maximum(row_block, 0).astype(jnp.int32)
    col_safe = jnp.maximum(col_block, 0).astype(jnp.int32)
    tiles = blocked[row_safe, :, col_safe, :]
    zeros_tile = jnp.zeros_like(tiles)
    return jnp.where(valid[:, :, None, None], tiles, zeros_tile)
```

```python
import math

import jax
import jax.numpy as jnp
from jax import lax
from jax.experimental import pallas as pl
from jax.experimental.pallas import tpu as pltpu
from jax.sharding import PartitionSpec as P

MESH = pl.DeviceIdType.MESH
BLOCK = 256
SIDE = 4
TILES = 34
BATCHES = (8, 9, 9, 8)


def pick(index, values):
    chosen = values[0]
    for place in range(1, len(values)):
        chosen = jnp.where(index == place, values[place], chosen)
    return chosen


def tile_list(h, y):
    z = [lax.rem(h + step, SIDE) for step in range(SIDE)]
    same, near, far = y, lax.rem(y + 1, SIDE), lax.rem(y + 2, SIDE)

    def make(z1, y1, z2, y2, tile):
        first = z1 * SIDE + y1 <= z2 * SIDE + y2
        one, two = y1 * SIDE + z1, y2 * SIDE + z2
        return (jnp.where(first, one, two), jnp.where(first, two, one), tile)

    def own(a, b):
        step = (b - a) % SIDE
        base = lax.rem(z[a], 2) if step == 2 else z[a]
        return make(z[a], same, z[b], same, 16 + 4 * step + base)

    def side(a, b):
        return make(z[a], same, z[b], near, SIDE * z[a] + z[b])

    def across(a):
        b = (a + 1) % SIDE
        return make(z[a], same, z[b], far, 26 + z[a])

    half = jnp.where(y >= 2, 2, 0)
    return [
        own(0, 0), side(0, 0),
        own(3, 3), own(3, 0), side(0, 3), side(3, 0), side(3, 3), across(3),
        own(1, 1), own(0, 1), own(1, 3), side(1, 1), side(1, 0), side(0, 1), side(1, 3), side(3, 1), across(0),
        own(2, 2), own(1, 2), own(2, 3), own(0, 2), side(2, 0), side(0, 2), side(2, 1), side(1, 2), side(2, 2),
        side(2, 3), side(3, 2), across(1), across(2),
        make(half, same, half, far, 30), make(half + 1, same, half + 1, far, 31),
        make(0, same, 2, far, 32), make(1, same, 3, far, 33),
    ]


def kernel(
    scale, x_ref, out_ref, blocks, relay, part, pair, xfirst, xlast, total, zhalf, zpart,
    local_sem, zs, zr, ys, yr, ps, pr, xs, xr, ws, wr,
):
    tm, space = lax.axis_index("tm"), lax.axis_index("space")
    h, y = tm // SIDE, lax.rem(tm, SIDE)
    x, low, core = space // SIDE, lax.rem(space // 2, 2), lax.rem(space, 2)

    def device(h_=h, y_=y, x_=x, low_=low, core_=core):
        return (h_ * SIDE + y_, x_ * SIDE + low_ * 2 + core_)

    def up(value, step, size=SIDE):
        return lax.rem(value + step, size)

    hp, hm, h2 = up(h, 1), up(h, 3), up(h, 2)
    yp, ym = up(y, 1), up(y, 3)
    xp, xm, x2 = up(x, 1), up(x, 3), up(x, 2)
    other = 1 - core
    place = h * 2 + low
    zp, zm = up(place, 1, 8), up(place, 7, 8)
    dev_hp, dev_hm = device(h_=hp), device(h_=hm)
    dev_yp, dev_ym = device(y_=yp), device(y_=ym)
    dev_xp, dev_xm = device(x_=xp), device(x_=xm)
    dev_zp = device(h_=zp // 2, low_=lax.rem(zp, 2))
    dev_zm = device(h_=zm // 2, low_=lax.rem(zm, 2))
    dev_pair = device(core_=other)

    barrier = pltpu.get_barrier_semaphore()
    peers = (dev_hp, dev_hm, dev_yp, dev_ym, dev_xp, dev_xm, dev_zp, dev_zm, dev_pair)
    for peer in peers:
        pl.semaphore_signal(barrier, inc=1, device_id=peer, device_id_type=MESH)
    pl.semaphore_wait(barrier, len(peers))

    started = []

    def send(src, dst, send_sem, recv_sem, peer):
        copy = pltpu.make_async_remote_copy(
            src_ref=src, dst_ref=dst, send_sem=send_sem, recv_sem=recv_sem, device_id=peer, device_id_type=MESH
        )
        copy.start()
        started.append(copy)
        return copy

    def cells(which):
        return pl.ds(pl.multiple_of(which * BLOCK, BLOCK), BLOCK)

    every = slice(None)
    first_rows, last_rows = pl.ds(0, BLOCK // 2), pl.ds(BLOCK // 2, BLOCK // 2)

    local = pltpu.make_async_copy(x_ref.at[:, :, cells(h)], blocks.at[y, h], local_sem)
    local.start()
    to_hp = send(x_ref.at[:, :, cells(hp)], blocks.at[y, h], zs.at[0], zr.at[0], dev_hp)
    to_hm = send(x_ref.at[:, :, cells(hm)], blocks.at[y, h], zs.at[1], zr.at[1], dev_hm)
    via_hp = send(x_ref.at[:, first_rows, cells(h2)], relay.at[0], zs.at[2], zr.at[2], dev_hp)
    via_hm = send(x_ref.at[:, last_rows, cells(h2)], relay.at[1], zs.at[3], zr.at[3], dev_hm)

    direct, onward = {}, {}

    def spread(key, z):
        down = send(blocks.at[y, z], blocks.at[y, z], ys.at[key, 0], yr.at[key, 0], dev_ym)
        above = send(blocks.at[y, z, pl.ds(1, 2)], blocks.at[y, z, pl.ds(1, 2)], ys.at[key, 1], yr.at[key, 1], dev_yp)
        direct[key] = (down, above)

    def forward(key, z):
        down, above = direct[key]
        down.wait_recv()
        first = send(blocks.at[yp, z, pl.ds(0, 1)], blocks.at[yp, z, pl.ds(0, 1)], ys.at[key, 2], yr.at[key, 2], dev_ym)
        above.wait_recv()
        rest = send(blocks.at[ym, z, pl.ds(1, 2)], blocks.at[ym, z, pl.ds(1, 2)], ys.at[key, 3], yr.at[key, 3], dev_yp)
        onward[key] = (first, rest)

    def gathered(key):
        for copy in onward[key]:
            copy.wait_recv()

    tiles = tile_list(h, y)
    starts = [sum(BATCHES[:number]) for number in range(len(BATCHES))]

    def compute(number):
        begin, size = starts[number], BATCHES[number]
        some = tiles[begin:begin + size]

        @pl.loop(0, size)
        def _(step):
            left = pick(step, [tile[0] for tile in some])
            right = pick(step, [tile[1] for tile in some])
            ly, lz, ry, rz = left // SIDE, lax.rem(left, SIDE), right // SIDE, lax.rem(right, SIDE)
            product = None
            for comp in range(3):
                term = lax.dot_general(
                    blocks[ly, lz, comp], blocks[ry, rz, comp], (((1,), (1,)), ((), ())),
                    preferred_element_type=jnp.float32,
                )
                product = term if product is None else product + term
            slot = begin + step
            for row in range(BLOCK // 8):
                for lane in range(2):
                    place_x, place_low, place_core, place_row = row // 8, row // 4 % 2, row // 2 % 2, row % 2
                    part[slot, place_core, place_x, place_low * 4 + place_row * 2 + lane] = product[
                        row * 8:row * 8 + 8, lane * 128:lane * 128 + 128
                    ]

        span = pl.ds(begin, size)
        return send(part.at[span, other], pair.at[span], ps.at[number], pr.at[number], dev_pair)

    def add_pair(number, copy):
        begin, size = starts[number], BATCHES[number]
        copy.wait_recv()

        @pl.loop(begin, begin + size)
        def _(slot):
            part[slot, core] = part[slot, core] + pair[slot]

        span = pl.ds(begin, size)
        return (
            send(part.at[span, core, x2, pl.ds(0, 4)], xfirst.at[0, span], xs.at[number, 0], xr.at[number, 0], dev_xp),
            send(part.at[span, core, x2, pl.ds(4, 4)], xfirst.at[1, span], xs.at[number, 1], xr.at[number, 1], dev_xm),
        )

    def add_first(number, copies):
        begin, size = starts[number], BATCHES[number]
        for copy in copies:
            copy.wait_recv()

        @pl.loop(begin, begin + size)
        def _(slot):
            part[slot, core, xp, 0:4] = part[slot, core, xp, 0:4] + xfirst[0, slot]
            part[slot, core, xm, 4:8] = part[slot, core, xm, 4:8] + xfirst[1, slot]

        span = pl.ds(begin, size)
        return (
            send(part.at[span, core, xp], xlast.at[0, span], xs.at[number, 2], xr.at[number, 2], dev_xp),
            send(part.at[span, core, xm], xlast.at[1, span], xs.at[number, 3], xr.at[number, 3], dev_xm),
        )

    def add_last(number, copies):
        begin, size = starts[number], BATCHES[number]
        for copy in copies:
            copy.wait_recv()
        some = tiles[begin:begin + size]

        @pl.loop(0, size)
        def _(step):
            slot = begin + step
            total[pick(step, [tile[2] for tile in some])] = part[slot, core, x] + xlast[0, slot] + xlast[1, slot]

    local.wait()
    spread(0, h)
    forward(0, h)
    to_hp.wait_recv()
    spread(1, hm)
    to_hm.wait_recv()
    spread(2, hp)
    via_hp.wait_recv()
    on_hp = send(relay.at[0], blocks.at[y, hm, :, first_rows], zs.at[4], zr.at[4], dev_hp)
    via_hm.wait_recv()
    on_hm = send(relay.at[1], blocks.at[y, hp, :, last_rows], zs.at[5], zr.at[5], dev_hm)
    gathered(0)
    forward(1, hm)
    forward(2, hp)
    on_hp.wait_recv()
    on_hm.wait_recv()
    spread(3, h2)
    gathered(1)
    pair0 = compute(0)
    gathered(2)
    pair1 = compute(1)
    first0 = add_pair(0, pair0)
    forward(3, h2)
    first1 = add_pair(1, pair1)
    last0 = add_first(0, first0)
    last1 = add_first(1, first1)
    gathered(3)
    pair2 = compute(2)
    pair3 = compute(3)
    first2 = add_pair(2, pair2)
    add_last(0, last0)
    first3 = add_pair(3, pair3)
    last2 = add_first(2, first2)
    add_last(1, last1)
    last3 = add_first(3, first3)
    add_last(2, last2)
    add_last(3, last3)

    def piece(step):
        target = up(place, step, 8)
        return lax.rem(target, 2) * 4 + target // 2

    four = piece(4)
    near_half, far_half = pl.ds(0, TILES // 2), pl.ds(TILES // 2, TILES // 2)
    go_up = send(total.at[near_half, four], zhalf.at[0], ws.at[0, 0], wr.at[0, 0], dev_zp)
    go_down = send(total.at[far_half, four], zhalf.at[1], ws.at[1, 0], wr.at[1, 0], dev_zm)
    for step in range(3):
        above, below = piece(3 - step), piece(5 + step)
        go_up.wait_recv()
        if step == 0:
            total[0:TILES // 2, above] = total[0:TILES // 2, above] + zhalf[0]
        else:
            total[:, above] = total[:, above] + zpart[0, step - 1]
        go_up = send(total.at[:, above], zpart.at[0, step], ws.at[0, step + 1], wr.at[0, step + 1], dev_zp)
        go_down.wait_recv()
        if step == 0:
            total[TILES // 2:TILES, below] = total[TILES // 2:TILES, below] + zhalf[1]
        else:
            total[:, below] = total[:, below] + zpart[1, step - 1]
        go_down = send(total.at[:, below], zpart.at[1, step], ws.at[1, step + 1], wr.at[1, step + 1], dev_zm)
    go_up.wait_recv()
    go_down.wait_recv()
    out_ref[...] = (total[:, piece(0)] + zpart[0, 2] + zpart[1, 2]) * scale
    for copy in started:
        copy.wait_send()


def reduced(snapshots, scale):
    count = len(BATCHES)
    dma = pltpu.SemaphoreType.DMA
    f32, b16 = jnp.float32, jnp.bfloat16
    return pl.pallas_call(
        lambda *refs: kernel(scale, *refs),
        out_shape=jax.ShapeDtypeStruct((TILES, 8, 128), f32),
        in_specs=[pl.BlockSpec(memory_space=pl.ANY)],
        out_specs=pl.BlockSpec(memory_space=pltpu.VMEM),
        scratch_shapes=[
            pltpu.VMEM((4, 4, 3, BLOCK, BLOCK), b16),
            pltpu.VMEM((2, 3, BLOCK // 2, BLOCK), b16),
            pltpu.VMEM((TILES, 2, 4, 8, 8, 128), f32),
            pltpu.VMEM((TILES, 4, 8, 8, 128), f32),
            pltpu.VMEM((2, TILES, 4, 8, 128), f32),
            pltpu.VMEM((2, TILES, 8, 8, 128), f32),
            pltpu.VMEM((TILES, 8, 8, 128), f32),
            pltpu.VMEM((2, TILES // 2, 8, 128), f32),
            pltpu.VMEM((2, 3, TILES, 8, 128), f32),
            dma(()), dma((6,)), dma((6,)), dma((4, 4)), dma((4, 4)), dma((count,)), dma((count,)),
            dma((count, 4)), dma((count, 4)), dma((2, 4)), dma((2, 4)),
        ],
        compiler_params=pltpu.CompilerParams(collective_id=0, has_side_effects=True, vmem_limit_bytes=60 * 2**20),
        name="gram_reduce",
    )(snapshots)


def tile_index(table):
    a, b = table[:, 0], table[:, 1]
    za, ya, zb, yb = a // SIDE, a % SIDE, b // SIDE, b % SIDE
    dy, dz = (yb - ya) % SIDE, (zb - za) % SIDE
    own = jnp.where(dz == 2, 24 + za % 2, jnp.where(dz == 3, 20 + zb, 16 + 4 * dz + za))
    low = za < 2
    far_y = jnp.where(dz == 3, yb, jnp.where((dz == 0) & ~low, yb, ya))
    far_t = jnp.where(
        dz == 1, 26 + za, jnp.where(dz == 3, 26 + zb, jnp.where(dz == 0, 30 + za % 2, 32 + za))
    )
    which_y = jnp.where(dy == 2, far_y, jnp.where(dy == 3, yb, ya))
    which_t = jnp.where(
        dy == 0, own, jnp.where(dy == 1, 4 * za + zb, jnp.where(dy == 3, 4 * zb + za, far_t))
    )
    return jnp.where(a >= 0, which_y * TILES + which_t, SIDE * TILES)


def per_device(snapshots, tile_table):
    cells_dev = snapshots.shape[2]
    scale = 1.0 / math.sqrt(3 * cells_dev * lax.axis_size("space"))
    table = tile_table[0]
    index = tile_index(table)
    pieces = reduced(snapshots, scale)
    whole = lax.all_gather(pieces, "tm", axis=0, tiled=False)
    whole = whole.reshape(SIDE, SIDE * TILES, 8, 128)
    chosen = jnp.take(whole, jnp.minimum(index, SIDE * TILES - 1), axis=1)
    chosen = jnp.where((index < SIDE * TILES)[None, :, None, None], chosen, jnp.zeros_like(chosen))
    slots = table.shape[0]
    chosen = chosen.reshape(2, 2, slots, 8, 128).transpose(2, 0, 3, 1, 4)
    return chosen.reshape(1, slots, 16, BLOCK)


def solution(mesh):
    in_specs = (P(None, "tm", "space"), P("tm", None, None))
    out_specs = P("tm", None, "space", None)
    return jax.shard_map(
        per_device, mesh=mesh, in_specs=in_specs, out_specs=out_specs, check_vma=False
    )
```

```python
import math

import jax
import jax.numpy as jnp
from jax import lax
from jax.experimental import pallas as pl
from jax.experimental.pallas import tpu as pltpu
from jax.sharding import PartitionSpec as P

MESH = pl.DeviceIdType.MESH
BLOCK = 256
SIDE = 4
SLOTS = 20
TILES = 34
BATCHES = (8, 9, 9, 8)


def pick(index, values):
    chosen = values[0]
    for place in range(1, len(values)):
        chosen = jnp.where(index == place, values[place], chosen)
    return chosen


def tile_list(h, y):
    z = [lax.rem(h + step, SIDE) for step in range(SIDE)]
    same, near, far = y, lax.rem(y + 1, SIDE), lax.rem(y + 2, SIDE)

    def make(z1, y1, z2, y2, tile):
        first = z1 * SIDE + y1 <= z2 * SIDE + y2
        one, two = y1 * SIDE + z1, y2 * SIDE + z2
        return (jnp.where(first, one, two), jnp.where(first, two, one), tile)

    def own(a, b):
        step = (b - a) % SIDE
        base = lax.rem(z[a], 2) if step == 2 else z[a]
        return make(z[a], same, z[b], same, 16 + 4 * step + base)

    def side(a, b):
        return make(z[a], same, z[b], near, SIDE * z[a] + z[b])

    def across(a):
        b = (a + 1) % SIDE
        return make(z[a], same, z[b], far, 26 + z[a])

    half = jnp.where(y >= 2, 2, 0)
    return [
        own(0, 0), side(0, 0),
        own(3, 3), own(3, 0), side(0, 3), side(3, 0), side(3, 3), across(3),
        own(1, 1), own(0, 1), own(1, 3), side(1, 1), side(1, 0), side(0, 1), side(1, 3), side(3, 1), across(0),
        own(2, 2), own(1, 2), own(2, 3), own(0, 2), side(2, 0), side(0, 2), side(2, 1), side(1, 2), side(2, 2),
        side(2, 3), side(3, 2), across(1), across(2),
        make(half, same, half, far, 30), make(half + 1, same, half + 1, far, 31),
        make(0, same, 2, far, 32), make(1, same, 3, far, 33),
    ]


def kernel(
    scale, x_ref, index_ref, out_ref, blocks, relay, part, pair, xfirst, xlast, total, zhalf, zpart,
    indices, wanted, pieces, chosen, through, landed,
    local_sem, zs, zr, ys, yr, ps, pr, xs, xr, ws, wr, ts, tr, gs, gr, os, onr,
):
    tm, space = lax.axis_index("tm"), lax.axis_index("space")
    h, y = tm // SIDE, lax.rem(tm, SIDE)
    x, low, core = space // SIDE, lax.rem(space // 2, 2), lax.rem(space, 2)

    def device(h_=h, y_=y, x_=x, low_=low, core_=core):
        return (h_ * SIDE + y_, x_ * SIDE + low_ * 2 + core_)

    def up(value, step, size=SIDE):
        return lax.rem(value + step, size)

    hp, hm, h2 = up(h, 1), up(h, 3), up(h, 2)
    yp, ym = up(y, 1), up(y, 3)
    xp, xm, x2 = up(x, 1), up(x, 3), up(x, 2)
    other = 1 - core
    place = h * 2 + low
    zp, zm = up(place, 1, 8), up(place, 7, 8)
    dev_hp, dev_hm, dev_h2 = device(h_=hp), device(h_=hm), device(h_=h2)
    dev_yp, dev_ym = device(y_=yp), device(y_=ym)
    dev_xp, dev_xm = device(x_=xp), device(x_=xm)
    dev_zp = device(h_=zp // 2, low_=lax.rem(zp, 2))
    dev_zm = device(h_=zm // 2, low_=lax.rem(zm, 2))
    dev_pair = device(core_=other)

    barrier = pltpu.get_barrier_semaphore()
    peers = (dev_hp, dev_hm, dev_h2, dev_yp, dev_ym, dev_xp, dev_xm, dev_zp, dev_zm, dev_pair)
    for peer in peers:
        pl.semaphore_signal(barrier, inc=1, device_id=peer, device_id_type=MESH)
    pl.semaphore_wait(barrier, len(peers))

    started = []

    def send(src, dst, send_sem, recv_sem, peer):
        copy = pltpu.make_async_remote_copy(
            src_ref=src, dst_ref=dst, send_sem=send_sem, recv_sem=recv_sem, device_id=peer, device_id_type=MESH
        )
        copy.start()
        started.append(copy)
        return copy

    def cells(which):
        return pl.ds(pl.multiple_of(which * BLOCK, BLOCK), BLOCK)

    every = slice(None)
    first_rows, last_rows = pl.ds(0, BLOCK // 2), pl.ds(BLOCK // 2, BLOCK // 2)

    local = pltpu.make_async_copy(x_ref.at[:, :, cells(h)], blocks.at[y, h], local_sem)
    local.start()
    own_index = pltpu.make_async_copy(index_ref, indices.at[h], ts.at[3])
    own_index.start()
    to_hp = send(x_ref.at[:, :, cells(hp)], blocks.at[y, h], zs.at[0], zr.at[0], dev_hp)
    to_hm = send(x_ref.at[:, :, cells(hm)], blocks.at[y, h], zs.at[1], zr.at[1], dev_hm)
    via_hp = send(x_ref.at[:, first_rows, cells(h2)], relay.at[0], zs.at[2], zr.at[2], dev_hp)
    via_hm = send(x_ref.at[:, last_rows, cells(h2)], relay.at[1], zs.at[3], zr.at[3], dev_hm)

    told = [
        send(index_ref, indices.at[h], ts.at[number], tr.at[number], peer)
        for number, peer in enumerate((dev_hp, dev_hm, dev_h2))
    ]

    direct, onward = {}, {}

    def spread(key, z):
        down = send(blocks.at[y, z], blocks.at[y, z], ys.at[key, 0], yr.at[key, 0], dev_ym)
        above = send(blocks.at[y, z, pl.ds(1, 2)], blocks.at[y, z, pl.ds(1, 2)], ys.at[key, 1], yr.at[key, 1], dev_yp)
        direct[key] = (down, above)

    def forward(key, z):
        down, above = direct[key]
        down.wait_recv()
        first = send(blocks.at[yp, z, pl.ds(0, 1)], blocks.at[yp, z, pl.ds(0, 1)], ys.at[key, 2], yr.at[key, 2], dev_ym)
        above.wait_recv()
        rest = send(blocks.at[ym, z, pl.ds(1, 2)], blocks.at[ym, z, pl.ds(1, 2)], ys.at[key, 3], yr.at[key, 3], dev_yp)
        onward[key] = (first, rest)

    def gathered(key):
        for copy in onward[key]:
            copy.wait_recv()

    tiles = tile_list(h, y)
    starts = [sum(BATCHES[:number]) for number in range(len(BATCHES))]

    def compute(number):
        begin, size = starts[number], BATCHES[number]
        some = tiles[begin:begin + size]

        @pl.loop(0, size)
        def _(step):
            left = pick(step, [tile[0] for tile in some])
            right = pick(step, [tile[1] for tile in some])
            ly, lz, ry, rz = left // SIDE, lax.rem(left, SIDE), right // SIDE, lax.rem(right, SIDE)
            product = None
            for comp in range(3):
                term = lax.dot_general(
                    blocks[ly, lz, comp], blocks[ry, rz, comp], (((1,), (1,)), ((), ())),
                    preferred_element_type=jnp.float32,
                )
                product = term if product is None else product + term
            slot = begin + step
            for row in range(BLOCK // 8):
                for lane in range(2):
                    place_x, place_low, place_core, place_row = row // 8, row // 4 % 2, row // 2 % 2, row % 2
                    part[slot, place_core, place_x, place_low * 4 + place_row * 2 + lane] = product[
                        row * 8:row * 8 + 8, lane * 128:lane * 128 + 128
                    ]

        span = pl.ds(begin, size)
        return send(part.at[span, other], pair.at[span], ps.at[number], pr.at[number], dev_pair)

    def add_pair(number, copy):
        begin, size = starts[number], BATCHES[number]
        copy.wait_recv()

        @pl.loop(begin, begin + size)
        def _(slot):
            part[slot, core] = part[slot, core] + pair[slot]

        span = pl.ds(begin, size)
        return (
            send(part.at[span, core, x2, pl.ds(0, 4)], xfirst.at[0, span], xs.at[number, 0], xr.at[number, 0], dev_xp),
            send(part.at[span, core, x2, pl.ds(4, 4)], xfirst.at[1, span], xs.at[number, 1], xr.at[number, 1], dev_xm),
        )

    def add_first(number, copies):
        begin, size = starts[number], BATCHES[number]
        for copy in copies:
            copy.wait_recv()

        @pl.loop(begin, begin + size)
        def _(slot):
            part[slot, core, xp, 0:4] = part[slot, core, xp, 0:4] + xfirst[0, slot]
            part[slot, core, xm, 4:8] = part[slot, core, xm, 4:8] + xfirst[1, slot]

        span = pl.ds(begin, size)
        return (
            send(part.at[span, core, xp], xlast.at[0, span], xs.at[number, 2], xr.at[number, 2], dev_xp),
            send(part.at[span, core, xm], xlast.at[1, span], xs.at[number, 3], xr.at[number, 3], dev_xm),
        )

    def add_last(number, copies):
        begin, size = starts[number], BATCHES[number]
        for copy in copies:
            copy.wait_recv()
        some = tiles[begin:begin + size]

        @pl.loop(0, size)
        def _(step):
            slot = begin + step
            total[pick(step, [tile[2] for tile in some])] = part[slot, core, x] + xlast[0, slot] + xlast[1, slot]

    local.wait()
    spread(0, h)
    forward(0, h)
    to_hp.wait_recv()
    spread(1, hm)
    to_hm.wait_recv()
    spread(2, hp)
    via_hp.wait_recv()
    on_hp = send(relay.at[0], blocks.at[y, hm, :, first_rows], zs.at[4], zr.at[4], dev_hp)
    via_hm.wait_recv()
    on_hm = send(relay.at[1], blocks.at[y, hp, :, last_rows], zs.at[5], zr.at[5], dev_hm)
    gathered(0)
    forward(1, hm)
    forward(2, hp)
    on_hp.wait_recv()
    on_hm.wait_recv()
    spread(3, h2)
    gathered(1)
    pair0 = compute(0)
    gathered(2)
    pair1 = compute(1)
    first0 = add_pair(0, pair0)
    forward(3, h2)
    first1 = add_pair(1, pair1)
    last0 = add_first(0, first0)
    last1 = add_first(1, first1)
    gathered(3)
    pair2 = compute(2)
    pair3 = compute(3)
    first2 = add_pair(2, pair2)
    add_last(0, last0)
    first3 = add_pair(3, pair3)
    last2 = add_first(2, first2)
    add_last(1, last1)
    last3 = add_first(3, first3)
    add_last(2, last2)
    add_last(3, last3)

    def piece(step):
        target = up(place, step, 8)
        return lax.rem(target, 2) * 4 + target // 2

    four = piece(4)
    near_half, far_half = pl.ds(0, TILES // 2), pl.ds(TILES // 2, TILES // 2)
    go_up = send(total.at[near_half, four], zhalf.at[0], ws.at[0, 0], wr.at[0, 0], dev_zp)
    go_down = send(total.at[far_half, four], zhalf.at[1], ws.at[1, 0], wr.at[1, 0], dev_zm)
    for step in range(3):
        above, below = piece(3 - step), piece(5 + step)
        go_up.wait_recv()
        if step == 0:
            total[0:TILES // 2, above] = total[0:TILES // 2, above] + zhalf[0]
        else:
            total[:, above] = total[:, above] + zpart[0, step - 1]
        go_up = send(total.at[:, above], zpart.at[0, step], ws.at[0, step + 1], wr.at[0, step + 1], dev_zp)
        go_down.wait_recv()
        if step == 0:
            total[TILES // 2:TILES, below] = total[TILES // 2:TILES, below] + zhalf[1]
        else:
            total[:, below] = total[:, below] + zpart[1, step - 1]
        go_down = send(total.at[:, below], zpart.at[1, step], ws.at[1, step + 1], wr.at[1, step + 1], dev_zm)
    go_up.wait_recv()
    go_down.wait_recv()
    mine = pl.ds(y * TILES, TILES)
    pieces[mine] = (total[:, piece(0)] + zpart[0, 2] + zpart[1, 2]) * scale
    pieces[SIDE * TILES] = jnp.zeros((8, 128), jnp.float32)

    to_yp = send(pieces.at[mine], pieces.at[mine], gs.at[0], gr.at[0], dev_yp)
    to_ym = send(pieces.at[mine], pieces.at[mine], gs.at[1], gr.at[1], dev_ym)
    own_index.wait()
    for copy in told:
        copy.wait_recv()
    listed = pltpu.make_async_copy(indices, wanted, local_sem)
    listed.start()
    listed.wait()
    to_yp.wait_recv()
    early = pl.ds(ym * TILES, TILES // 2)
    on_yp = send(pieces.at[early], pieces.at[early], gs.at[2], gr.at[2], dev_yp)
    to_ym.wait_recv()
    late = pl.ds(yp * TILES + TILES // 2, TILES // 2)
    on_ym = send(pieces.at[late], pieces.at[late], gs.at[3], gr.at[3], dev_ym)
    on_yp.wait_recv()
    on_ym.wait_recv()

    def choose(number, z):
        @pl.loop(0, SLOTS)
        def _(slot):
            chosen[number, slot] = pieces[wanted[z, 0, slot]]

    half = SLOTS // 2
    choose(2, h2)
    far_hp = send(chosen.at[2, pl.ds(0, half)], through.at[0], os.at[2], onr.at[2], dev_hp)
    far_hm = send(chosen.at[2, pl.ds(half, half)], through.at[1], os.at[3], onr.at[3], dev_hm)
    choose(0, hp)
    out_hp = send(chosen.at[0], landed.at[0], os.at[0], onr.at[0], dev_hp)
    choose(1, hm)
    out_hm = send(chosen.at[1], landed.at[1], os.at[1], onr.at[1], dev_hm)
    far_hp.wait_recv()
    last_hp = send(through.at[0], landed.at[2, pl.ds(0, half)], os.at[4], onr.at[4], dev_hp)
    far_hm.wait_recv()
    last_hm = send(through.at[1], landed.at[2, pl.ds(half, half)], os.at[5], onr.at[5], dev_hm)

    @pl.loop(0, SLOTS)
    def _(slot):
        out_ref[h, slot] = pieces[wanted[h, 0, slot]]

    out_hp.wait_recv()
    out_ref[hm] = landed[0]
    out_hm.wait_recv()
    out_ref[hp] = landed[1]
    last_hp.wait_recv()
    last_hm.wait_recv()
    out_ref[h2] = landed[2]
    for copy in started:
        copy.wait_send()


def gram(snapshots, index, scale):
    count = len(BATCHES)
    dma = pltpu.SemaphoreType.DMA
    f32, b16 = jnp.float32, jnp.bfloat16
    return pl.pallas_call(
        lambda *refs: kernel(scale, *refs),
        out_shape=jax.ShapeDtypeStruct((SIDE, SLOTS, 8, 128), f32),
        in_specs=[pl.BlockSpec(memory_space=pl.ANY)] * 2,
        out_specs=pl.BlockSpec(memory_space=pltpu.VMEM),
        scratch_shapes=[
            pltpu.VMEM((4, 4, 3, BLOCK, BLOCK), b16),
            pltpu.VMEM((2, 3, BLOCK // 2, BLOCK), b16),
            pltpu.VMEM((TILES, 2, 4, 8, 8, 128), f32),
            pltpu.VMEM((TILES, 4, 8, 8, 128), f32),
            pltpu.VMEM((2, TILES, 4, 8, 128), f32),
            pltpu.VMEM((2, TILES, 8, 8, 128), f32),
            pltpu.VMEM((TILES, 8, 8, 128), f32),
            pltpu.VMEM((2, TILES // 2, 8, 128), f32),
            pltpu.VMEM((2, 3, TILES, 8, 128), f32),
            pltpu.VMEM((SIDE, 8, 128), jnp.int32),
            pltpu.SMEM((SIDE, 8, 128), jnp.int32),
            pltpu.VMEM((SIDE * TILES + 1, 8, 128), f32),
            pltpu.VMEM((3, SLOTS, 8, 128), f32),
            pltpu.VMEM((2, SLOTS // 2, 8, 128), f32),
            pltpu.VMEM((3, SLOTS, 8, 128), f32),
            dma(()), dma((6,)), dma((6,)), dma((4, 4)), dma((4, 4)), dma((count,)), dma((count,)),
            dma((count, 4)), dma((count, 4)), dma((2, 4)), dma((2, 4)),
            dma((4,)), dma((3,)), dma((4,)), dma((4,)), dma((6,)), dma((6,)),
        ],
        compiler_params=pltpu.CompilerParams(collective_id=0, has_side_effects=True, vmem_limit_bytes=60 * 2**20),
        name="gram_tiles",
    )(snapshots, index)


def tile_index(table):
    a, b = table[:, 0], table[:, 1]
    za, ya, zb, yb = a // SIDE, a % SIDE, b // SIDE, b % SIDE
    dy, dz = (yb - ya) % SIDE, (zb - za) % SIDE
    own = jnp.where(dz == 2, 24 + za % 2, jnp.where(dz == 3, 20 + zb, 16 + 4 * dz + za))
    low = za < 2
    far_y = jnp.where(dz == 3, yb, jnp.where((dz == 0) & ~low, yb, ya))
    far_t = jnp.where(
        dz == 1, 26 + za, jnp.where(dz == 3, 26 + zb, jnp.where(dz == 0, 30 + za % 2, 32 + za))
    )
    which_y = jnp.where(dy == 2, far_y, jnp.where(dy == 3, yb, ya))
    which_t = jnp.where(
        dy == 0, own, jnp.where(dy == 1, 4 * za + zb, jnp.where(dy == 3, 4 * zb + za, far_t))
    )
    return jnp.where(a >= 0, which_y * TILES + which_t, SIDE * TILES)


def per_device(snapshots, tile_table):
    cells_dev = snapshots.shape[2]
    scale = 1.0 / math.sqrt(3 * cells_dev * lax.axis_size("space"))
    table = tile_table[0]
    slots = table.shape[0]
    index = jnp.broadcast_to(jnp.pad(tile_index(table), (0, 128 - slots)), (8, 128))
    tiles = gram(snapshots, index, scale).reshape(2, 2, slots, 8, 128)
    return tiles.transpose(2, 0, 3, 1, 4).reshape(1, slots, 16, BLOCK)


def solution(mesh):
    in_specs = (P(None, "tm", "space"), P("tm", None, None))
    out_specs = P("tm", None, "space", None)
    return jax.shard_map(
        per_device, mesh=mesh, in_specs=in_specs, out_specs=out_specs, check_vma=False
    )
```

```python
import math

import jax
import jax.numpy as jnp
from jax import lax
from jax.experimental import pallas as pl
from jax.experimental.pallas import tpu as pltpu
from jax.sharding import PartitionSpec as P

MESH = pl.DeviceIdType.MESH
BLOCK = 256
SIDE = 4
SLOTS = 20
TILES = 34
BATCHES = (8, 9, 6, 6, 5)
CHUNKS = ((0, 16), (16, 18))


def pick(index, values):
    chosen = values[0]
    for place in range(1, len(values)):
        chosen = jnp.where(index == place, values[place], chosen)
    return chosen


def tile_list(h, y):
    z = [lax.rem(h + step, SIDE) for step in range(SIDE)]
    same, near, far = y, lax.rem(y + 1, SIDE), lax.rem(y + 2, SIDE)

    def make(z1, y1, z2, y2, tile):
        first = z1 * SIDE + y1 <= z2 * SIDE + y2
        one, two = y1 * SIDE + z1, y2 * SIDE + z2
        return (jnp.where(first, one, two), jnp.where(first, two, one), tile)

    def own(a, b):
        step = (b - a) % SIDE
        base = lax.rem(z[a], 2) if step == 2 else z[a]
        return make(z[a], same, z[b], same, 16 + 4 * step + base)

    def side(a, b):
        return make(z[a], same, z[b], near, SIDE * z[a] + z[b])

    def across(a):
        b = (a + 1) % SIDE
        return make(z[a], same, z[b], far, 26 + z[a])

    half = jnp.where(y >= 2, 2, 0)
    return [
        own(0, 0), side(0, 0),
        own(3, 3), own(3, 0), side(0, 3), side(3, 0), side(3, 3), across(3),
        own(1, 1), own(0, 1), own(1, 3), side(1, 1), side(1, 0), side(0, 1), side(1, 3), side(3, 1), across(0),
        own(2, 2), own(1, 2), own(2, 3), own(0, 2), side(2, 0), side(0, 2), side(2, 1), side(1, 2), side(2, 2),
        side(2, 3), side(3, 2), across(1), across(2),
        make(half, same, half, far, 30), make(half + 1, same, half + 1, far, 31),
        make(0, same, 2, far, 32), make(1, same, 3, far, 33),
    ]


def kernel(
    scale, x_ref, index_ref, out_ref, blocks, relay, part, pair, xfirst, xlast, total, zpart,
    indices, wanted, pieces, chosen, through, landed,
    local_sem, zs, zr, ys, yr, ps, pr, xs, xr, ws, wr, ts, tr, gs, gr, os, onr,
):
    tm, space = lax.axis_index("tm"), lax.axis_index("space")
    h, y = tm // SIDE, lax.rem(tm, SIDE)
    x, low, core = space // SIDE, lax.rem(space // 2, 2), lax.rem(space, 2)

    def device(h_=h, y_=y, x_=x, low_=low, core_=core):
        return (h_ * SIDE + y_, x_ * SIDE + low_ * 2 + core_)

    def up(value, step, size=SIDE):
        return lax.rem(value + step, size)

    hp, hm, h2 = up(h, 1), up(h, 3), up(h, 2)
    yp, ym = up(y, 1), up(y, 3)
    xp, xm, x2 = up(x, 1), up(x, 3), up(x, 2)
    other = 1 - core
    place = h * 2 + low
    zp, zm = up(place, 1, 8), up(place, 7, 8)
    dev_hp, dev_hm, dev_h2 = device(h_=hp), device(h_=hm), device(h_=h2)
    dev_yp, dev_ym = device(y_=yp), device(y_=ym)
    dev_xp, dev_xm = device(x_=xp), device(x_=xm)
    dev_zp = device(h_=zp // 2, low_=lax.rem(zp, 2))
    dev_zm = device(h_=zm // 2, low_=lax.rem(zm, 2))
    dev_pair = device(core_=other)

    barrier = pltpu.get_barrier_semaphore()
    peers = (dev_hp, dev_hm, dev_h2, dev_yp, dev_ym, dev_xp, dev_xm, dev_zp, dev_zm, dev_pair)
    for peer in peers:
        pl.semaphore_signal(barrier, inc=1, device_id=peer, device_id_type=MESH)
    pl.semaphore_wait(barrier, len(peers))

    started = []

    def send(src, dst, send_sem, recv_sem, peer):
        copy = pltpu.make_async_remote_copy(
            src_ref=src, dst_ref=dst, send_sem=send_sem, recv_sem=recv_sem, device_id=peer, device_id_type=MESH
        )
        copy.start()
        started.append(copy)
        return copy

    def cells(which):
        return pl.ds(pl.multiple_of(which * BLOCK, BLOCK), BLOCK)

    every = slice(None)
    first_rows, last_rows = pl.ds(0, BLOCK // 2), pl.ds(BLOCK // 2, BLOCK // 2)

    local = pltpu.make_async_copy(x_ref.at[:, :, cells(h)], blocks.at[y, h], local_sem)
    local.start()
    own_index = pltpu.make_async_copy(index_ref, indices.at[h], ts.at[3])
    own_index.start()
    comps = range(3)
    to_hp = [send(x_ref.at[k, :, cells(hp)], blocks.at[y, h, k], zs.at[0, k], zr.at[0, k], dev_hp) for k in comps]
    to_hm = [send(x_ref.at[k, :, cells(hm)], blocks.at[y, h, k], zs.at[1, k], zr.at[1, k], dev_hm) for k in comps]

    moved, passed = {}, {}

    def spread(key, z, k, src=None):
        src = blocks.at[y, z, k] if src is None else src
        dst = blocks.at[y, z, k]
        moved[key, k, 0] = send(src, dst, ys.at[key, k, 0], yr.at[key, k, 0], dev_ym)
        if k > 0:
            moved[key, k, 1] = send(src, dst, ys.at[key, k, 1], yr.at[key, k, 1], dev_yp)

    def forward(key, z, k):
        if k == 0:
            moved[key, k, 0].wait_recv()
            block, peer = blocks.at[yp, z, k], dev_ym
        else:
            moved[key, k, 1].wait_recv()
            block, peer = blocks.at[ym, z, k], dev_yp
        passed[key, k] = send(block, block, ys.at[key, k, 2], yr.at[key, k, 2], peer)

    def gathered(key):
        for k in comps:
            if k > 0:
                moved[key, k, 0].wait_recv()
            passed[key, k].wait_recv()

    for k in comps:
        spread(0, h, k, x_ref.at[k, :, cells(h)])
    via_hp = [send(x_ref.at[k, first_rows, cells(h2)], relay.at[0, k], zs.at[2, k], zr.at[2, k], dev_hp) for k in comps]
    via_hm = [send(x_ref.at[k, last_rows, cells(h2)], relay.at[1, k], zs.at[3, k], zr.at[3, k], dev_hm) for k in comps]
    told = [
        send(index_ref, indices.at[h], ts.at[number], tr.at[number], peer)
        for number, peer in enumerate((dev_hp, dev_hm, dev_h2))
    ]
    on_hp, on_hm = {}, {}

    def onward(k):
        via_hp[k].wait_recv()
        on_hp[k] = send(relay.at[0, k], blocks.at[y, hm, k, first_rows], zs.at[4, k], zr.at[4, k], dev_hp)
        via_hm[k].wait_recv()
        on_hm[k] = send(relay.at[1, k], blocks.at[y, hp, k, last_rows], zs.at[5, k], zr.at[5, k], dev_hm)

    def spread_far(k):
        on_hp[k].wait_recv()
        on_hm[k].wait_recv()
        spread(3, h2, k)

    tiles = tile_list(h, y)
    starts = [sum(BATCHES[:number]) for number in range(len(BATCHES))]

    def compute(number):
        begin, size = starts[number], BATCHES[number]
        some = tiles[begin:begin + size]

        @pl.loop(0, size)
        def _(step):
            left = pick(step, [tile[0] for tile in some])
            right = pick(step, [tile[1] for tile in some])
            ly, lz, ry, rz = left // SIDE, lax.rem(left, SIDE), right // SIDE, lax.rem(right, SIDE)
            product = None
            for comp in range(3):
                term = lax.dot_general(
                    blocks[ly, lz, comp], blocks[ry, rz, comp], (((1,), (1,)), ((), ())),
                    preferred_element_type=jnp.float32,
                )
                product = term if product is None else product + term
            slot = begin + step
            for row in range(BLOCK // 8):
                for lane in range(2):
                    place_x, place_low, place_core, place_row = row // 8, row // 4 % 2, row // 2 % 2, row % 2
                    part[slot, place_core, place_x, place_low * 4 + place_row * 2 + lane] = product[
                        row * 8:row * 8 + 8, lane * 128:lane * 128 + 128
                    ]

        span = pl.ds(begin, size)
        return send(part.at[span, other], pair.at[span], ps.at[number], pr.at[number], dev_pair)

    def add_pair(number, copy):
        begin, size = starts[number], BATCHES[number]
        copy.wait_recv()

        @pl.loop(begin, begin + size)
        def _(slot):
            part[slot, core] = part[slot, core] + pair[slot]

        span = pl.ds(begin, size)
        return (
            send(part.at[span, core, x2, pl.ds(0, 4)], xfirst.at[0, span], xs.at[number, 0], xr.at[number, 0], dev_xp),
            send(part.at[span, core, x2, pl.ds(4, 4)], xfirst.at[1, span], xs.at[number, 1], xr.at[number, 1], dev_xm),
        )

    def add_first(number, copies):
        begin, size = starts[number], BATCHES[number]
        for copy in copies:
            copy.wait_recv()

        @pl.loop(begin, begin + size)
        def _(slot):
            part[slot, core, xp, 0:4] = part[slot, core, xp, 0:4] + xfirst[0, slot]
            part[slot, core, xm, 4:8] = part[slot, core, xm, 4:8] + xfirst[1, slot]

        span = pl.ds(begin, size)
        return (
            send(part.at[span, core, xp], xlast.at[0, span], xs.at[number, 2], xr.at[number, 2], dev_xp),
            send(part.at[span, core, xm], xlast.at[1, span], xs.at[number, 3], xr.at[number, 3], dev_xm),
        )

    def add_last(number, copies):
        begin, size = starts[number], BATCHES[number]
        for copy in copies:
            copy.wait_recv()
        some = tiles[begin:begin + size]

        @pl.loop(0, size)
        def _(step):
            slot = begin + step
            total[pick(step, [tile[2] for tile in some])] = part[slot, core, x] + xlast[0, slot] + xlast[1, slot]

    for k in comps:
        forward(0, h, k)
    for k in comps:
        to_hp[k].wait_recv()
        spread(1, hm, k)
    to_hm[0].wait_recv()
    spread(2, hp, 0)
    forward(1, hm, 0)
    forward(1, hm, 1)
    to_hm[1].wait_recv()
    spread(2, hp, 1)
    onward(0)
    forward(1, hm, 2)
    to_hm[2].wait_recv()
    spread(2, hp, 2)
    onward(1)
    onward(2)
    forward(2, hp, 0)
    forward(2, hp, 1)
    local.wait()
    gathered(0)
    gathered(1)
    pair0 = compute(0)
    forward(2, hp, 2)
    spread_far(0)
    first0 = add_pair(0, pair0)
    spread_far(1)
    last0 = add_first(0, first0)
    spread_far(2)
    gathered(2)
    pair1 = compute(1)
    forward(3, h2, 0)
    first1 = add_pair(1, pair1)
    forward(3, h2, 1)
    last1 = add_first(1, first1)
    forward(3, h2, 2)
    add_last(0, last0)
    gathered(3)
    pair2 = compute(2)
    pair3 = compute(3)
    first2 = add_pair(2, pair2)
    pair4 = compute(4)
    first3 = add_pair(3, pair3)
    add_last(1, last1)
    first4 = add_pair(4, pair4)
    last2 = add_first(2, first2)
    last3 = add_first(3, first3)
    last4 = add_first(4, first4)
    add_last(2, last2)
    add_last(3, last3)
    add_last(4, last4)

    def piece(step):
        target = up(place, step, 8)
        return lax.rem(target, 2) * 4 + target // 2

    rings = ((0, 0, 4), (1, 1, 4), (0, 1, 3), (1, 0, 3))
    flying = {}

    def pass_on(chunk, way, hops, number):
        begin, size = CHUNKS[chunk]
        span = pl.ds(begin, size)
        distance = hops - number
        which = piece(distance if way == 0 else 8 - distance)
        if number > 0:
            flying[chunk, way].wait_recv()
            total[begin:begin + size, which] = total[begin:begin + size, which] + zpart[way, number - 1, begin:begin + size]
        flying[chunk, way] = send(
            total.at[span, which], zpart.at[way, number, span],
            ws.at[chunk, way, number], wr.at[chunk, way, number], dev_zp if way == 0 else dev_zm,
        )

    for number in range(4):
        for chunk, way, hops in rings:
            if number < hops:
                pass_on(chunk, way, hops, number)

    pieces[SIDE * TILES] = jnp.zeros((8, 128), jnp.float32)
    shared, onto = {}, {}
    for chunk, (begin, size) in enumerate(CHUNKS):
        for way in range(2):
            flying[chunk, way].wait_recv()
        up_last, down_last = (3, 2) if chunk == 0 else (2, 3)
        end = begin + size
        value = total[begin:end, piece(0)] + zpart[0, up_last, begin:end] + zpart[1, down_last, begin:end]
        span = pl.ds(y * TILES + begin, size)
        pieces[span] = value * scale
        shared[chunk] = (
            send(pieces.at[span], pieces.at[span], gs.at[chunk, 0], gr.at[chunk, 0], dev_yp),
            send(pieces.at[span], pieces.at[span], gs.at[chunk, 1], gr.at[chunk, 1], dev_ym),
        )
    own_index.wait()
    for copy in told:
        copy.wait_recv()
    listed = pltpu.make_async_copy(indices, wanted, local_sem)
    listed.start()
    listed.wait()
    for chunk, (begin, size) in enumerate(CHUNKS):
        half = size // 2
        to_yp, to_ym = shared[chunk]
        to_yp.wait_recv()
        early = pl.ds(ym * TILES + begin, half)
        on_yp = send(pieces.at[early], pieces.at[early], gs.at[chunk, 2], gr.at[chunk, 2], dev_yp)
        to_ym.wait_recv()
        late = pl.ds(yp * TILES + begin + half, half)
        on_ym = send(pieces.at[late], pieces.at[late], gs.at[chunk, 3], gr.at[chunk, 3], dev_ym)
        onto[chunk] = (on_yp, on_ym)
    for chunk in range(len(CHUNKS)):
        for copy in onto[chunk]:
            copy.wait_recv()

    def choose(number, z):
        @pl.loop(0, SLOTS)
        def _(slot):
            chosen[number, slot] = pieces[wanted[z, 0, slot]]

    half = SLOTS // 2
    choose(2, h2)
    far_hp = send(chosen.at[2, pl.ds(0, half)], through.at[0], os.at[2], onr.at[2], dev_hp)
    far_hm = send(chosen.at[2, pl.ds(half, half)], through.at[1], os.at[3], onr.at[3], dev_hm)
    choose(0, hp)
    out_hp = send(chosen.at[0], landed.at[0], os.at[0], onr.at[0], dev_hp)
    choose(1, hm)
    out_hm = send(chosen.at[1], landed.at[1], os.at[1], onr.at[1], dev_hm)
    far_hp.wait_recv()
    last_hp = send(through.at[0], landed.at[2, pl.ds(0, half)], os.at[4], onr.at[4], dev_hp)
    far_hm.wait_recv()
    last_hm = send(through.at[1], landed.at[2, pl.ds(half, half)], os.at[5], onr.at[5], dev_hm)

    @pl.loop(0, SLOTS)
    def _(slot):
        out_ref[h, slot] = pieces[wanted[h, 0, slot]]

    out_hp.wait_recv()
    out_ref[hm] = landed[0]
    out_hm.wait_recv()
    out_ref[hp] = landed[1]
    last_hp.wait_recv()
    last_hm.wait_recv()
    out_ref[h2] = landed[2]
    for copy in started:
        copy.wait_send()


def gram(snapshots, index, scale):
    count = len(BATCHES)
    dma = pltpu.SemaphoreType.DMA
    f32, b16 = jnp.float32, jnp.bfloat16
    return pl.pallas_call(
        lambda *refs: kernel(scale, *refs),
        out_shape=jax.ShapeDtypeStruct((SIDE, SLOTS, 8, 128), f32),
        in_specs=[pl.BlockSpec(memory_space=pl.ANY)] * 2,
        out_specs=pl.BlockSpec(memory_space=pltpu.VMEM),
        scratch_shapes=[
            pltpu.VMEM((4, 4, 3, BLOCK, BLOCK), b16),
            pltpu.VMEM((2, 3, BLOCK // 2, BLOCK), b16),
            pltpu.VMEM((TILES, 2, 4, 8, 8, 128), f32),
            pltpu.VMEM((TILES, 4, 8, 8, 128), f32),
            pltpu.VMEM((2, TILES, 4, 8, 128), f32),
            pltpu.VMEM((2, TILES, 8, 8, 128), f32),
            pltpu.VMEM((TILES, 8, 8, 128), f32),
            pltpu.VMEM((2, 4, TILES, 8, 128), f32),
            pltpu.VMEM((SIDE, 8, 128), jnp.int32),
            pltpu.SMEM((SIDE, 8, 128), jnp.int32),
            pltpu.VMEM((SIDE * TILES + 1, 8, 128), f32),
            pltpu.VMEM((3, SLOTS, 8, 128), f32),
            pltpu.VMEM((2, SLOTS // 2, 8, 128), f32),
            pltpu.VMEM((3, SLOTS, 8, 128), f32),
            dma(()), dma((6, 3)), dma((6, 3)), dma((4, 3, 3)), dma((4, 3, 3)), dma((count,)), dma((count,)),
            dma((count, 4)), dma((count, 4)), dma((2, 2, 4)), dma((2, 2, 4)),
            dma((4,)), dma((3,)), dma((2, 4)), dma((2, 4)), dma((6,)), dma((6,)),
        ],
        compiler_params=pltpu.CompilerParams(collective_id=0, has_side_effects=True, vmem_limit_bytes=60 * 2**20),
        name="gram_tiles",
    )(snapshots, index)


def tile_index(table):
    a, b = table[:, 0], table[:, 1]
    za, ya, zb, yb = a // SIDE, a % SIDE, b // SIDE, b % SIDE
    dy, dz = (yb - ya) % SIDE, (zb - za) % SIDE
    own = jnp.where(dz == 2, 24 + za % 2, jnp.where(dz == 3, 20 + zb, 16 + 4 * dz + za))
    low = za < 2
    far_y = jnp.where(dz == 3, yb, jnp.where((dz == 0) & ~low, yb, ya))
    far_t = jnp.where(
        dz == 1, 26 + za, jnp.where(dz == 3, 26 + zb, jnp.where(dz == 0, 30 + za % 2, 32 + za))
    )
    which_y = jnp.where(dy == 2, far_y, jnp.where(dy == 3, yb, ya))
    which_t = jnp.where(
        dy == 0, own, jnp.where(dy == 1, 4 * za + zb, jnp.where(dy == 3, 4 * zb + za, far_t))
    )
    return jnp.where(a >= 0, which_y * TILES + which_t, SIDE * TILES)


def per_device(snapshots, tile_table):
    cells_dev = snapshots.shape[2]
    scale = 1.0 / math.sqrt(3 * cells_dev * lax.axis_size("space"))
    table = tile_table[0]
    slots = table.shape[0]
    index = jnp.broadcast_to(jnp.pad(tile_index(table), (0, 128 - slots)), (8, 128))
    tiles = gram(snapshots, index, scale).reshape(2, 2, slots, 8, 128)
    return tiles.transpose(2, 0, 3, 1, 4).reshape(1, slots, 16, BLOCK)


def solution(mesh):
    in_specs = (P(None, "tm", "space"), P("tm", None, None))
    out_specs = P("tm", None, "space", None)
    return jax.shard_map(
        per_device, mesh=mesh, in_specs=in_specs, out_specs=out_specs, check_vma=False
    )
```

```python
import math

import jax
import jax.numpy as jnp
from jax import lax
from jax.experimental import pallas as pl
from jax.experimental.pallas import tpu as pltpu
from jax.sharding import PartitionSpec as P

MESH = pl.DeviceIdType.MESH
BLOCK = 256
SIDE = 4
SLOTS = 20
TILES = 34
BATCHES = (8, 9, 6, 6, 5)
CHUNKS = ((0, 16), (16, 18))


def pick(index, values):
    chosen = values[0]
    for place in range(1, len(values)):
        chosen = jnp.where(index == place, values[place], chosen)
    return chosen


def tile_list(h, y):
    z = [lax.rem(h + step, SIDE) for step in range(SIDE)]
    same, near, back = y, lax.rem(y + 1, SIDE), lax.rem(y + 3, SIDE)

    def make(z1, y1, z2, y2, tile):
        first = z1 * SIDE + y1 <= z2 * SIDE + y2
        one, two = y1 * SIDE + z1, y2 * SIDE + z2
        return (jnp.where(first, one, two), jnp.where(first, two, one), tile)

    def own(a, b):
        step = (b - a) % SIDE
        base = lax.rem(z[a], 2) if step == 2 else z[a]
        return make(z[a], same, z[b], same, 16 + 4 * step + base)

    def side(a, b):
        return make(z[a], same, z[b], near, SIDE * z[a] + z[b])

    def across(a):
        b = (a + 1) % SIDE
        return make(z[a], back, z[b], near, 26 + z[a])

    half = jnp.where(back >= 2, 2, 0)
    return [
        own(0, 0), side(0, 0),
        own(3, 3), own(3, 0), side(0, 3), side(3, 0), side(3, 3), across(3),
        own(1, 1), own(0, 1), own(1, 3), side(1, 1), side(1, 0), side(0, 1), side(1, 3), side(3, 1), across(0),
        own(2, 2), own(1, 2), own(2, 3), own(0, 2), side(2, 0), side(0, 2), side(2, 1), side(1, 2), side(2, 2),
        side(2, 3), side(3, 2), across(1), across(2),
        make(half, back, half, near, 30), make(half + 1, back, half + 1, near, 31),
        make(0, back, 2, near, 32), make(1, back, 3, near, 33),
    ]


def kernel(
    scale, x_ref, index_ref, out_ref, blocks, relay, part, pair, xfirst, xlast, total, zpart,
    indices, wanted, pieces, chosen, through, landed,
    local_sem, zs, zr, ys, yr, ps, pr, xs, xr, ws, wr, ts, tr, gs, gr, os, onr,
):
    tm, space = lax.axis_index("tm"), lax.axis_index("space")
    h, y = tm // SIDE, lax.rem(tm, SIDE)
    x, low, core = space // SIDE, lax.rem(space // 2, 2), lax.rem(space, 2)

    def device(h_=h, y_=y, x_=x, low_=low, core_=core):
        return (h_ * SIDE + y_, x_ * SIDE + low_ * 2 + core_)

    def up(value, step, size=SIDE):
        return lax.rem(value + step, size)

    hp, hm, h2 = up(h, 1), up(h, 3), up(h, 2)
    yp, ym = up(y, 1), up(y, 3)
    xp, xm, x2 = up(x, 1), up(x, 3), up(x, 2)
    other = 1 - core
    place = h * 2 + low
    zp, zm = up(place, 1, 8), up(place, 7, 8)
    dev_hp, dev_hm, dev_h2 = device(h_=hp), device(h_=hm), device(h_=h2)
    dev_yp, dev_ym = device(y_=yp), device(y_=ym)
    dev_xp, dev_xm = device(x_=xp), device(x_=xm)
    dev_zp = device(h_=zp // 2, low_=lax.rem(zp, 2))
    dev_zm = device(h_=zm // 2, low_=lax.rem(zm, 2))
    dev_pair = device(core_=other)

    barrier = pltpu.get_barrier_semaphore()
    peers = (dev_hp, dev_hm, dev_h2, dev_yp, dev_ym, dev_xp, dev_xm, dev_zp, dev_zm, dev_pair)
    for peer in peers:
        pl.semaphore_signal(barrier, inc=1, device_id=peer, device_id_type=MESH)
    pl.semaphore_wait(barrier, len(peers))

    started = []

    def send(src, dst, send_sem, recv_sem, peer):
        copy = pltpu.make_async_remote_copy(
            src_ref=src, dst_ref=dst, send_sem=send_sem, recv_sem=recv_sem, device_id=peer, device_id_type=MESH
        )
        copy.start()
        started.append(copy)
        return copy

    def cells(which):
        return pl.ds(pl.multiple_of(which * BLOCK, BLOCK), BLOCK)

    every = slice(None)
    first_rows, last_rows = pl.ds(0, BLOCK // 2), pl.ds(BLOCK // 2, BLOCK // 2)

    local = pltpu.make_async_copy(x_ref.at[:, :, cells(h)], blocks.at[y, h], local_sem)
    local.start()
    own_index = pltpu.make_async_copy(index_ref, indices.at[h], ts.at[3])
    own_index.start()
    comps = range(3)
    to_hp, to_hm, via_hp, via_hm, on_hp, on_hm, moved = {}, {}, {}, {}, {}, {}, {}

    def near(k):
        to_hp[k] = send(x_ref.at[k, :, cells(hp)], blocks.at[y, h, k], zs.at[0, k], zr.at[0, k], dev_hp)
        to_hm[k] = send(x_ref.at[k, :, cells(hm)], blocks.at[y, h, k], zs.at[1, k], zr.at[1, k], dev_hm)

    def away(k):
        via_hp[k] = send(x_ref.at[k, first_rows, cells(h2)], relay.at[0, k], zs.at[2, k], zr.at[2, k], dev_hp)
        via_hm[k] = send(x_ref.at[k, last_rows, cells(h2)], relay.at[1, k], zs.at[3, k], zr.at[3, k], dev_hm)

    def spread(key, z, k, src=None):
        src = blocks.at[y, z, k] if src is None else src
        for way, peer in enumerate((dev_yp, dev_ym)):
            moved[key, k, way] = send(src, blocks.at[y, z, k], ys.at[key, k, way], yr.at[key, k, way], peer)

    def gathered(key):
        for k in comps:
            for way in range(2):
                moved[key, k, way].wait_recv()

    near(0)
    near(1)
    for k in comps:
        spread(0, h, k, x_ref.at[k, :, cells(h)])
    told = [
        send(index_ref, indices.at[h], ts.at[number], tr.at[number], peer)
        for number, peer in enumerate((dev_hp, dev_hm, dev_h2))
    ]

    def onward(k):
        via_hp[k].wait_recv()
        on_hp[k] = send(relay.at[0, k], blocks.at[y, hm, k, first_rows], zs.at[4, k], zr.at[4, k], dev_hp)
        via_hm[k].wait_recv()
        on_hm[k] = send(relay.at[1, k], blocks.at[y, hp, k, last_rows], zs.at[5, k], zr.at[5, k], dev_hm)

    def spread_far(k):
        on_hp[k].wait_recv()
        on_hm[k].wait_recv()
        spread(3, h2, k)

    tiles = tile_list(h, y)
    starts = [sum(BATCHES[:number]) for number in range(len(BATCHES))]

    def compute(number):
        begin, size = starts[number], BATCHES[number]
        some = tiles[begin:begin + size]

        @pl.loop(0, size)
        def _(step):
            left = pick(step, [tile[0] for tile in some])
            right = pick(step, [tile[1] for tile in some])
            ly, lz, ry, rz = left // SIDE, lax.rem(left, SIDE), right // SIDE, lax.rem(right, SIDE)
            product = None
            for comp in range(3):
                term = lax.dot_general(
                    blocks[ly, lz, comp], blocks[ry, rz, comp], (((1,), (1,)), ((), ())),
                    preferred_element_type=jnp.float32,
                )
                product = term if product is None else product + term
            slot = begin + step
            for row in range(BLOCK // 8):
                for lane in range(2):
                    place_x, place_low, place_core, place_row = row // 8, row // 4 % 2, row // 2 % 2, row % 2
                    part[slot, place_core, place_x, place_low * 4 + place_row * 2 + lane] = product[
                        row * 8:row * 8 + 8, lane * 128:lane * 128 + 128
                    ]

        span = pl.ds(begin, size)
        return send(part.at[span, other], pair.at[span], ps.at[number], pr.at[number], dev_pair)

    def add_pair(number, copy):
        begin, size = starts[number], BATCHES[number]
        copy.wait_recv()

        @pl.loop(begin, begin + size)
        def _(slot):
            part[slot, core] = part[slot, core] + pair[slot]

        span = pl.ds(begin, size)
        return (
            send(part.at[span, core, x2, pl.ds(0, 4)], xfirst.at[0, span], xs.at[number, 0], xr.at[number, 0], dev_xp),
            send(part.at[span, core, x2, pl.ds(4, 4)], xfirst.at[1, span], xs.at[number, 1], xr.at[number, 1], dev_xm),
        )

    def add_first(number, copies):
        begin, size = starts[number], BATCHES[number]
        for copy in copies:
            copy.wait_recv()

        @pl.loop(begin, begin + size)
        def _(slot):
            part[slot, core, xp, 0:4] = part[slot, core, xp, 0:4] + xfirst[0, slot]
            part[slot, core, xm, 4:8] = part[slot, core, xm, 4:8] + xfirst[1, slot]

        span = pl.ds(begin, size)
        return (
            send(part.at[span, core, xp], xlast.at[0, span], xs.at[number, 2], xr.at[number, 2], dev_xp),
            send(part.at[span, core, xm], xlast.at[1, span], xs.at[number, 3], xr.at[number, 3], dev_xm),
        )

    def add_last(number, copies):
        begin, size = starts[number], BATCHES[number]
        for copy in copies:
            copy.wait_recv()
        some = tiles[begin:begin + size]

        @pl.loop(0, size)
        def _(step):
            slot = begin + step
            total[pick(step, [tile[2] for tile in some])] = part[slot, core, x] + xlast[0, slot] + xlast[1, slot]

    to_hp[0].wait_recv()
    spread(1, hm, 0)
    to_hm[0].wait_recv()
    near(2)
    to_hp[1].wait_recv()
    spread(1, hm, 1)
    to_hm[1].wait_recv()
    away(0)
    spread(2, hp, 0)
    to_hp[2].wait_recv()
    spread(1, hm, 2)
    to_hm[2].wait_recv()
    away(1)
    away(2)
    spread(2, hp, 1)
    spread(2, hp, 2)
    local.wait()
    gathered(0)
    onward(0)
    gathered(1)
    pair0 = compute(0)
    onward(1)
    first0 = add_pair(0, pair0)
    onward(2)
    last0 = add_first(0, first0)
    gathered(2)
    pair1 = compute(1)
    spread_far(0)
    first1 = add_pair(1, pair1)
    spread_far(1)
    last1 = add_first(1, first1)
    spread_far(2)
    add_last(0, last0)
    gathered(3)
    pair2 = compute(2)
    pair3 = compute(3)
    first2 = add_pair(2, pair2)
    pair4 = compute(4)
    first3 = add_pair(3, pair3)
    add_last(1, last1)
    first4 = add_pair(4, pair4)
    last2 = add_first(2, first2)
    last3 = add_first(3, first3)
    last4 = add_first(4, first4)
    add_last(2, last2)
    add_last(3, last3)
    add_last(4, last4)

    def piece(step):
        target = up(place, step, 8)
        return lax.rem(target, 2) * 4 + target // 2

    rings = ((0, 0, 4), (1, 1, 4), (0, 1, 3), (1, 0, 3))
    flying = {}

    def pass_on(chunk, way, hops, number):
        begin, size = CHUNKS[chunk]
        span = pl.ds(begin, size)
        distance = hops - number
        which = piece(distance if way == 0 else 8 - distance)
        if number > 0:
            flying[chunk, way].wait_recv()
            total[begin:begin + size, which] = total[begin:begin + size, which] + zpart[way, number - 1, begin:begin + size]
        flying[chunk, way] = send(
            total.at[span, which], zpart.at[way, number, span],
            ws.at[chunk, way, number], wr.at[chunk, way, number], dev_zp if way == 0 else dev_zm,
        )

    for number in range(4):
        for chunk, way, hops in rings:
            if number < hops:
                pass_on(chunk, way, hops, number)

    pieces[SIDE * TILES] = jnp.zeros((8, 128), jnp.float32)
    shared, onto = {}, {}
    for chunk, (begin, size) in enumerate(CHUNKS):
        for way in range(2):
            flying[chunk, way].wait_recv()
        up_last, down_last = (3, 2) if chunk == 0 else (2, 3)
        end = begin + size
        value = total[begin:end, piece(0)] + zpart[0, up_last, begin:end] + zpart[1, down_last, begin:end]
        span = pl.ds(y * TILES + begin, size)
        pieces[span] = value * scale
        shared[chunk] = (
            send(pieces.at[span], pieces.at[span], gs.at[chunk, 0], gr.at[chunk, 0], dev_yp),
            send(pieces.at[span], pieces.at[span], gs.at[chunk, 1], gr.at[chunk, 1], dev_ym),
        )
    own_index.wait()
    for copy in told:
        copy.wait_recv()
    listed = pltpu.make_async_copy(indices, wanted, local_sem)
    listed.start()
    listed.wait()
    for chunk, (begin, size) in enumerate(CHUNKS):
        half = size // 2
        to_yp, to_ym = shared[chunk]
        to_yp.wait_recv()
        early = pl.ds(ym * TILES + begin, half)
        on_yp = send(pieces.at[early], pieces.at[early], gs.at[chunk, 2], gr.at[chunk, 2], dev_yp)
        to_ym.wait_recv()
        late = pl.ds(yp * TILES + begin + half, half)
        on_ym = send(pieces.at[late], pieces.at[late], gs.at[chunk, 3], gr.at[chunk, 3], dev_ym)
        onto[chunk] = (on_yp, on_ym)
    for chunk in range(len(CHUNKS)):
        for copy in onto[chunk]:
            copy.wait_recv()

    def choose(number, z):
        @pl.loop(0, SLOTS)
        def _(slot):
            chosen[number, slot] = pieces[wanted[z, 0, slot]]

    half = SLOTS // 2
    choose(2, h2)
    far_hp = send(chosen.at[2, pl.ds(0, half)], through.at[0], os.at[2], onr.at[2], dev_hp)
    far_hm = send(chosen.at[2, pl.ds(half, half)], through.at[1], os.at[3], onr.at[3], dev_hm)
    choose(0, hp)
    out_hp = send(chosen.at[0], landed.at[0], os.at[0], onr.at[0], dev_hp)
    choose(1, hm)
    out_hm = send(chosen.at[1], landed.at[1], os.at[1], onr.at[1], dev_hm)
    far_hp.wait_recv()
    last_hp = send(through.at[0], landed.at[2, pl.ds(0, half)], os.at[4], onr.at[4], dev_hp)
    far_hm.wait_recv()
    last_hm = send(through.at[1], landed.at[2, pl.ds(half, half)], os.at[5], onr.at[5], dev_hm)

    @pl.loop(0, SLOTS)
    def _(slot):
        out_ref[h, slot] = pieces[wanted[h, 0, slot]]

    out_hp.wait_recv()
    out_ref[hm] = landed[0]
    out_hm.wait_recv()
    out_ref[hp] = landed[1]
    last_hp.wait_recv()
    last_hm.wait_recv()
    out_ref[h2] = landed[2]
    for copy in started:
        copy.wait_send()


def gram(snapshots, index, scale):
    count = len(BATCHES)
    dma = pltpu.SemaphoreType.DMA
    f32, b16 = jnp.float32, jnp.bfloat16
    return pl.pallas_call(
        lambda *refs: kernel(scale, *refs),
        out_shape=jax.ShapeDtypeStruct((SIDE, SLOTS, 8, 128), f32),
        in_specs=[pl.BlockSpec(memory_space=pl.ANY)] * 2,
        out_specs=pl.BlockSpec(memory_space=pltpu.VMEM),
        scratch_shapes=[
            pltpu.VMEM((4, 4, 3, BLOCK, BLOCK), b16),
            pltpu.VMEM((2, 3, BLOCK // 2, BLOCK), b16),
            pltpu.VMEM((TILES, 2, 4, 8, 8, 128), f32),
            pltpu.VMEM((TILES, 4, 8, 8, 128), f32),
            pltpu.VMEM((2, TILES, 4, 8, 128), f32),
            pltpu.VMEM((2, TILES, 8, 8, 128), f32),
            pltpu.VMEM((TILES, 8, 8, 128), f32),
            pltpu.VMEM((2, 4, TILES, 8, 128), f32),
            pltpu.VMEM((SIDE, 8, 128), jnp.int32),
            pltpu.SMEM((SIDE, 8, 128), jnp.int32),
            pltpu.VMEM((SIDE * TILES + 1, 8, 128), f32),
            pltpu.VMEM((3, SLOTS, 8, 128), f32),
            pltpu.VMEM((2, SLOTS // 2, 8, 128), f32),
            pltpu.VMEM((3, SLOTS, 8, 128), f32),
            dma(()), dma((6, 3)), dma((6, 3)), dma((4, 3, 2)), dma((4, 3, 2)), dma((count,)), dma((count,)),
            dma((count, 4)), dma((count, 4)), dma((2, 2, 4)), dma((2, 2, 4)),
            dma((4,)), dma((3,)), dma((2, 4)), dma((2, 4)), dma((6,)), dma((6,)),
        ],
        compiler_params=pltpu.CompilerParams(collective_id=0, has_side_effects=True, vmem_limit_bytes=60 * 2**20),
        name="gram_tiles",
    )(snapshots, index)


def tile_index(table):
    a, b = table[:, 0], table[:, 1]
    za, ya, zb, yb = a // SIDE, a % SIDE, b // SIDE, b % SIDE
    dy, dz = (yb - ya) % SIDE, (zb - za) % SIDE
    own = jnp.where(dz == 2, 24 + za % 2, jnp.where(dz == 3, 20 + zb, 16 + 4 * dz + za))
    low = za < 2
    far_y = jnp.where(dz == 3, yb, jnp.where((dz == 0) & ~low, yb, ya))
    far_t = jnp.where(
        dz == 1, 26 + za, jnp.where(dz == 3, 26 + zb, jnp.where(dz == 0, 30 + za % 2, 32 + za))
    )
    which_y = jnp.where(dy == 2, (far_y + 1) % SIDE, jnp.where(dy == 3, yb, ya))
    which_t = jnp.where(
        dy == 0, own, jnp.where(dy == 1, 4 * za + zb, jnp.where(dy == 3, 4 * zb + za, far_t))
    )
    return jnp.where(a >= 0, which_y * TILES + which_t, SIDE * TILES)


def per_device(snapshots, tile_table):
    cells_dev = snapshots.shape[2]
    scale = 1.0 / math.sqrt(3 * cells_dev * lax.axis_size("space"))
    table = tile_table[0]
    slots = table.shape[0]
    index = jnp.broadcast_to(jnp.pad(tile_index(table), (0, 128 - slots)), (8, 128))
    tiles = gram(snapshots, index, scale).reshape(2, 2, slots, 8, 128)
    return tiles.transpose(2, 0, 3, 1, 4).reshape(1, slots, 16, BLOCK)


def solution(mesh):
    in_specs = (P(None, "tm", "space"), P("tm", None, None))
    out_specs = P("tm", None, "space", None)
    return jax.shard_map(
        per_device, mesh=mesh, in_specs=in_specs, out_specs=out_specs, check_vma=False
    )
```

```python
import math

import jax
import jax.numpy as jnp
from jax import lax
from jax.experimental import pallas as pl
from jax.experimental.pallas import tpu as pltpu
from jax.sharding import PartitionSpec as P

MESH = pl.DeviceIdType.MESH
BLOCK = 256
SIDE = 4
SLOTS = 20
TILES = 34
BATCHES = (7, 8, 6, 5, 8)
NEAR, FAR = 26, 8
CHUNKS = ((0, 14), (14, 12), (26, 4), (30, 4))
SHARES = ((26, 8), (0, 14), (14, 12))


def pick(index, values):
    chosen = values[0]
    for place in range(1, len(values)):
        chosen = jnp.where(index == place, values[place], chosen)
    return chosen


def tile_list(h, y):
    z = [lax.rem(h + step, SIDE) for step in range(SIDE)]
    same, near, back = y, lax.rem(y + 1, SIDE), lax.rem(y + 3, SIDE)

    def make(z1, y1, z2, y2, tile):
        first = z1 * SIDE + y1 <= z2 * SIDE + y2
        one, two = y1 * SIDE + z1, y2 * SIDE + z2
        return (jnp.where(first, one, two), jnp.where(first, two, one), tile)

    def own(a, b):
        step = (b - a) % SIDE
        base = lax.rem(z[a], 2) if step == 2 else z[a]
        return make(z[a], same, z[b], same, 16 + 4 * step + base)

    def side(a, b):
        return make(z[a], same, z[b], near, SIDE * z[a] + z[b])

    half = jnp.where(back >= 2, 2, 0)
    return [
        own(0, 0), side(0, 0), own(3, 3), own(3, 0), side(0, 3), side(3, 0), side(3, 3),
        own(1, 1), own(0, 1), own(1, 3), side(1, 1), side(1, 0), side(0, 1), side(1, 3), side(3, 1),
        own(2, 2), own(1, 2), own(2, 3), own(0, 2), side(2, 0), side(0, 2), side(2, 1), side(1, 2), side(2, 2),
        side(2, 3), side(3, 2),
        make(0, back, 1, near, 26), make(1, back, 2, near, 27), make(2, back, 3, near, 28), make(3, back, 0, near, 29),
        make(half, back, half, near, 30), make(half + 1, back, half + 1, near, 31),
        make(0, back, 2, near, 32), make(1, back, 3, near, 33),
    ]


def kernel(
    scale, x_ref, index_ref, out_ref, blocks, relay, part, pair, xfirst, xlast, total, zpart, zfar, zsum, xfar,
    indices, wanted, pieces, chosen, through, landed,
    local_sem, zs, zr, ys, yr, ps, pr, xs, xr, ws, wr, fs, fr, ts, tr, gs, gr, os, onr,
):
    tm, space = lax.axis_index("tm"), lax.axis_index("space")
    h, y = tm // SIDE, lax.rem(tm, SIDE)
    x, low, core = space // SIDE, lax.rem(space // 2, 2), lax.rem(space, 2)

    def device(h_=h, y_=y, x_=x, low_=low, core_=core):
        return (h_ * SIDE + y_, x_ * SIDE + low_ * 2 + core_)

    def up(value, step, size=SIDE):
        return lax.rem(value + step, size)

    hp, hm, h2 = up(h, 1), up(h, 3), up(h, 2)
    yp, ym = up(y, 1), up(y, 3)
    xp, xm, x2 = up(x, 1), up(x, 3), up(x, 2)
    other = 1 - core
    place = h * 2 + low
    zp, zm = up(place, 1, 8), up(place, 7, 8)
    dev_hp, dev_hm, dev_h2 = device(h_=hp), device(h_=hm), device(h_=h2)
    dev_yp, dev_ym = device(y_=yp), device(y_=ym)
    dev_xp, dev_xm = device(x_=xp), device(x_=xm)
    dev_zp = device(h_=zp // 2, low_=lax.rem(zp, 2))
    dev_zm = device(h_=zm // 2, low_=lax.rem(zm, 2))
    dev_pair = device(core_=other)

    barrier = pltpu.get_barrier_semaphore()
    peers = (dev_hp, dev_hm, dev_h2, dev_yp, dev_ym, dev_xp, dev_xm, dev_zp, dev_zm, dev_pair)
    for peer in peers:
        pl.semaphore_signal(barrier, inc=1, device_id=peer, device_id_type=MESH)
    pl.semaphore_wait(barrier, len(peers))

    started = []

    def send(src, dst, send_sem, recv_sem, peer):
        copy = pltpu.make_async_remote_copy(
            src_ref=src, dst_ref=dst, send_sem=send_sem, recv_sem=recv_sem, device_id=peer, device_id_type=MESH
        )
        copy.start()
        started.append(copy)
        return copy

    def cells(which):
        return pl.ds(pl.multiple_of(which * BLOCK, BLOCK), BLOCK)

    every = slice(None)
    first_rows, last_rows = pl.ds(0, BLOCK // 2), pl.ds(BLOCK // 2, BLOCK // 2)

    local = pltpu.make_async_copy(x_ref.at[:, :, cells(h)], blocks.at[y, h], local_sem)
    local.start()
    own_index = pltpu.make_async_copy(index_ref, indices.at[h], ts.at[3])
    own_index.start()
    comps = range(3)
    to_hp, to_hm, via_hp, via_hm, on_hp, on_hm, moved = {}, {}, {}, {}, {}, {}, {}

    def near(k):
        to_hp[k] = send(x_ref.at[k, :, cells(hp)], blocks.at[y, h, k], zs.at[0, k], zr.at[0, k], dev_hp)
        to_hm[k] = send(x_ref.at[k, :, cells(hm)], blocks.at[y, h, k], zs.at[1, k], zr.at[1, k], dev_hm)

    def away(k):
        via_hp[k] = send(x_ref.at[k, first_rows, cells(h2)], relay.at[0, k], zs.at[2, k], zr.at[2, k], dev_hp)
        via_hm[k] = send(x_ref.at[k, last_rows, cells(h2)], relay.at[1, k], zs.at[3, k], zr.at[3, k], dev_hm)

    def spread(key, z, k, src=None):
        src = blocks.at[y, z, k] if src is None else src
        for way, peer in enumerate((dev_yp, dev_ym)):
            moved[key, k, way] = send(src, blocks.at[y, z, k], ys.at[key, k, way], yr.at[key, k, way], peer)

    def gathered(key):
        for k in comps:
            for way in range(2):
                moved[key, k, way].wait_recv()

    near(0)
    near(1)
    for k in comps:
        spread(0, h, k, x_ref.at[k, :, cells(h)])
    told = [
        send(index_ref, indices.at[h], ts.at[number], tr.at[number], peer)
        for number, peer in enumerate((dev_hp, dev_hm, dev_h2))
    ]

    def onward(k):
        via_hp[k].wait_recv()
        on_hp[k] = send(relay.at[0, k], blocks.at[y, hm, k, first_rows], zs.at[4, k], zr.at[4, k], dev_hp)
        via_hm[k].wait_recv()
        on_hm[k] = send(relay.at[1, k], blocks.at[y, hp, k, last_rows], zs.at[5, k], zr.at[5, k], dev_hm)

    def spread_far(k):
        on_hp[k].wait_recv()
        on_hm[k].wait_recv()
        spread(3, h2, k)

    tiles = tile_list(h, y)
    starts = [sum(BATCHES[:number]) for number in range(len(BATCHES))]

    def compute(number):
        begin, size = starts[number], BATCHES[number]
        some = tiles[begin:begin + size]

        @pl.loop(0, size)
        def _(step):
            left = pick(step, [tile[0] for tile in some])
            right = pick(step, [tile[1] for tile in some])
            ly, lz, ry, rz = left // SIDE, lax.rem(left, SIDE), right // SIDE, lax.rem(right, SIDE)
            product = None
            for comp in range(3):
                term = lax.dot_general(
                    blocks[ly, lz, comp], blocks[ry, rz, comp], (((1,), (1,)), ((), ())),
                    preferred_element_type=jnp.float32,
                )
                product = term if product is None else product + term
            slot = begin + step
            for row in range(BLOCK // 8):
                for lane in range(2):
                    place_x, place_low, place_core, place_row = row // 8, row // 4 % 2, row // 2 % 2, row % 2
                    part[slot, place_core, place_x, place_low * 4 + place_row * 2 + lane] = product[
                        row * 8:row * 8 + 8, lane * 128:lane * 128 + 128
                    ]

        span = pl.ds(begin, size)
        return send(part.at[span, other], pair.at[span], ps.at[number], pr.at[number], dev_pair)

    def add_pair(number, copy):
        begin, size = starts[number], BATCHES[number]
        copy.wait_recv()

        @pl.loop(begin, begin + size)
        def _(slot):
            part[slot, core] = part[slot, core] + pair[slot]

        if begin == NEAR:
            return None
        span = pl.ds(begin, size)
        return (
            send(part.at[span, core, x2, pl.ds(0, 4)], xfirst.at[0, span], xs.at[number, 0], xr.at[number, 0], dev_xp),
            send(part.at[span, core, x2, pl.ds(4, 4)], xfirst.at[1, span], xs.at[number, 1], xr.at[number, 1], dev_xm),
        )

    def add_first(number, copies):
        begin, size = starts[number], BATCHES[number]
        for copy in copies:
            copy.wait_recv()

        @pl.loop(begin, begin + size)
        def _(slot):
            part[slot, core, xp, 0:4] = part[slot, core, xp, 0:4] + xfirst[0, slot]
            part[slot, core, xm, 4:8] = part[slot, core, xm, 4:8] + xfirst[1, slot]

        span = pl.ds(begin, size)
        return (
            send(part.at[span, core, xp], xlast.at[0, span], xs.at[number, 2], xr.at[number, 2], dev_xp),
            send(part.at[span, core, xm], xlast.at[1, span], xs.at[number, 3], xr.at[number, 3], dev_xm),
        )

    def add_last(number, copies):
        begin, size = starts[number], BATCHES[number]
        for copy in copies:
            copy.wait_recv()
        some = tiles[begin:begin + size]

        @pl.loop(0, size)
        def _(step):
            slot = begin + step
            total[pick(step, [tile[2] for tile in some])] = part[slot, core, x] + xlast[0, slot] + xlast[1, slot]

    def piece(step):
        target = up(place, step, 8)
        return lax.rem(target, 2) * 4 + target // 2

    flying = {}

    def pass_on(chunk, way, number):
        begin, size = CHUNKS[chunk]
        hops = 4 if chunk % 2 == way else 3
        if number >= hops:
            return
        distance = hops - number
        which = piece(distance if way == 0 else 8 - distance)
        if begin < NEAR:
            source, box, at, whole = total, zpart, (), ()
        else:
            source, box, at, whole = part, zfar, (core, every), (every,)
        if number > 0:
            flying[chunk, way].wait_recv()
            old = box[(way, number - 1, pl.ds(begin % NEAR, size)) + whole]
            where = (pl.ds(begin, size),) + at + (which,)
            source[where] = source[where] + old
        flying[chunk, way] = send(
            source.at[(pl.ds(begin, size),) + at + (which,)], box.at[way, number, pl.ds(begin % NEAR, size)],
            ws.at[chunk, way, number], wr.at[chunk, way, number], dev_zp if way == 0 else dev_zm,
        )

    def pass_all(chunks, number):
        for first in range(2):
            for chunk in chunks:
                pass_on(chunk, (chunk + first) % 2, number)

    def arrived(chunk):
        for way in range(2):
            flying[chunk, way].wait_recv()
        return (3, 2) if chunk % 2 == 0 else (2, 3)

    def far_sums():
        for chunk in (2, 3):
            begin, size = CHUNKS[chunk]
            above, below = arrived(chunk)
            here = begin - NEAR
            zsum[here:here + size] = (
                part[begin:begin + size, core, :, piece(0)]
                + zfar[0, above, here:here + size] + zfar[1, below, here:here + size]
            )
        first, rest = pl.ds(0, FAR // 2), pl.ds(FAR // 2, FAR // 2)
        return (
            send(zsum.at[first, x2], xfar.at[0, 0, first], fs.at[0], fr.at[0], dev_xp),
            send(zsum.at[rest, x2], xfar.at[0, 1, rest], fs.at[1], fr.at[1], dev_xm),
        )

    def far_cross(copies):
        middle = FAR // 2
        copies[0].wait_recv()
        zsum[0:middle, xp] = zsum[0:middle, xp] + xfar[0, 0, 0:middle]
        copies[1].wait_recv()
        zsum[middle:FAR, xm] = zsum[middle:FAR, xm] + xfar[0, 1, middle:FAR]
        return (
            send(zsum.at[:, xp], xfar.at[1, 0], fs.at[2], fr.at[2], dev_xp),
            send(zsum.at[:, xm], xfar.at[1, 1], fs.at[3], fr.at[3], dev_xm),
        )

    shared = {}

    def share(number, value):
        begin, size = SHARES[number]
        span = pl.ds(y * TILES + begin, size)
        pieces[span] = value * scale
        shared[number] = (
            send(pieces.at[span], pieces.at[span], gs.at[number, 0], gr.at[number, 0], dev_yp),
            send(pieces.at[span], pieces.at[span], gs.at[number, 1], gr.at[number, 1], dev_ym),
        )

    to_hp[0].wait_recv()
    spread(1, hm, 0)
    to_hm[0].wait_recv()
    near(2)
    to_hp[1].wait_recv()
    spread(1, hm, 1)
    to_hm[1].wait_recv()
    away(0)
    spread(2, hp, 0)
    to_hp[2].wait_recv()
    spread(1, hm, 2)
    to_hm[2].wait_recv()
    away(1)
    away(2)
    spread(2, hp, 1)
    spread(2, hp, 2)
    local.wait()
    gathered(0)
    onward(0)
    gathered(1)
    pair0 = compute(0)
    onward(1)
    first0 = add_pair(0, pair0)
    onward(2)
    last0 = add_first(0, first0)
    gathered(2)
    pair1 = compute(1)
    spread_far(0)
    first1 = add_pair(1, pair1)
    spread_far(1)
    last1 = add_first(1, first1)
    spread_far(2)
    add_last(0, last0)
    add_last(1, last1)
    gathered(3)
    pair2 = compute(2)
    pair4 = compute(4)
    first2 = add_pair(2, pair2)
    pair3 = compute(3)
    add_pair(4, pair4)
    pass_all((2, 3), 0)
    first3 = add_pair(3, pair3)
    last2 = add_first(2, first2)
    pass_all((2, 3), 1)
    last3 = add_first(3, first3)
    pass_all((2, 3), 2)
    add_last(2, last2)
    pass_all((2, 3), 3)
    add_last(3, last3)
    pass_all((0, 1), 0)
    far = far_sums()
    pass_all((0, 1), 1)
    far = far_cross(far)
    pass_all((0, 1), 2)
    for copy in far:
        copy.wait_recv()
    share(0, zsum[:, x] + xfar[1, 0] + xfar[1, 1])
    pass_all((0, 1), 3)
    for chunk in range(2):
        above, below = arrived(chunk)
        begin, end = CHUNKS[chunk][0], sum(CHUNKS[chunk])
        share(chunk + 1, total[begin:end, piece(0)] + zpart[0, above, begin:end] + zpart[1, below, begin:end])

    pieces[SIDE * TILES] = jnp.zeros((8, 128), jnp.float32)
    onto = {}
    own_index.wait()
    for copy in told:
        copy.wait_recv()
    listed = pltpu.make_async_copy(indices, wanted, local_sem)
    listed.start()
    listed.wait()
    for chunk, (begin, size) in enumerate(SHARES):
        half = size // 2
        to_yp, to_ym = shared[chunk]
        to_yp.wait_recv()
        early = pl.ds(ym * TILES + begin, half)
        on_yp = send(pieces.at[early], pieces.at[early], gs.at[chunk, 2], gr.at[chunk, 2], dev_yp)
        to_ym.wait_recv()
        late = pl.ds(yp * TILES + begin + half, half)
        on_ym = send(pieces.at[late], pieces.at[late], gs.at[chunk, 3], gr.at[chunk, 3], dev_ym)
        onto[chunk] = (on_yp, on_ym)
    for chunk in range(len(SHARES)):
        for copy in onto[chunk]:
            copy.wait_recv()

    def choose(number, z):
        @pl.loop(0, SLOTS)
        def _(slot):
            chosen[number, slot] = pieces[wanted[z, 0, slot]]

    half = SLOTS // 2
    choose(2, h2)
    far_hp = send(chosen.at[2, pl.ds(0, half)], through.at[0], os.at[2], onr.at[2], dev_hp)
    far_hm = send(chosen.at[2, pl.ds(half, half)], through.at[1], os.at[3], onr.at[3], dev_hm)
    choose(0, hp)
    out_hp = send(chosen.at[0], landed.at[0], os.at[0], onr.at[0], dev_hp)
    choose(1, hm)
    out_hm = send(chosen.at[1], landed.at[1], os.at[1], onr.at[1], dev_hm)
    far_hp.wait_recv()
    last_hp = send(through.at[0], landed.at[2, pl.ds(0, half)], os.at[4], onr.at[4], dev_hp)
    far_hm.wait_recv()
    last_hm = send(through.at[1], landed.at[2, pl.ds(half, half)], os.at[5], onr.at[5], dev_hm)

    @pl.loop(0, SLOTS)
    def _(slot):
        out_ref[h, slot] = pieces[wanted[h, 0, slot]]

    out_hp.wait_recv()
    out_ref[hm] = landed[0]
    out_hm.wait_recv()
    out_ref[hp] = landed[1]
    last_hp.wait_recv()
    last_hm.wait_recv()
    out_ref[h2] = landed[2]
    for copy in started:
        copy.wait_send()


def gram(snapshots, index, scale):
    count = len(BATCHES)
    dma = pltpu.SemaphoreType.DMA
    f32, b16 = jnp.float32, jnp.bfloat16
    return pl.pallas_call(
        lambda *refs: kernel(scale, *refs),
        out_shape=jax.ShapeDtypeStruct((SIDE, SLOTS, 8, 128), f32),
        in_specs=[pl.BlockSpec(memory_space=pl.ANY)] * 2,
        out_specs=pl.BlockSpec(memory_space=pltpu.VMEM),
        scratch_shapes=[
            pltpu.VMEM((4, 4, 3, BLOCK, BLOCK), b16),
            pltpu.VMEM((2, 3, BLOCK // 2, BLOCK), b16),
            pltpu.VMEM((TILES, 2, 4, 8, 8, 128), f32),
            pltpu.VMEM((TILES, 4, 8, 8, 128), f32),
            pltpu.VMEM((2, NEAR, 4, 8, 128), f32),
            pltpu.VMEM((2, NEAR, 8, 8, 128), f32),
            pltpu.VMEM((NEAR, 8, 8, 128), f32),
            pltpu.VMEM((2, 4, NEAR, 8, 128), f32),
            pltpu.VMEM((2, 4, FAR, 4, 8, 128), f32),
            pltpu.VMEM((FAR, 4, 8, 128), f32),
            pltpu.VMEM((2, 2, FAR, 8, 128), f32),
            pltpu.VMEM((SIDE, 8, 128), jnp.int32),
            pltpu.SMEM((SIDE, 8, 128), jnp.int32),
            pltpu.VMEM((SIDE * TILES + 1, 8, 128), f32),
            pltpu.VMEM((3, SLOTS, 8, 128), f32),
            pltpu.VMEM((2, SLOTS // 2, 8, 128), f32),
            pltpu.VMEM((3, SLOTS, 8, 128), f32),
            dma(()), dma((6, 3)), dma((6, 3)), dma((4, 3, 2)), dma((4, 3, 2)), dma((count,)), dma((count,)),
            dma((count, 4)), dma((count, 4)), dma((4, 2, 4)), dma((4, 2, 4)), dma((4,)), dma((4,)),
            dma((4,)), dma((3,)), dma((3, 4)), dma((3, 4)), dma((6,)), dma((6,)),
        ],
        compiler_params=pltpu.CompilerParams(collective_id=0, has_side_effects=True, vmem_limit_bytes=60 * 2**20),
        name="gram_tiles",
    )(snapshots, index)


def tile_index(table):
    a, b = table[:, 0], table[:, 1]
    za, ya, zb, yb = a // SIDE, a % SIDE, b // SIDE, b % SIDE
    dy, dz = (yb - ya) % SIDE, (zb - za) % SIDE
    own = jnp.where(dz == 2, 24 + za % 2, jnp.where(dz == 3, 20 + zb, 16 + 4 * dz + za))
    low = za < 2
    far_y = jnp.where(dz == 3, yb, jnp.where((dz == 0) & ~low, yb, ya))
    far_t = jnp.where(
        dz == 1, 26 + za, jnp.where(dz == 3, 26 + zb, jnp.where(dz == 0, 30 + za % 2, 32 + za))
    )
    which_y = jnp.where(dy == 2, (far_y + 1) % SIDE, jnp.where(dy == 3, yb, ya))
    which_t = jnp.where(
        dy == 0, own, jnp.where(dy == 1, 4 * za + zb, jnp.where(dy == 3, 4 * zb + za, far_t))
    )
    return jnp.where(a >= 0, which_y * TILES + which_t, SIDE * TILES)


def per_device(snapshots, tile_table):
    cells_dev = snapshots.shape[2]
    scale = 1.0 / math.sqrt(3 * cells_dev * lax.axis_size("space"))
    table = tile_table[0]
    slots = table.shape[0]
    index = jnp.broadcast_to(jnp.pad(tile_index(table), (0, 128 - slots)), (8, 128))
    tiles = gram(snapshots, index, scale).reshape(2, 2, slots, 8, 128)
    return tiles.transpose(2, 0, 3, 1, 4).reshape(1, slots, 16, BLOCK)


def solution(mesh):
    in_specs = (P(None, "tm", "space"), P("tm", None, None))
    out_specs = P("tm", None, "space", None)
    return jax.shard_map(
        per_device, mesh=mesh, in_specs=in_specs, out_specs=out_specs, check_vma=False
    )
```

```python
import math

import jax
import jax.numpy as jnp
from jax import lax
from jax.experimental import pallas as pl
from jax.experimental.pallas import tpu as pltpu
from jax.sharding import PartitionSpec as P

MESH = pl.DeviceIdType.MESH
BLOCK = 256
SIDE = 4
SLOTS = 20
TILES = 34
BATCHES = (2, 5, 8, 5, 6, 8)
NEAR, FAR = 26, 8
CHUNKS = ((0, 14), (14, 12), (26, 4), (30, 4))
SHARES = ((26, 8), (0, 14), (14, 12))


def tile_list(h, y):
    z = [lax.rem(h + step, SIDE) for step in range(SIDE)]
    same, near, back = y, lax.rem(y + 1, SIDE), lax.rem(y + 3, SIDE)

    def make(z1, y1, z2, y2, tile):
        first = z1 * SIDE + y1 <= z2 * SIDE + y2
        one, two = y1 * SIDE + z1, y2 * SIDE + z2
        return (jnp.where(first, one, two), jnp.where(first, two, one), tile)

    def own(a, b):
        step = (b - a) % SIDE
        base = lax.rem(z[a], 2) if step == 2 else z[a]
        return make(z[a], same, z[b], same, 16 + 4 * step + base)

    def side(a, b):
        return make(z[a], same, z[b], near, SIDE * z[a] + z[b])

    def across(a):
        return make(z[a], back, z[(a + 1) % SIDE], near, 26 + z[a])

    def level(a):
        return make(a, back, a, near, 30 + a - half)

    def cross(a):
        low = lax.rem(z[a], 2)
        return make(low, back, low + 2, near, 32 + low)

    half = jnp.where(back >= 2, 2, 0)
    early = jnp.where(z[2] == half, half + 1, half)
    late = 2 * half + 1 - early
    return [
        own(0, 0), side(0, 0), own(3, 3), own(3, 0), side(0, 3), side(3, 0), side(3, 3),
        own(1, 1), own(0, 1), own(1, 3), side(1, 1), side(1, 0), side(0, 1), side(1, 3), side(3, 1),
        own(2, 2), own(1, 2), own(2, 3), own(0, 2), side(2, 0), side(0, 2), side(2, 1), side(1, 2), side(2, 2),
        side(2, 3), side(3, 2),
        across(0), across(3), cross(1), level(early),
        across(1), across(2), cross(0), level(late),
    ]


def kernel(
    scale, x_ref, index_ref, out_ref, blocks, relay, part, pair, xfirst, xlast, total, zpart, zfar, zsum, xfar,
    indices, wanted, pieces, chosen, through, landed,
    local_sem, zs, zr, ys, yr, ps, pr, xs, xr, ws, wr, fs, fr, ts, tr, gs, gr, os, onr,
):
    tm, space = lax.axis_index("tm"), lax.axis_index("space")
    h, y = tm // SIDE, lax.rem(tm, SIDE)
    x, low, core = space // SIDE, lax.rem(space // 2, 2), lax.rem(space, 2)

    def device(h_=h, y_=y, x_=x, low_=low, core_=core):
        return (h_ * SIDE + y_, x_ * SIDE + low_ * 2 + core_)

    def up(value, step, size=SIDE):
        return lax.rem(value + step, size)

    hp, hm, h2 = up(h, 1), up(h, 3), up(h, 2)
    yp, ym = up(y, 1), up(y, 3)
    xp, xm, x2 = up(x, 1), up(x, 3), up(x, 2)
    other = 1 - core
    place = h * 2 + low
    zp, zm = up(place, 1, 8), up(place, 7, 8)
    dev_hp, dev_hm, dev_h2 = device(h_=hp), device(h_=hm), device(h_=h2)
    dev_yp, dev_ym = device(y_=yp), device(y_=ym)
    dev_xp, dev_xm = device(x_=xp), device(x_=xm)
    dev_zp = device(h_=zp // 2, low_=lax.rem(zp, 2))
    dev_zm = device(h_=zm // 2, low_=lax.rem(zm, 2))
    dev_pair = device(core_=other)

    barrier = pltpu.get_barrier_semaphore()
    peers = (dev_hp, dev_hm, dev_h2, dev_yp, dev_ym, dev_xp, dev_xm, dev_zp, dev_zm, dev_pair)
    for peer in peers:
        pl.semaphore_signal(barrier, inc=1, device_id=peer, device_id_type=MESH)
    pl.semaphore_wait(barrier, len(peers))

    started = []

    def send(src, dst, send_sem, recv_sem, peer):
        copy = pltpu.make_async_remote_copy(
            src_ref=src, dst_ref=dst, send_sem=send_sem, recv_sem=recv_sem, device_id=peer, device_id_type=MESH
        )
        copy.start()
        started.append(copy)
        return copy

    def cells(which):
        return pl.ds(pl.multiple_of(which * BLOCK, BLOCK), BLOCK)

    every = slice(None)
    first_rows, last_rows = pl.ds(0, BLOCK // 2), pl.ds(BLOCK // 2, BLOCK // 2)

    local = pltpu.make_async_copy(x_ref.at[:, :, cells(h)], blocks.at[y, h], local_sem)
    local.start()
    own_index = pltpu.make_async_copy(index_ref, indices.at[h], ts.at[3])
    own_index.start()
    comps = range(3)
    to_hp, to_hm, via_hp, via_hm, on_hp, on_hm, moved = {}, {}, {}, {}, {}, {}, {}

    def near(k):
        to_hp[k] = send(x_ref.at[k, :, cells(hp)], blocks.at[y, h, k], zs.at[0, k], zr.at[0, k], dev_hp)
        to_hm[k] = send(x_ref.at[k, :, cells(hm)], blocks.at[y, h, k], zs.at[1, k], zr.at[1, k], dev_hm)

    def away(k):
        via_hp[k] = send(x_ref.at[k, first_rows, cells(h2)], relay.at[0, k], zs.at[2, k], zr.at[2, k], dev_hp)
        via_hm[k] = send(x_ref.at[k, last_rows, cells(h2)], relay.at[1, k], zs.at[3, k], zr.at[3, k], dev_hm)

    def spread(key, z, k, src=None):
        src = blocks.at[y, z, k] if src is None else src
        for way, peer in enumerate((dev_yp, dev_ym)):
            moved[key, k, way] = send(src, blocks.at[y, z, k], ys.at[key, k, way], yr.at[key, k, way], peer)

    def gathered(key):
        for k in comps:
            for way in range(2):
                moved[key, k, way].wait_recv()

    near(0)
    near(1)
    for k in comps:
        spread(0, h, k, x_ref.at[k, :, cells(h)])
    told = [
        send(index_ref, indices.at[h], ts.at[number], tr.at[number], peer)
        for number, peer in enumerate((dev_hp, dev_hm, dev_h2))
    ]

    def onward(k):
        via_hp[k].wait_recv()
        on_hp[k] = send(relay.at[0, k], blocks.at[y, hm, k, first_rows], zs.at[4, k], zr.at[4, k], dev_hp)
        via_hm[k].wait_recv()
        on_hm[k] = send(relay.at[1, k], blocks.at[y, hp, k, last_rows], zs.at[5, k], zr.at[5, k], dev_hm)

    def spread_far(k):
        on_hp[k].wait_recv()
        on_hm[k].wait_recv()
        spread(3, h2, k)

    tiles = tile_list(h, y)
    starts = [sum(BATCHES[:number]) for number in range(len(BATCHES))]

    def compute(begin, size):
        for slot, (left, right, tile) in enumerate(tiles[begin:begin + size], begin):
            ly, lz, ry, rz = left // SIDE, lax.rem(left, SIDE), right // SIDE, lax.rem(right, SIDE)
            product = None
            for comp in range(3):
                term = lax.dot_general(
                    blocks[ly, lz, comp], blocks[ry, rz, comp], (((1,), (1,)), ((), ())),
                    preferred_element_type=jnp.float32,
                )
                product = term if product is None else product + term
            slot = tile if slot >= NEAR else slot
            for row in range(BLOCK // 8):
                for lane in range(2):
                    place_x, place_low, place_core, place_row = row // 8, row // 4 % 2, row // 2 % 2, row % 2
                    part[slot, place_core, place_x, place_low * 4 + place_row * 2 + lane] = product[
                        row * 8:row * 8 + 8, lane * 128:lane * 128 + 128
                    ]

    def swap(number):
        span = pl.ds(starts[number], BATCHES[number])
        return send(part.at[span, other], pair.at[span], ps.at[number], pr.at[number], dev_pair)

    def begin_batch(number):
        compute(starts[number], BATCHES[number])
        return swap(number)

    def add_pair(number, copy):
        begin, size = starts[number], BATCHES[number]
        copy.wait_recv()

        @pl.loop(begin, begin + size)
        def _(slot):
            part[slot, core] = part[slot, core] + pair[slot]

        if begin == NEAR:
            return None
        span = pl.ds(begin, size)
        return (
            send(part.at[span, core, x2, pl.ds(0, 4)], xfirst.at[0, span], xs.at[number, 0], xr.at[number, 0], dev_xp),
            send(part.at[span, core, x2, pl.ds(4, 4)], xfirst.at[1, span], xs.at[number, 1], xr.at[number, 1], dev_xm),
        )

    def add_first(number, copies):
        begin, size = starts[number], BATCHES[number]
        for copy in copies:
            copy.wait_recv()

        @pl.loop(begin, begin + size)
        def _(slot):
            part[slot, core, xp, 0:4] = part[slot, core, xp, 0:4] + xfirst[0, slot]
            part[slot, core, xm, 4:8] = part[slot, core, xm, 4:8] + xfirst[1, slot]

        span = pl.ds(begin, size)
        return (
            send(part.at[span, core, xp], xlast.at[0, span], xs.at[number, 2], xr.at[number, 2], dev_xp),
            send(part.at[span, core, xm], xlast.at[1, span], xs.at[number, 3], xr.at[number, 3], dev_xm),
        )

    def add_last(number, copies):
        begin, size = starts[number], BATCHES[number]
        for copy in copies:
            copy.wait_recv()
        for slot in range(begin, begin + size):
            total[tiles[slot][2]] = part[slot, core, x] + xlast[0, slot] + xlast[1, slot]

    def piece(step):
        target = up(place, step, 8)
        return lax.rem(target, 2) * 4 + target // 2

    flying = {}

    def pass_on(chunk, way, number):
        begin, size = CHUNKS[chunk]
        hops = 4 if chunk % 2 == way else 3
        if number >= hops:
            return
        distance = hops - number
        which = piece(distance if way == 0 else 8 - distance)
        if begin < NEAR:
            source, box, at, whole = total, zpart, (), ()
        else:
            source, box, at, whole = part, zfar, (core, every), (every,)
        if number > 0:
            flying[chunk, way].wait_recv()
            old = box[(way, number - 1, pl.ds(begin % NEAR, size)) + whole]
            where = (pl.ds(begin, size),) + at + (which,)
            source[where] = source[where] + old
        flying[chunk, way] = send(
            source.at[(pl.ds(begin, size),) + at + (which,)], box.at[way, number, pl.ds(begin % NEAR, size)],
            ws.at[chunk, way, number], wr.at[chunk, way, number], dev_zp if way == 0 else dev_zm,
        )

    def pass_all(chunks, number):
        for first in range(2):
            for chunk in chunks:
                pass_on(chunk, (chunk + first) % 2, number)

    def arrived(chunk):
        for way in range(2):
            flying[chunk, way].wait_recv()
        return (3, 2) if chunk % 2 == 0 else (2, 3)

    def far_sums():
        for chunk in (2, 3):
            begin, size = CHUNKS[chunk]
            above, below = arrived(chunk)
            here = begin - NEAR
            zsum[here:here + size] = (
                part[begin:begin + size, core, :, piece(0)]
                + zfar[0, above, here:here + size] + zfar[1, below, here:here + size]
            )
        first, rest = pl.ds(0, FAR // 2), pl.ds(FAR // 2, FAR // 2)
        return (
            send(zsum.at[first, x2], xfar.at[0, 0, first], fs.at[0], fr.at[0], dev_xp),
            send(zsum.at[rest, x2], xfar.at[0, 1, rest], fs.at[1], fr.at[1], dev_xm),
        )

    def far_cross(copies):
        middle = FAR // 2
        copies[0].wait_recv()
        zsum[0:middle, xp] = zsum[0:middle, xp] + xfar[0, 0, 0:middle]
        copies[1].wait_recv()
        zsum[middle:FAR, xm] = zsum[middle:FAR, xm] + xfar[0, 1, middle:FAR]
        return (
            send(zsum.at[:, xp], xfar.at[1, 0], fs.at[2], fr.at[2], dev_xp),
            send(zsum.at[:, xm], xfar.at[1, 1], fs.at[3], fr.at[3], dev_xm),
        )

    shared = {}

    def share(number, value):
        begin, size = SHARES[number]
        span = pl.ds(y * TILES + begin, size)
        pieces[span] = value * scale
        shared[number] = (
            send(pieces.at[span], pieces.at[span], gs.at[number, 0], gr.at[number, 0], dev_yp),
            send(pieces.at[span], pieces.at[span], gs.at[number, 1], gr.at[number, 1], dev_ym),
        )

    to_hp[0].wait_recv()
    spread(1, hm, 0)
    to_hm[0].wait_recv()
    near(2)
    local.wait()
    gathered(0)
    pair0 = begin_batch(0)
    to_hp[1].wait_recv()
    spread(1, hm, 1)
    to_hm[1].wait_recv()
    away(0)
    spread(2, hp, 0)
    first0 = add_pair(0, pair0)
    last0 = add_first(0, first0)
    to_hp[2].wait_recv()
    spread(1, hm, 2)
    to_hm[2].wait_recv()
    away(1)
    away(2)
    spread(2, hp, 1)
    spread(2, hp, 2)
    onward(0)
    add_last(0, last0)
    gathered(1)
    pair1 = begin_batch(1)
    onward(1)
    first1 = add_pair(1, pair1)
    onward(2)
    gathered(2)
    pair2 = begin_batch(2)
    last1 = add_first(1, first1)
    spread_far(0)
    first2 = add_pair(2, pair2)
    spread_far(1)
    compute(NEAR, 4)
    spread_far(2)
    last2 = add_first(2, first2)
    add_last(1, last1)
    gathered(3)
    pair3 = begin_batch(3)
    compute(NEAR + 4, 4)
    pair5 = swap(5)
    pair4 = begin_batch(4)
    first3 = add_pair(3, pair3)
    add_pair(5, pair5)
    pass_all((2, 3), 0)
    first4 = add_pair(4, pair4)
    last3 = add_first(3, first3)
    pass_all((2, 3), 1)
    last4 = add_first(4, first4)
    add_last(2, last2)
    pass_all((2, 3), 2)
    add_last(3, last3)
    pass_all((2, 3), 3)
    add_last(4, last4)
    pass_all((0, 1), 0)
    far = far_sums()
    pass_all((0, 1), 1)
    far = far_cross(far)
    pass_all((0, 1), 2)
    for copy in far:
        copy.wait_recv()
    share(0, zsum[:, x] + xfar[1, 0] + xfar[1, 1])
    pass_all((0, 1), 3)
    for chunk in range(2):
        above, below = arrived(chunk)
        begin, end = CHUNKS[chunk][0], sum(CHUNKS[chunk])
        share(chunk + 1, total[begin:end, piece(0)] + zpart[0, above, begin:end] + zpart[1, below, begin:end])

    pieces[SIDE * TILES] = jnp.zeros((8, 128), jnp.float32)
    onto = {}
    own_index.wait()
    for copy in told:
        copy.wait_recv()
    listed = pltpu.make_async_copy(indices, wanted, local_sem)
    listed.start()
    listed.wait()
    for chunk, (begin, size) in enumerate(SHARES):
        half = size // 2
        to_yp, to_ym = shared[chunk]
        to_yp.wait_recv()
        early = pl.ds(ym * TILES + begin, half)
        on_yp = send(pieces.at[early], pieces.at[early], gs.at[chunk, 2], gr.at[chunk, 2], dev_yp)
        to_ym.wait_recv()
        late = pl.ds(yp * TILES + begin + half, half)
        on_ym = send(pieces.at[late], pieces.at[late], gs.at[chunk, 3], gr.at[chunk, 3], dev_ym)
        onto[chunk] = (on_yp, on_ym)
    for chunk in range(len(SHARES)):
        for copy in onto[chunk]:
            copy.wait_recv()

    def choose(number, z):
        @pl.loop(0, SLOTS)
        def _(slot):
            chosen[number, slot] = pieces[wanted[z, 0, slot]]

    half = SLOTS // 2
    choose(2, h2)
    far_hp = send(chosen.at[2, pl.ds(0, half)], through.at[0], os.at[2], onr.at[2], dev_hp)
    far_hm = send(chosen.at[2, pl.ds(half, half)], through.at[1], os.at[3], onr.at[3], dev_hm)
    choose(0, hp)
    out_hp = send(chosen.at[0], landed.at[0], os.at[0], onr.at[0], dev_hp)
    choose(1, hm)
    out_hm = send(chosen.at[1], landed.at[1], os.at[1], onr.at[1], dev_hm)
    far_hp.wait_recv()
    last_hp = send(through.at[0], landed.at[2, pl.ds(0, half)], os.at[4], onr.at[4], dev_hp)
    far_hm.wait_recv()
    last_hm = send(through.at[1], landed.at[2, pl.ds(half, half)], os.at[5], onr.at[5], dev_hm)

    @pl.loop(0, SLOTS)
    def _(slot):
        out_ref[h, slot] = pieces[wanted[h, 0, slot]]

    out_hp.wait_recv()
    out_ref[hm] = landed[0]
    out_hm.wait_recv()
    out_ref[hp] = landed[1]
    last_hp.wait_recv()
    last_hm.wait_recv()
    out_ref[h2] = landed[2]
    for copy in started:
        copy.wait_send()


def gram(snapshots, index, scale):
    count = len(BATCHES)
    dma = pltpu.SemaphoreType.DMA
    f32, b16 = jnp.float32, jnp.bfloat16
    return pl.pallas_call(
        lambda *refs: kernel(scale, *refs),
        out_shape=jax.ShapeDtypeStruct((SIDE, SLOTS, 8, 128), f32),
        in_specs=[pl.BlockSpec(memory_space=pl.ANY)] * 2,
        out_specs=pl.BlockSpec(memory_space=pltpu.VMEM),
        scratch_shapes=[
            pltpu.VMEM((4, 4, 3, BLOCK, BLOCK), b16),
            pltpu.VMEM((2, 3, BLOCK // 2, BLOCK), b16),
            pltpu.VMEM((TILES, 2, 4, 8, 8, 128), f32),
            pltpu.VMEM((TILES, 4, 8, 8, 128), f32),
            pltpu.VMEM((2, NEAR, 4, 8, 128), f32),
            pltpu.VMEM((2, NEAR, 8, 8, 128), f32),
            pltpu.VMEM((NEAR, 8, 8, 128), f32),
            pltpu.VMEM((2, 4, NEAR, 8, 128), f32),
            pltpu.VMEM((2, 4, FAR, 4, 8, 128), f32),
            pltpu.VMEM((FAR, 4, 8, 128), f32),
            pltpu.VMEM((2, 2, FAR, 8, 128), f32),
            pltpu.VMEM((SIDE, 8, 128), jnp.int32),
            pltpu.SMEM((SIDE, 8, 128), jnp.int32),
            pltpu.VMEM((SIDE * TILES + 1, 8, 128), f32),
            pltpu.VMEM((3, SLOTS, 8, 128), f32),
            pltpu.VMEM((2, SLOTS // 2, 8, 128), f32),
            pltpu.VMEM((3, SLOTS, 8, 128), f32),
            dma(()), dma((6, 3)), dma((6, 3)), dma((4, 3, 2)), dma((4, 3, 2)), dma((count,)), dma((count,)),
            dma((count, 4)), dma((count, 4)), dma((4, 2, 4)), dma((4, 2, 4)), dma((4,)), dma((4,)),
            dma((4,)), dma((3,)), dma((3, 4)), dma((3, 4)), dma((6,)), dma((6,)),
        ],
        compiler_params=pltpu.CompilerParams(collective_id=0, has_side_effects=True, vmem_limit_bytes=60 * 2**20),
        name="gram_tiles",
    )(snapshots, index)


def tile_index(table):
    a, b = table[:, 0], table[:, 1]
    za, ya, zb, yb = a // SIDE, a % SIDE, b // SIDE, b % SIDE
    dy, dz = (yb - ya) % SIDE, (zb - za) % SIDE
    own = jnp.where(dz == 2, 24 + za % 2, jnp.where(dz == 3, 20 + zb, 16 + 4 * dz + za))
    low = za < 2
    far_y = jnp.where(dz == 3, yb, jnp.where((dz == 0) & ~low, yb, ya))
    far_t = jnp.where(
        dz == 1, 26 + za, jnp.where(dz == 3, 26 + zb, jnp.where(dz == 0, 30 + za % 2, 32 + za))
    )
    which_y = jnp.where(dy == 2, (far_y + 1) % SIDE, jnp.where(dy == 3, yb, ya))
    which_t = jnp.where(
        dy == 0, own, jnp.where(dy == 1, 4 * za + zb, jnp.where(dy == 3, 4 * zb + za, far_t))
    )
    return jnp.where(a >= 0, which_y * TILES + which_t, SIDE * TILES)


def per_device(snapshots, tile_table):
    cells_dev = snapshots.shape[2]
    scale = 1.0 / math.sqrt(3 * cells_dev * lax.axis_size("space"))
    table = tile_table[0]
    slots = table.shape[0]
    index = jnp.broadcast_to(jnp.pad(tile_index(table), (0, 128 - slots)), (8, 128))
    tiles = gram(snapshots, index, scale).reshape(2, 2, slots, 8, 128)
    return tiles.transpose(2, 0, 3, 1, 4).reshape(1, slots, 16, BLOCK)


def solution(mesh):
    in_specs = (P(None, "tm", "space"), P("tm", None, None))
    out_specs = P("tm", None, "space", None)
    return jax.shard_map(
        per_device, mesh=mesh, in_specs=in_specs, out_specs=out_specs, check_vma=False
    )
```

```python
import math

import jax
import jax.numpy as jnp
from jax import lax
from jax.experimental import pallas as pl
from jax.experimental.pallas import tpu as pltpu
from jax.sharding import PartitionSpec as P

MESH = pl.DeviceIdType.MESH
BLOCK = 256
SIDE = 4
SLOTS = 20
TILES = 34
BATCHES = (2, 5, 8, 5, 6, 8)
NEAR, FAR = 26, 8
CHUNKS = ((0, 7), (7, 7), (14, 6), (20, 6), (26, 4), (30, 4))
SHARES = ((26, 8), (0, 14), (14, 12))


def tile_list(h, y):
    z = [lax.rem(h + step, SIDE) for step in range(SIDE)]
    same, near, back = y, lax.rem(y + 1, SIDE), lax.rem(y + 3, SIDE)

    def make(z1, y1, z2, y2, tile):
        first = z1 * SIDE + y1 <= z2 * SIDE + y2
        one, two = y1 * SIDE + z1, y2 * SIDE + z2
        return (jnp.where(first, one, two), jnp.where(first, two, one), tile)

    def own(a, b):
        step = (b - a) % SIDE
        base = 12 + lax.rem(z[a], 2) if step == 2 else z[a] + (22 if step == 1 else 8)
        return make(z[a], same, z[b], same, base)

    def side(a, b):
        step = (b - a) % SIDE
        return make(z[a], same, z[b], near, z[a] + (0, 4, 14, 18)[step])

    def across(a):
        return make(z[a], back, z[(a + 1) % SIDE], near, 26 + z[a])

    def level(a):
        return make(a, back, a, near, 30 + a - half)

    def cross(a):
        low = lax.rem(z[a], 2)
        return make(low, back, low + 2, near, 32 + low)

    half = jnp.where(back >= 2, 2, 0)
    early = jnp.where(z[2] == half, half + 1, half)
    late = 2 * half + 1 - early
    return [
        own(0, 0), side(0, 0), own(3, 3), own(3, 0), side(0, 3), side(3, 0), side(3, 3),
        own(1, 1), own(0, 1), own(1, 3), side(1, 1), side(1, 0), side(0, 1), side(1, 3), side(3, 1),
        own(2, 2), own(0, 2), side(2, 2), side(2, 3), side(1, 2),
        own(1, 2), own(2, 3), side(2, 0), side(0, 2), side(2, 1), side(3, 2),
        across(0), across(3), cross(1), level(early),
        across(1), across(2), cross(0), level(late),
    ]


def tile_index(a, b):
    za, ya, zb, yb = a >> 2, a & 3, b >> 2, b & 3
    dy, dz, back = (yb - ya) & 3, (zb - za) & 3, (za - zb) & 3
    own = jnp.where(dz == 2, 12 + (za & 1), jnp.where(dz == 3, 22 + zb, za + jnp.where(dz == 1, 22, 8)))
    right = za + 4 * dz + jnp.where(dz >= 2, 6, 0)
    left = zb + 4 * back + jnp.where(back >= 2, 6, 0)
    far_y = jnp.where((dz == 3) | ((dz == 0) & (za >= 2)), yb, ya)
    far = jnp.where(dz == 1, 26 + za, jnp.where(dz == 3, 26 + zb, jnp.where(dz == 0, 30 + (za & 1), 32 + za)))
    which_y = jnp.where(dy == 2, (far_y + 1) & 3, jnp.where(dy == 3, yb, ya))
    which = jnp.where(dy == 0, own, jnp.where(dy == 1, right, jnp.where(dy == 3, left, far)))
    return jnp.where(a >= 0, which_y * TILES + which, SIDE * TILES)


def kernel(
    scale, x_ref, table_ref, out_ref, blocks, relay, part, pair, xfirst, xlast, total, zpart, zfar, zsum, xfar,
    indices, wanted, pieces, chosen, through, landed,
    local_sem, zs, zr, ys, yr, ps, pr, xs, xr, ws, wr, fs, fr, ts, tr, gs, gr, os, onr,
):
    tm, space = lax.axis_index("tm"), lax.axis_index("space")
    h, y = tm // SIDE, lax.rem(tm, SIDE)
    x, low, core = space // SIDE, lax.rem(space // 2, 2), lax.rem(space, 2)

    def device(h_=h, y_=y, x_=x, low_=low, core_=core):
        return (h_ * SIDE + y_, x_ * SIDE + low_ * 2 + core_)

    def up(value, step, size=SIDE):
        return lax.rem(value + step, size)

    hp, hm, h2 = up(h, 1), up(h, 3), up(h, 2)
    yp, ym = up(y, 1), up(y, 3)
    xp, xm, x2 = up(x, 1), up(x, 3), up(x, 2)
    other = 1 - core
    place = h * 2 + low
    zp, zm = up(place, 1, 8), up(place, 7, 8)
    dev_hp, dev_hm = device(h_=hp), device(h_=hm)
    dev_yp, dev_ym = device(y_=yp), device(y_=ym)
    dev_xp, dev_xm = device(x_=xp), device(x_=xm)
    dev_zp = device(h_=zp // 2, low_=lax.rem(zp, 2))
    dev_zm = device(h_=zm // 2, low_=lax.rem(zm, 2))
    dev_pair = device(core_=other)

    barrier = pltpu.get_barrier_semaphore()
    peers = (dev_hp, dev_hm, dev_yp, dev_ym, dev_xp, dev_xm, dev_zp, dev_zm, dev_pair)
    for peer in peers:
        pl.semaphore_signal(barrier, inc=1, device_id=peer, device_id_type=MESH)
    pl.semaphore_wait(barrier, len(peers))

    started = []

    def send(src, dst, send_sem, recv_sem, peer):
        copy = pltpu.make_async_remote_copy(
            src_ref=src, dst_ref=dst, send_sem=send_sem, recv_sem=recv_sem, device_id=peer, device_id_type=MESH
        )
        copy.start()
        started.append(copy)
        return copy

    def cells(which):
        return pl.ds(pl.multiple_of(which * BLOCK, BLOCK), BLOCK)

    every = slice(None)
    first_rows, last_rows = pl.ds(0, BLOCK // 2), pl.ds(BLOCK // 2, BLOCK // 2)

    local = pltpu.make_async_copy(x_ref.at[:, :, cells(h)], blocks.at[y, h], local_sem)
    local.start()
    comps = range(3)
    to_hp, to_hm, via_hp, via_hm, on_hp, on_hm, moved = {}, {}, {}, {}, {}, {}, {}

    def near(k):
        to_hp[k] = send(x_ref.at[k, :, cells(hp)], blocks.at[y, h, k], zs.at[0, k], zr.at[0, k], dev_hp)
        to_hm[k] = send(x_ref.at[k, :, cells(hm)], blocks.at[y, h, k], zs.at[1, k], zr.at[1, k], dev_hm)

    def away(k):
        via_hp[k] = send(x_ref.at[k, first_rows, cells(h2)], relay.at[0, k], zs.at[2, k], zr.at[2, k], dev_hp)
        via_hm[k] = send(x_ref.at[k, last_rows, cells(h2)], relay.at[1, k], zs.at[3, k], zr.at[3, k], dev_hm)

    def spread(key, z, k, src=None):
        src = blocks.at[y, z, k] if src is None else src
        for way, peer in enumerate((dev_yp, dev_ym)):
            moved[key, k, way] = send(src, blocks.at[y, z, k], ys.at[key, k, way], yr.at[key, k, way], peer)

    def gathered(key):
        for k in comps:
            for way in range(2):
                moved[key, k, way].wait_recv()

    near(0)
    near(1)
    for k in comps:
        spread(0, h, k, x_ref.at[k, :, cells(h)])
    indices[h] = jnp.zeros((8, 128), jnp.int32)
    indices[h, 0:1, 0:SLOTS] = tile_index(table_ref[0, 0:1, :], table_ref[0, 1:2, :])
    told = [
        send(indices.at[h], indices.at[h], ts.at[number], tr.at[number], peer)
        for number, peer in enumerate((dev_hp, dev_hm))
    ]

    def onward(k):
        via_hp[k].wait_recv()
        on_hp[k] = send(relay.at[0, k], blocks.at[y, hm, k, first_rows], zs.at[4, k], zr.at[4, k], dev_hp)
        via_hm[k].wait_recv()
        on_hm[k] = send(relay.at[1, k], blocks.at[y, hp, k, last_rows], zs.at[5, k], zr.at[5, k], dev_hm)

    def spread_far(k):
        on_hp[k].wait_recv()
        on_hm[k].wait_recv()
        spread(3, h2, k)

    tiles = tile_list(h, y)
    starts = [sum(BATCHES[:number]) for number in range(len(BATCHES))]

    def compute(begin, size):
        for slot, (left, right, tile) in enumerate(tiles[begin:begin + size], begin):
            ly, lz, ry, rz = left // SIDE, lax.rem(left, SIDE), right // SIDE, lax.rem(right, SIDE)
            product = None
            for comp in range(3):
                term = lax.dot_general(
                    blocks[ly, lz, comp], blocks[ry, rz, comp], (((1,), (1,)), ((), ())),
                    preferred_element_type=jnp.float32,
                )
                product = term if product is None else product + term
            slot = tile if slot >= NEAR else slot
            for row in range(BLOCK // 8):
                for lane in range(2):
                    place_x, place_low, place_core, place_row = row // 8, row // 4 % 2, row // 2 % 2, row % 2
                    part[slot, place_core, place_x, place_low * 4 + place_row * 2 + lane] = product[
                        row * 8:row * 8 + 8, lane * 128:lane * 128 + 128
                    ]

    def swap(number):
        span = pl.ds(starts[number], BATCHES[number])
        return send(part.at[span, other], pair.at[span], ps.at[number], pr.at[number], dev_pair)

    def begin_batch(number):
        compute(starts[number], BATCHES[number])
        return swap(number)

    def add_pair(number, copy):
        begin, size = starts[number], BATCHES[number]
        copy.wait_recv()

        @pl.loop(begin, begin + size)
        def _(slot):
            part[slot, core] = part[slot, core] + pair[slot]

        if begin == NEAR:
            return None
        span = pl.ds(begin, size)
        return (
            send(part.at[span, core, x2, pl.ds(0, 4)], xfirst.at[0, span], xs.at[number, 0], xr.at[number, 0], dev_xp),
            send(part.at[span, core, x2, pl.ds(4, 4)], xfirst.at[1, span], xs.at[number, 1], xr.at[number, 1], dev_xm),
        )

    def add_first(number, copies):
        begin, size = starts[number], BATCHES[number]
        for copy in copies:
            copy.wait_recv()

        @pl.loop(begin, begin + size)
        def _(slot):
            part[slot, core, xp, 0:4] = part[slot, core, xp, 0:4] + xfirst[0, slot]
            part[slot, core, xm, 4:8] = part[slot, core, xm, 4:8] + xfirst[1, slot]

        span = pl.ds(begin, size)
        return (
            send(part.at[span, core, xp], xlast.at[0, span], xs.at[number, 2], xr.at[number, 2], dev_xp),
            send(part.at[span, core, xm], xlast.at[1, span], xs.at[number, 3], xr.at[number, 3], dev_xm),
        )

    def add_last(number, copies):
        begin, size = starts[number], BATCHES[number]
        for copy in copies:
            copy.wait_recv()
        for slot in range(begin, begin + size):
            total[tiles[slot][2]] = part[slot, core, x] + xlast[0, slot] + xlast[1, slot]

    def piece(step):
        target = up(place, step, 8)
        return lax.rem(target, 2) * 4 + target // 2

    flying = {}

    def pass_on(chunk, way, number):
        begin, size = CHUNKS[chunk]
        hops = 4 if chunk % 2 == way else 3
        if number >= hops:
            return
        distance = hops - number
        which = piece(distance if way == 0 else 8 - distance)
        if begin < NEAR:
            source, box, at, whole = total, zpart, (), ()
        else:
            source, box, at, whole = part, zfar, (core, every), (every,)
        if number > 0:
            flying[chunk, way].wait_recv()
            old = box[(way, number - 1, pl.ds(begin % NEAR, size)) + whole]
            where = (pl.ds(begin, size),) + at + (which,)
            source[where] = source[where] + old
        flying[chunk, way] = send(
            source.at[(pl.ds(begin, size),) + at + (which,)], box.at[way, number, pl.ds(begin % NEAR, size)],
            ws.at[chunk, way, number], wr.at[chunk, way, number], dev_zp if way == 0 else dev_zm,
        )

    def pass_all(chunks, number):
        for first in range(2):
            for chunk in chunks:
                pass_on(chunk, (chunk + first) % 2, number)

    def arrived(chunk):
        for way in range(2):
            flying[chunk, way].wait_recv()
        return (3, 2) if chunk % 2 == 0 else (2, 3)

    def far_sums():
        for chunk in (4, 5):
            begin, size = CHUNKS[chunk]
            above, below = arrived(chunk)
            here = begin - NEAR
            zsum[here:here + size] = (
                part[begin:begin + size, core, :, piece(0)]
                + zfar[0, above, here:here + size] + zfar[1, below, here:here + size]
            )
        first, rest = pl.ds(0, FAR // 2), pl.ds(FAR // 2, FAR // 2)
        return (
            send(zsum.at[first, x2], xfar.at[0, 0, first], fs.at[0], fr.at[0], dev_xp),
            send(zsum.at[rest, x2], xfar.at[0, 1, rest], fs.at[1], fr.at[1], dev_xm),
        )

    def far_cross(copies):
        middle = FAR // 2
        copies[0].wait_recv()
        zsum[0:middle, xp] = zsum[0:middle, xp] + xfar[0, 0, 0:middle]
        copies[1].wait_recv()
        zsum[middle:FAR, xm] = zsum[middle:FAR, xm] + xfar[0, 1, middle:FAR]
        return (
            send(zsum.at[:, xp], xfar.at[1, 0], fs.at[2], fr.at[2], dev_xp),
            send(zsum.at[:, xm], xfar.at[1, 1], fs.at[3], fr.at[3], dev_xm),
        )

    shared = {}

    def share(number, value):
        begin, size = SHARES[number]
        span = pl.ds(y * TILES + begin, size)
        pieces[span] = value * scale
        shared[number] = (
            send(pieces.at[span], pieces.at[span], gs.at[number, 0], gr.at[number, 0], dev_yp),
            send(pieces.at[span], pieces.at[span], gs.at[number, 1], gr.at[number, 1], dev_ym),
        )

    def share_near(number, chunks):
        parts = []
        for chunk in chunks:
            above, below = arrived(chunk)
            begin, end = CHUNKS[chunk][0], sum(CHUNKS[chunk])
            parts.append(total[begin:end, piece(0)] + zpart[0, above, begin:end] + zpart[1, below, begin:end])
        share(number, jnp.concatenate(parts))

    to_hp[0].wait_recv()
    spread(1, hm, 0)
    to_hm[0].wait_recv()
    near(2)
    local.wait()
    gathered(0)
    pair0 = begin_batch(0)
    to_hp[1].wait_recv()
    spread(1, hm, 1)
    to_hm[1].wait_recv()
    away(0)
    spread(2, hp, 0)
    first0 = add_pair(0, pair0)
    last0 = add_first(0, first0)
    to_hp[2].wait_recv()
    spread(1, hm, 2)
    to_hm[2].wait_recv()
    away(1)
    away(2)
    spread(2, hp, 1)
    spread(2, hp, 2)
    onward(0)
    add_last(0, last0)
    told[0].wait_recv()
    told.append(send(indices.at[hm], indices.at[hm], ts.at[2], tr.at[2], dev_hp))
    gathered(1)
    pair1 = begin_batch(1)
    onward(1)
    first1 = add_pair(1, pair1)
    onward(2)
    gathered(2)
    pair2 = begin_batch(2)
    last1 = add_first(1, first1)
    spread_far(0)
    first2 = add_pair(2, pair2)
    spread_far(1)
    compute(NEAR, 4)
    spread_far(2)
    last2 = add_first(2, first2)
    add_last(1, last1)
    gathered(3)
    pair3 = begin_batch(3)
    compute(NEAR + 4, 4)
    pair5 = swap(5)
    pair4 = begin_batch(4)
    first3 = add_pair(3, pair3)
    add_pair(5, pair5)
    pass_all((4, 5), 0)
    first4 = add_pair(4, pair4)
    last3 = add_first(3, first3)
    pass_all((4, 5), 1)
    add_last(2, last2)
    last4 = add_first(4, first4)
    pass_all((4, 5), 2)
    add_last(3, last3)
    pass_all((0, 1), 0)
    pass_all((4, 5), 3)
    pass_all((0, 1), 1)
    add_last(4, last4)
    pass_all((2, 3), 0)
    far = far_sums()
    pass_all((0, 1), 2)
    pass_all((2, 3), 1)
    far = far_cross(far)
    pass_all((0, 1), 3)
    pass_all((2, 3), 2)
    for copy in far:
        copy.wait_recv()
    share(0, zsum[:, x] + xfar[1, 0] + xfar[1, 1])
    share_near(1, (0, 1))
    pass_all((2, 3), 3)
    share_near(2, (2, 3))

    pieces[SIDE * TILES] = jnp.zeros((8, 128), jnp.float32)
    onto = {}
    told[1].wait_recv()
    told[2].wait_recv()
    listed = pltpu.make_async_copy(indices, wanted, local_sem)
    listed.start()
    listed.wait()
    for chunk, (begin, size) in enumerate(SHARES):
        half = size // 2
        to_yp, to_ym = shared[chunk]
        to_yp.wait_recv()
        early = pl.ds(ym * TILES + begin, half)
        on_yp = send(pieces.at[early], pieces.at[early], gs.at[chunk, 2], gr.at[chunk, 2], dev_yp)
        to_ym.wait_recv()
        late = pl.ds(yp * TILES + begin + half, half)
        on_ym = send(pieces.at[late], pieces.at[late], gs.at[chunk, 3], gr.at[chunk, 3], dev_ym)
        onto[chunk] = (on_yp, on_ym)
    for chunk in range(len(SHARES)):
        for copy in onto[chunk]:
            copy.wait_recv()

    def choose(number, z):
        @pl.loop(0, SLOTS)
        def _(slot):
            chosen[number, slot] = pieces[wanted[z, 0, slot]]

    half = SLOTS // 2
    choose(2, h2)
    far_hp = send(chosen.at[2, pl.ds(0, half)], through.at[0], os.at[2], onr.at[2], dev_hp)
    far_hm = send(chosen.at[2, pl.ds(half, half)], through.at[1], os.at[3], onr.at[3], dev_hm)
    choose(0, hp)
    out_hp = send(chosen.at[0], landed.at[0], os.at[0], onr.at[0], dev_hp)
    choose(1, hm)
    out_hm = send(chosen.at[1], landed.at[1], os.at[1], onr.at[1], dev_hm)
    far_hp.wait_recv()
    last_hp = send(through.at[0], landed.at[2, pl.ds(0, half)], os.at[4], onr.at[4], dev_hp)
    far_hm.wait_recv()
    last_hm = send(through.at[1], landed.at[2, pl.ds(half, half)], os.at[5], onr.at[5], dev_hm)

    def put(z, slot, value):
        rows, lanes = pl.multiple_of(z // 2 * 8, 8), pl.multiple_of(lax.rem(z, 2) * 128, 128)
        out_ref[0, slot, pl.ds(rows, 8), pl.ds(lanes, 128)] = value

    for slot in range(SLOTS):
        put(h, slot, pieces[wanted[h, 0, slot]])
    out_hp.wait_recv()
    for slot in range(SLOTS):
        put(hm, slot, landed[0, slot])
    out_hm.wait_recv()
    for slot in range(SLOTS):
        put(hp, slot, landed[1, slot])
    last_hp.wait_recv()
    last_hm.wait_recv()
    for slot in range(SLOTS):
        put(h2, slot, landed[2, slot])
    for copy in started:
        copy.wait_send()


def gram(snapshots, table, scale):
    count = len(BATCHES)
    dma = pltpu.SemaphoreType.DMA
    f32, b16 = jnp.float32, jnp.bfloat16
    return pl.pallas_call(
        lambda *refs: kernel(scale, *refs),
        out_shape=jax.ShapeDtypeStruct((1, SLOTS, 16, BLOCK), f32),
        in_specs=[pl.BlockSpec(memory_space=pl.ANY), pl.BlockSpec(memory_space=pltpu.VMEM)],
        out_specs=pl.BlockSpec(memory_space=pltpu.VMEM),
        scratch_shapes=[
            pltpu.VMEM((4, 4, 3, BLOCK, BLOCK), b16),
            pltpu.VMEM((2, 3, BLOCK // 2, BLOCK), b16),
            pltpu.VMEM((TILES, 2, 4, 8, 8, 128), f32),
            pltpu.VMEM((TILES, 4, 8, 8, 128), f32),
            pltpu.VMEM((2, NEAR, 4, 8, 128), f32),
            pltpu.VMEM((2, NEAR, 8, 8, 128), f32),
            pltpu.VMEM((NEAR, 8, 8, 128), f32),
            pltpu.VMEM((2, 4, NEAR, 8, 128), f32),
            pltpu.VMEM((2, 4, FAR, 4, 8, 128), f32),
            pltpu.VMEM((FAR, 4, 8, 128), f32),
            pltpu.VMEM((2, 2, FAR, 8, 128), f32),
            pltpu.VMEM((SIDE, 8, 128), jnp.int32),
            pltpu.SMEM((SIDE, 8, 128), jnp.int32),
            pltpu.VMEM((SIDE * TILES + 1, 8, 128), f32),
            pltpu.VMEM((3, SLOTS, 8, 128), f32),
            pltpu.VMEM((2, SLOTS // 2, 8, 128), f32),
            pltpu.VMEM((3, SLOTS, 8, 128), f32),
            dma(()), dma((6, 3)), dma((6, 3)), dma((4, 3, 2)), dma((4, 3, 2)), dma((count,)), dma((count,)),
            dma((count, 4)), dma((count, 4)), dma((6, 2, 4)), dma((6, 2, 4)), dma((4,)), dma((4,)),
            dma((3,)), dma((3,)), dma((3, 4)), dma((3, 4)), dma((6,)), dma((6,)),
        ],
        compiler_params=pltpu.CompilerParams(collective_id=0, has_side_effects=True, vmem_limit_bytes=60 * 2**20),
        name="gram_tiles",
    )(snapshots, table)


def per_device(snapshots, tile_table):
    scale = 1.0 / math.sqrt(3 * snapshots.shape[2] * lax.axis_size("space"))
    return gram(snapshots, jnp.transpose(tile_table, (0, 2, 1)), scale)


def solution(mesh):
    in_specs = (P(None, "tm", "space"), P("tm", None, None))
    out_specs = P("tm", None, "space", None)
    return jax.shard_map(
        per_device, mesh=mesh, in_specs=in_specs, out_specs=out_specs, check_vma=False
    )
```

```python
import math

import jax
import jax.numpy as jnp
from jax import lax
from jax.experimental import pallas as pl
from jax.experimental.pallas import tpu as pltpu
from jax.sharding import PartitionSpec as P

MESH = pl.DeviceIdType.MESH
BLOCK = 256
SIDE = 4
SLOTS = 20
TILES = 34
BATCHES = (1, 4, 8, 5, 6, 10)
NEAR, FAR = 24, 10
CHUNKS = ((0, 6), (6, 6), (12, 6), (18, 6), (24, 5), (29, 5))
SHARES = ((24, 10), (0, 12), (12, 12))


def tile_list(h, y):
    z = [lax.rem(h + step, SIDE) for step in range(SIDE)]
    same, near, back = y, lax.rem(y + 1, SIDE), lax.rem(y + 3, SIDE)

    def make(z1, y1, z2, y2, tile):
        first = z1 * SIDE + y1 <= z2 * SIDE + y2
        one, two = y1 * SIDE + z1, y2 * SIDE + z2
        return (jnp.where(first, one, two), jnp.where(first, two, one), tile)

    def own(a, b):
        step = (b - a) % SIDE
        return make(z[a], same, z[b], same, 24 + 4 * step + (lax.rem(z[a], 2) if step == 2 else z[a]))

    def side(a, b):
        step = (b - a) % SIDE
        return make(z[a], same, z[b], near, z[a] + (0, 4, 12, 16)[step])

    def across(a):
        return make(z[a], back, z[(a + 1) % SIDE], near, 8 + z[a])

    def level(a):
        return make(a, back, a, near, 20 + a - half)

    def cross(a):
        low = lax.rem(z[a], 2)
        return make(low, back, low + 2, near, 22 + low)

    half = jnp.where(back >= 2, 2, 0)
    early = jnp.where(z[2] == half, half + 1, half)
    late = 2 * half + 1 - early
    return [
        side(0, 0),
        side(0, 3), side(3, 0), side(3, 3), across(3),
        side(1, 1), side(1, 0), side(0, 1), side(1, 3), side(3, 1), across(0), cross(1), level(early),
        side(2, 2), side(2, 3), side(1, 2), across(1), across(2),
        side(2, 0), side(0, 2), side(2, 1), side(3, 2), cross(0), level(late),
        own(0, 0), own(3, 3), own(3, 0), own(1, 1), own(0, 1), own(1, 3),
        own(2, 2), own(1, 2), own(2, 3), own(0, 2),
    ]


def tile_index(a, b):
    za, ya, zb, yb = a >> 2, a & 3, b >> 2, b & 3
    dy, dz, back = (yb - ya) & 3, (zb - za) & 3, (za - zb) & 3
    own = 24 + jnp.where(dz == 2, 8 + (za & 1), jnp.where(dz == 3, 4 + zb, za + 4 * dz))
    right = za + 4 * dz + jnp.where(dz >= 2, 4, 0)
    left = zb + 4 * back + jnp.where(back >= 2, 4, 0)
    far_y = jnp.where((dz == 3) | ((dz == 0) & (za >= 2)), yb, ya)
    far = jnp.where(dz == 1, 8 + za, jnp.where(dz == 3, 8 + zb, jnp.where(dz == 0, 20 + (za & 1), 22 + za)))
    which_y = jnp.where(dy == 2, (far_y + 1) & 3, jnp.where(dy == 3, yb, ya))
    which = jnp.where(dy == 0, own, jnp.where(dy == 1, right, jnp.where(dy == 3, left, far)))
    return jnp.where(a >= 0, which_y * TILES + which, SIDE * TILES)


def kernel(
    x_ref, table_ref, out_ref, blocks, relay, part, pair, xfirst, xlast, total, zpart, zfar, zsum, xfar,
    indices, wanted, pieces, chosen, through, landed,
    local_sem, zs, zr, ys, yr, ps, pr, xs, xr, ws, wr, fs, fr, ts, tr, gs, gr, os, onr,
):
    tm, space = lax.axis_index("tm"), lax.axis_index("space")
    h, y = tm // SIDE, lax.rem(tm, SIDE)
    x, low, core = space // SIDE, lax.rem(space // 2, 2), lax.rem(space, 2)

    def device(h_=h, y_=y, x_=x, low_=low, core_=core):
        return (h_ * SIDE + y_, x_ * SIDE + low_ * 2 + core_)

    def up(value, step, size=SIDE):
        return lax.rem(value + step, size)

    hp, hm, h2 = up(h, 1), up(h, 3), up(h, 2)
    yp, ym = up(y, 1), up(y, 3)
    xp, xm, x2 = up(x, 1), up(x, 3), up(x, 2)
    other = 1 - core
    place = h * 2 + low
    zp, zm = up(place, 1, 8), up(place, 7, 8)
    dev_hp, dev_hm = device(h_=hp), device(h_=hm)
    dev_yp, dev_ym = device(y_=yp), device(y_=ym)
    dev_xp, dev_xm = device(x_=xp), device(x_=xm)
    dev_zp = device(h_=zp // 2, low_=lax.rem(zp, 2))
    dev_zm = device(h_=zm // 2, low_=lax.rem(zm, 2))
    dev_pair = device(core_=other)

    barrier = pltpu.get_barrier_semaphore()
    peers = (dev_hp, dev_hm, dev_yp, dev_ym, dev_xp, dev_xm, dev_zp, dev_zm, dev_pair)
    for peer in peers:
        pl.semaphore_signal(barrier, inc=1, device_id=peer, device_id_type=MESH)
    pl.semaphore_wait(barrier, len(peers))

    started = []

    def send(src, dst, send_sem, recv_sem, peer):
        copy = pltpu.make_async_remote_copy(
            src_ref=src, dst_ref=dst, send_sem=send_sem, recv_sem=recv_sem, device_id=peer, device_id_type=MESH
        )
        copy.start()
        started.append(copy)
        return copy

    def cells(which):
        return pl.ds(pl.multiple_of(which * BLOCK, BLOCK), BLOCK)

    every = slice(None)
    first_rows, last_rows = pl.ds(0, BLOCK // 2), pl.ds(BLOCK // 2, BLOCK // 2)

    local = pltpu.make_async_copy(x_ref.at[:, :, cells(h)], blocks.at[y, h], local_sem)
    local.start()
    comps = range(3)
    to_hp, to_hm, via_hp, via_hm, on_hp, on_hm, moved = {}, {}, {}, {}, {}, {}, {}

    def near(k):
        to_hp[k] = send(x_ref.at[k, :, cells(hp)], blocks.at[y, h, k], zs.at[0, k], zr.at[0, k], dev_hp)
        to_hm[k] = send(x_ref.at[k, :, cells(hm)], blocks.at[y, h, k], zs.at[1, k], zr.at[1, k], dev_hm)

    def away(k):
        via_hp[k] = send(x_ref.at[k, first_rows, cells(h2)], relay.at[0, k], zs.at[2, k], zr.at[2, k], dev_hp)
        via_hm[k] = send(x_ref.at[k, last_rows, cells(h2)], relay.at[1, k], zs.at[3, k], zr.at[3, k], dev_hm)

    def spread(key, z, k, src=None):
        src = blocks.at[y, z, k] if src is None else src
        for way, peer in enumerate((dev_yp, dev_ym)):
            moved[key, k, way] = send(src, blocks.at[y, z, k], ys.at[key, k, way], yr.at[key, k, way], peer)

    def gathered(key):
        for k in comps:
            for way in range(2):
                moved[key, k, way].wait_recv()

    near(0)
    near(1)
    for k in comps:
        spread(0, h, k, x_ref.at[k, :, cells(h)])
    indices[h] = jnp.zeros((8, 128), jnp.int32)
    indices[h, 0:1, 0:SLOTS] = tile_index(table_ref[0, 0:1, :], table_ref[0, 1:2, :])
    told = [
        send(indices.at[h], indices.at[h], ts.at[number], tr.at[number], peer)
        for number, peer in enumerate((dev_hp, dev_hm))
    ]

    def onward(k):
        via_hp[k].wait_recv()
        on_hp[k] = send(relay.at[0, k], blocks.at[y, hm, k, first_rows], zs.at[4, k], zr.at[4, k], dev_hp)
        via_hm[k].wait_recv()
        on_hm[k] = send(relay.at[1, k], blocks.at[y, hp, k, last_rows], zs.at[5, k], zr.at[5, k], dev_hm)

    def spread_far(k):
        on_hp[k].wait_recv()
        on_hm[k].wait_recv()
        spread(3, h2, k)

    tiles = tile_list(h, y)
    starts = [sum(BATCHES[:number]) for number in range(len(BATCHES))]

    def compute(begin, size):
        for slot, (left, right, tile) in enumerate(tiles[begin:begin + size], begin):
            ly, lz, ry, rz = left // SIDE, lax.rem(left, SIDE), right // SIDE, lax.rem(right, SIDE)
            product = None
            for comp in range(3):
                term = lax.dot_general(
                    blocks[ly, lz, comp], blocks[ry, rz, comp], (((1,), (1,)), ((), ())),
                    preferred_element_type=jnp.float32,
                )
                product = term if product is None else product + term
            slot = tile if slot >= NEAR else slot
            for row in range(BLOCK // 8):
                for lane in range(2):
                    place_x, place_low, place_core, place_row = row // 8, row // 4 % 2, row // 2 % 2, row % 2
                    part[slot, place_core, place_x, place_low * 4 + place_row * 2 + lane] = product[
                        row * 8:row * 8 + 8, lane * 128:lane * 128 + 128
                    ]

    def swap(number):
        span = pl.ds(starts[number], BATCHES[number])
        return send(part.at[span, other], pair.at[span], ps.at[number], pr.at[number], dev_pair)

    def begin_batch(number):
        compute(starts[number], BATCHES[number])
        return swap(number)

    def add_pair(number, copy):
        begin, size = starts[number], BATCHES[number]
        copy.wait_recv()

        @pl.loop(begin, begin + size)
        def _(slot):
            part[slot, core] = part[slot, core] + pair[slot]

        if begin == NEAR:
            return None
        span = pl.ds(begin, size)
        return (
            send(part.at[span, core, x2, pl.ds(0, 4)], xfirst.at[0, span], xs.at[number, 0], xr.at[number, 0], dev_xp),
            send(part.at[span, core, x2, pl.ds(4, 4)], xfirst.at[1, span], xs.at[number, 1], xr.at[number, 1], dev_xm),
        )

    def add_first(number, copies):
        begin, size = starts[number], BATCHES[number]
        for copy in copies:
            copy.wait_recv()

        @pl.loop(begin, begin + size)
        def _(slot):
            part[slot, core, xp, 0:4] = part[slot, core, xp, 0:4] + xfirst[0, slot]
            part[slot, core, xm, 4:8] = part[slot, core, xm, 4:8] + xfirst[1, slot]

        span = pl.ds(begin, size)
        return (
            send(part.at[span, core, xp], xlast.at[0, span], xs.at[number, 2], xr.at[number, 2], dev_xp),
            send(part.at[span, core, xm], xlast.at[1, span], xs.at[number, 3], xr.at[number, 3], dev_xm),
        )

    def add_last(number, copies):
        begin, size = starts[number], BATCHES[number]
        for copy in copies:
            copy.wait_recv()
        for slot in range(begin, begin + size):
            total[tiles[slot][2]] = part[slot, core, x] + xlast[0, slot] + xlast[1, slot]

    def piece(step):
        target = up(place, step, 8)
        return lax.rem(target, 2) * 4 + target // 2

    flying = {}

    def pass_on(chunk, way, number):
        begin, size = CHUNKS[chunk]
        hops = 4 if chunk % 2 == way else 3
        if number >= hops:
            return
        distance = hops - number
        which = piece(distance if way == 0 else 8 - distance)
        span, here = pl.ds(begin, size), pl.ds(begin - NEAR, size)
        if number > 0:
            flying[chunk, way].wait_recv()
            part[span, core, :, which] = part[span, core, :, which] + zfar[way, number - 1, here]
        flying[chunk, way] = send(
            part.at[span, core, :, which], zfar.at[way, number, here],
            ws.at[chunk, way, number], wr.at[chunk, way, number], dev_zp if way == 0 else dev_zm,
        )

    def pass_some(chunks, first, number):
        for chunk in chunks:
            pass_on(chunk, (chunk + first) % 2, number)

    def pass_all(chunks, number):
        for first in range(2):
            pass_some(chunks, first, number)

    def arrived(chunk):
        for way in range(2):
            flying[chunk, way].wait_recv()
        return (3, 2) if chunk % 2 == 0 else (2, 3)

    def far_sums():
        for chunk in (4, 5):
            begin, size = CHUNKS[chunk]
            above, below = arrived(chunk)
            here = begin - NEAR
            zsum[here:here + size] = (
                part[begin:begin + size, core, :, piece(0)]
                + zfar[0, above, here:here + size] + zfar[1, below, here:here + size]
            )
        first, rest = pl.ds(0, FAR // 2), pl.ds(FAR // 2, FAR // 2)
        return (
            send(zsum.at[first, x2], xfar.at[0, 0, first], fs.at[0], fr.at[0], dev_xp),
            send(zsum.at[rest, x2], xfar.at[0, 1, rest], fs.at[1], fr.at[1], dev_xm),
        )

    def far_cross(copies):
        middle = FAR // 2
        copies[0].wait_recv()
        zsum[0:middle, xp] = zsum[0:middle, xp] + xfar[0, 0, 0:middle]
        copies[1].wait_recv()
        zsum[middle:FAR, xm] = zsum[middle:FAR, xm] + xfar[0, 1, middle:FAR]
        return (
            send(zsum.at[:, xp], xfar.at[1, 0], fs.at[2], fr.at[2], dev_xp),
            send(zsum.at[:, xm], xfar.at[1, 1], fs.at[3], fr.at[3], dev_xm),
        )

    shared = {}

    def share(number, value):
        begin, size = SHARES[number]
        span = pl.ds(y * TILES + begin, size)
        pieces[span] = value
        shared[number] = (
            send(pieces.at[span], pieces.at[span], gs.at[number, 0], gr.at[number, 0], dev_yp),
            send(pieces.at[span], pieces.at[span], gs.at[number, 1], gr.at[number, 1], dev_ym),
        )

    next_by, next_two = (dev_zp, dev_zm), (dev_hp, dev_hm)

    def step_on(chunk, way, kind, distance, peer):
        span = pl.ds(*CHUNKS[chunk])
        which = piece(distance if way == 0 else 8 - distance)
        flying[chunk, way, kind] = send(
            total.at[span, which], zpart.at[way, kind, span], ws.at[chunk, way, kind], wr.at[chunk, way, kind], peer
        )

    def launch(chunks):
        for chunk in chunks:
            way = chunk % 2
            step_on(chunk, way, 0, 4, next_two[way])
        for chunk in chunks:
            for way in range(2):
                step_on(chunk, way, 1, 3, next_by[way])
        for chunk in chunks:
            for way in range(2):
                step_on(chunk, way, 2, 1, next_by[way])

    def meet(chunks):
        for chunk in chunks:
            begin, end = CHUNKS[chunk][0], sum(CHUNKS[chunk])
            for way in (1 - chunk % 2, chunk % 2):
                which = piece(2 if way == 0 else 6)
                flying[chunk, way, 1].wait_recv()
                added = total[begin:end, which] + zpart[way, 1, begin:end]
                if chunk % 2 == way:
                    flying[chunk, way, 0].wait_recv()
                    added = added + zpart[way, 0, begin:end]
                total[begin:end, which] = added
                step_on(chunk, way, 3, 2, next_two[way])

    def share_near(number, chunks):
        parts = []
        for chunk in chunks:
            begin, end = CHUNKS[chunk][0], sum(CHUNKS[chunk])
            value = total[begin:end, piece(0)]
            for kind in (2, 3):
                for way in range(2):
                    flying[chunk, way, kind].wait_recv()
                    value = value + zpart[way, kind, begin:end]
            parts.append(value)
        share(number, jnp.concatenate(parts))

    to_hp[0].wait_recv()
    spread(1, hm, 0)
    to_hm[0].wait_recv()
    near(2)
    local.wait()
    gathered(0)
    pair0 = begin_batch(0)
    to_hp[1].wait_recv()
    spread(1, hm, 1)
    to_hm[1].wait_recv()
    away(0)
    spread(2, hp, 0)
    first0 = add_pair(0, pair0)
    last0 = add_first(0, first0)
    to_hp[2].wait_recv()
    spread(1, hm, 2)
    to_hm[2].wait_recv()
    away(1)
    away(2)
    spread(2, hp, 1)
    spread(2, hp, 2)
    onward(0)
    add_last(0, last0)
    told[0].wait_recv()
    told.append(send(indices.at[hm], indices.at[hm], ts.at[2], tr.at[2], dev_hp))
    gathered(1)
    pair1 = begin_batch(1)
    onward(1)
    first1 = add_pair(1, pair1)
    onward(2)
    gathered(2)
    pair2 = begin_batch(2)
    last1 = add_first(1, first1)
    spread_far(0)
    first2 = add_pair(2, pair2)
    spread_far(1)
    compute(NEAR, 6)
    spread_far(2)
    compute(NEAR + 6, 4)
    pair5 = swap(5)
    last2 = add_first(2, first2)
    add_pair(5, pair5)
    pass_all((4, 5), 0)
    add_last(1, last1)
    gathered(3)
    pair3 = begin_batch(3)
    pair4 = begin_batch(4)
    pass_some((4, 5), 0, 1)
    first3 = add_pair(3, pair3)
    pass_some((4, 5), 1, 1)
    first4 = add_pair(4, pair4)
    pass_some((4, 5), 0, 2)
    last3 = add_first(3, first3)
    pass_some((4, 5), 1, 2)
    last4 = add_first(4, first4)
    add_last(2, last2)
    pass_some((4, 5), 0, 3)
    add_last(3, last3)
    launch((0, 1))
    far = far_sums()
    meet((0, 1))
    add_last(4, last4)
    launch((2, 3))
    far = far_cross(far)
    meet((2, 3))
    for copy in far:
        copy.wait_recv()
    share(0, zsum[:, x] + xfar[1, 0] + xfar[1, 1])
    share_near(1, (0, 1))
    share_near(2, (2, 3))

    pieces[SIDE * TILES] = jnp.zeros((8, 128), jnp.float32)
    onto = {}
    told[1].wait_recv()
    told[2].wait_recv()
    listed = pltpu.make_async_copy(indices, wanted, local_sem)
    listed.start()
    listed.wait()
    for chunk, (begin, size) in enumerate(SHARES):
        half = size // 2
        to_yp, to_ym = shared[chunk]
        to_yp.wait_recv()
        early = pl.ds(ym * TILES + begin, half)
        on_yp = send(pieces.at[early], pieces.at[early], gs.at[chunk, 2], gr.at[chunk, 2], dev_yp)
        to_ym.wait_recv()
        late = pl.ds(yp * TILES + begin + half, half)
        on_ym = send(pieces.at[late], pieces.at[late], gs.at[chunk, 3], gr.at[chunk, 3], dev_ym)
        onto[chunk] = (on_yp, on_ym)
    for chunk in range(len(SHARES)):
        for copy in onto[chunk]:
            copy.wait_recv()

    def choose(number, z):
        @pl.loop(0, SLOTS)
        def _(slot):
            chosen[number, slot] = pieces[wanted[z, 0, slot]]

    half = SLOTS // 2
    choose(2, h2)
    far_hp = send(chosen.at[2, pl.ds(0, half)], through.at[0], os.at[2], onr.at[2], dev_hp)
    far_hm = send(chosen.at[2, pl.ds(half, half)], through.at[1], os.at[3], onr.at[3], dev_hm)
    choose(0, hp)
    out_hp = send(chosen.at[0], landed.at[0], os.at[0], onr.at[0], dev_hp)
    choose(1, hm)
    out_hm = send(chosen.at[1], landed.at[1], os.at[1], onr.at[1], dev_hm)
    far_hp.wait_recv()
    last_hp = send(through.at[0], landed.at[2, pl.ds(0, half)], os.at[4], onr.at[4], dev_hp)
    far_hm.wait_recv()
    last_hm = send(through.at[1], landed.at[2, pl.ds(half, half)], os.at[5], onr.at[5], dev_hm)

    def put(z, slot, value):
        rows, lanes = pl.multiple_of(z // 2 * 8, 8), pl.multiple_of(lax.rem(z, 2) * 128, 128)
        out_ref[0, slot, pl.ds(rows, 8), pl.ds(lanes, 128)] = value

    for slot in range(SLOTS):
        put(h, slot, pieces[wanted[h, 0, slot]])
    out_hp.wait_recv()
    for slot in range(SLOTS):
        put(hm, slot, landed[0, slot])
    out_hm.wait_recv()
    for slot in range(SLOTS):
        put(hp, slot, landed[1, slot])
    last_hp.wait_recv()
    last_hm.wait_recv()
    for slot in range(SLOTS):
        put(h2, slot, landed[2, slot])
    for copy in started:
        copy.wait_send()


def gram(snapshots, table):
    count = len(BATCHES)
    dma = pltpu.SemaphoreType.DMA
    f32, b16 = jnp.float32, jnp.bfloat16
    return pl.pallas_call(
        kernel,
        out_shape=jax.ShapeDtypeStruct((1, SLOTS, 16, BLOCK), f32),
        in_specs=[pl.BlockSpec(memory_space=pl.ANY), pl.BlockSpec(memory_space=pltpu.VMEM)],
        out_specs=pl.BlockSpec(memory_space=pltpu.VMEM),
        scratch_shapes=[
            pltpu.VMEM((4, 4, 3, BLOCK, BLOCK), b16),
            pltpu.VMEM((2, 3, BLOCK // 2, BLOCK), b16),
            pltpu.VMEM((TILES, 2, 4, 8, 8, 128), f32),
            pltpu.VMEM((TILES, 4, 8, 8, 128), f32),
            pltpu.VMEM((2, NEAR, 4, 8, 128), f32),
            pltpu.VMEM((2, NEAR, 8, 8, 128), f32),
            pltpu.VMEM((NEAR, 8, 8, 128), f32),
            pltpu.VMEM((2, 4, NEAR, 8, 128), f32),
            pltpu.VMEM((2, 4, FAR, 4, 8, 128), f32),
            pltpu.VMEM((FAR, 4, 8, 128), f32),
            pltpu.VMEM((2, 2, FAR, 8, 128), f32),
            pltpu.VMEM((SIDE, 8, 128), jnp.int32),
            pltpu.SMEM((SIDE, 8, 128), jnp.int32),
            pltpu.VMEM((SIDE * TILES + 1, 8, 128), f32),
            pltpu.VMEM((3, SLOTS, 8, 128), f32),
            pltpu.VMEM((2, SLOTS // 2, 8, 128), f32),
            pltpu.VMEM((3, SLOTS, 8, 128), f32),
            dma(()), dma((6, 3)), dma((6, 3)), dma((4, 3, 2)), dma((4, 3, 2)), dma((count,)), dma((count,)),
            dma((count, 4)), dma((count, 4)), dma((6, 2, 4)), dma((6, 2, 4)), dma((4,)), dma((4,)),
            dma((3,)), dma((3,)), dma((3, 4)), dma((3, 4)), dma((6,)), dma((6,)),
        ],
        compiler_params=pltpu.CompilerParams(collective_id=0, has_side_effects=True, vmem_limit_bytes=60 * 2**20),
        name="gram_tiles",
    )(snapshots, table)


def per_device(snapshots, tile_table):
    scale = 1.0 / math.sqrt(3 * snapshots.shape[2] * lax.axis_size("space"))
    return gram(snapshots, jnp.transpose(tile_table, (0, 2, 1))) * scale


def solution(mesh):
    in_specs = (P(None, "tm", "space"), P("tm", None, None))
    out_specs = P("tm", None, "space", None)
    return jax.shard_map(
        per_device, mesh=mesh, in_specs=in_specs, out_specs=out_specs, check_vma=False
    )
```

```python
import math

import jax
import jax.numpy as jnp
from jax import lax
from jax.experimental import pallas as pl
from jax.experimental.pallas import tpu as pltpu
from jax.sharding import PartitionSpec as P

MESH = pl.DeviceIdType.MESH
BLOCK = 256
SIDE = 4
SLOTS = 20
TILES = 34
BATCHES = (1, 4, 8, 5, 6, 10)
NEAR, FAR = 24, 10
CHUNKS = ((0, 6), (6, 6), (12, 6), (18, 6), (24, 5), (29, 5))
SHARES = ((24, 10), (0, 12), (12, 12))


def tile_list(h, y):
    z = [lax.rem(h + step, SIDE) for step in range(SIDE)]
    same, near, back = y, lax.rem(y + 1, SIDE), lax.rem(y + 3, SIDE)

    def make(z1, y1, z2, y2, tile):
        first = z1 * SIDE + y1 <= z2 * SIDE + y2
        one, two = y1 * SIDE + z1, y2 * SIDE + z2
        return (jnp.where(first, one, two), jnp.where(first, two, one), tile)

    def own(a, b):
        step = (b - a) % SIDE
        return make(z[a], same, z[b], same, 24 + 4 * step + (lax.rem(z[a], 2) if step == 2 else z[a]))

    def side(a, b):
        step = (b - a) % SIDE
        return make(z[a], same, z[b], near, z[a] + (0, 4, 12, 16)[step])

    def across(a):
        return make(z[a], back, z[(a + 1) % SIDE], near, 8 + z[a])

    def level(a):
        return make(a, back, a, near, 20 + a - half)

    def cross(a):
        low = lax.rem(z[a], 2)
        return make(low, back, low + 2, near, 22 + low)

    half = jnp.where(back >= 2, 2, 0)
    early = jnp.where(z[2] == half, half + 1, half)
    late = 2 * half + 1 - early
    return [
        side(0, 0),
        side(0, 3), side(3, 0), side(3, 3), across(3),
        side(1, 1), side(1, 0), side(0, 1), side(1, 3), side(3, 1), across(0), cross(1), level(early),
        side(2, 2), side(2, 3), side(1, 2), across(1), across(2),
        side(2, 0), side(0, 2), side(2, 1), side(3, 2), cross(0), level(late),
        own(0, 0), own(3, 3), own(3, 0), own(1, 1), own(0, 1), own(1, 3),
        own(2, 2), own(1, 2), own(2, 3), own(0, 2),
    ]


def tile_index(a, b):
    za, ya, zb, yb = a >> 2, a & 3, b >> 2, b & 3
    dy, dz, back = (yb - ya) & 3, (zb - za) & 3, (za - zb) & 3
    own = 24 + jnp.where(dz == 2, 8 + (za & 1), jnp.where(dz == 3, 4 + zb, za + 4 * dz))
    right = za + 4 * dz + jnp.where(dz >= 2, 4, 0)
    left = zb + 4 * back + jnp.where(back >= 2, 4, 0)
    far_y = jnp.where((dz == 3) | ((dz == 0) & (za >= 2)), yb, ya)
    far = jnp.where(dz == 1, 8 + za, jnp.where(dz == 3, 8 + zb, jnp.where(dz == 0, 20 + (za & 1), 22 + za)))
    which_y = jnp.where(dy == 2, (far_y + 1) & 3, jnp.where(dy == 3, yb, ya))
    which = jnp.where(dy == 0, own, jnp.where(dy == 1, right, jnp.where(dy == 3, left, far)))
    return jnp.where(a >= 0, which_y * TILES + which, SIDE * TILES)


def kernel(
    x_ref, table_ref, out_ref, blocks, relay, part, pair, xfirst, xlast, total, zpart, zfar, zsum, xfar,
    indices, wanted, pieces, chosen, through, landed,
    local_sem, zs, zr, ys, yr, ps, pr, xs, xr, ws, wr, fs, fr, ts, tr, gs, gr, os, onr,
):
    tm, space = lax.axis_index("tm"), lax.axis_index("space")
    h, y = tm // SIDE, lax.rem(tm, SIDE)
    x, low, core = space // SIDE, lax.rem(space // 2, 2), lax.rem(space, 2)

    def device(h_=h, y_=y, x_=x, low_=low, core_=core):
        return (h_ * SIDE + y_, x_ * SIDE + low_ * 2 + core_)

    def up(value, step, size=SIDE):
        return lax.rem(value + step, size)

    hp, hm, h2 = up(h, 1), up(h, 3), up(h, 2)
    yp, ym = up(y, 1), up(y, 3)
    xp, xm, x2 = up(x, 1), up(x, 3), up(x, 2)
    other = 1 - core
    place = h * 2 + low
    zp, zm = up(place, 1, 8), up(place, 7, 8)
    dev_hp, dev_hm = device(h_=hp), device(h_=hm)
    dev_yp, dev_ym = device(y_=yp), device(y_=ym)
    dev_xp, dev_xm = device(x_=xp), device(x_=xm)
    dev_zp = device(h_=zp // 2, low_=lax.rem(zp, 2))
    dev_zm = device(h_=zm // 2, low_=lax.rem(zm, 2))
    dev_pair = device(core_=other)

    barrier = pltpu.get_barrier_semaphore()
    peers = (dev_hp, dev_hm, device(y_=up(y, 2)), dev_yp, dev_ym, dev_xp, dev_xm, dev_zp, dev_zm, dev_pair)
    for peer in peers:
        pl.semaphore_signal(barrier, inc=1, device_id=peer, device_id_type=MESH)
    pl.semaphore_wait(barrier, len(peers))

    started = []

    def send(src, dst, send_sem, recv_sem, peer):
        copy = pltpu.make_async_remote_copy(
            src_ref=src, dst_ref=dst, send_sem=send_sem, recv_sem=recv_sem, device_id=peer, device_id_type=MESH
        )
        copy.start()
        started.append(copy)
        return copy

    def cells(which):
        return pl.ds(pl.multiple_of(which * BLOCK, BLOCK), BLOCK)

    every = slice(None)
    first_rows, last_rows = pl.ds(0, BLOCK // 2), pl.ds(BLOCK // 2, BLOCK // 2)

    local = pltpu.make_async_copy(x_ref.at[:, :, cells(h)], blocks.at[y, h], local_sem)
    local.start()
    comps = range(3)
    to_hp, to_hm, via_hp, via_hm, on_hp, on_hm, moved = {}, {}, {}, {}, {}, {}, {}

    def near(k):
        to_hp[k] = send(x_ref.at[k, :, cells(hp)], blocks.at[y, h, k], zs.at[0, k], zr.at[0, k], dev_hp)
        to_hm[k] = send(x_ref.at[k, :, cells(hm)], blocks.at[y, h, k], zs.at[1, k], zr.at[1, k], dev_hm)

    def away(k):
        via_hp[k] = send(x_ref.at[k, first_rows, cells(h2)], relay.at[0, k], zs.at[2, k], zr.at[2, k], dev_hp)
        via_hm[k] = send(x_ref.at[k, last_rows, cells(h2)], relay.at[1, k], zs.at[3, k], zr.at[3, k], dev_hm)

    def spread(key, z, k, src=None):
        src = blocks.at[y, z, k] if src is None else src
        for way, peer in enumerate((dev_yp, dev_ym)):
            moved[key, k, way] = send(src, blocks.at[y, z, k], ys.at[key, k, way], yr.at[key, k, way], peer)

    def gathered(key):
        for k in comps:
            for way in range(2):
                moved[key, k, way].wait_recv()

    near(0)
    near(1)
    for k in comps:
        spread(0, h, k, x_ref.at[k, :, cells(h)])
    indices[h] = jnp.zeros((8, 128), jnp.int32)
    indices[h, 0:1, 0:SLOTS] = tile_index(table_ref[0, 0:1, :], table_ref[0, 1:2, :])
    told = [
        send(indices.at[h], indices.at[h], ts.at[number], tr.at[number], peer)
        for number, peer in enumerate((dev_hp, dev_hm))
    ]

    def onward(k):
        via_hp[k].wait_recv()
        on_hp[k] = send(relay.at[0, k], blocks.at[y, hm, k, first_rows], zs.at[4, k], zr.at[4, k], dev_hp)
        via_hm[k].wait_recv()
        on_hm[k] = send(relay.at[1, k], blocks.at[y, hp, k, last_rows], zs.at[5, k], zr.at[5, k], dev_hm)

    def spread_far(k):
        on_hp[k].wait_recv()
        on_hm[k].wait_recv()
        spread(3, h2, k)

    tiles = tile_list(h, y)
    starts = [sum(BATCHES[:number]) for number in range(len(BATCHES))]

    def compute(begin, size):
        for slot, (left, right, tile) in enumerate(tiles[begin:begin + size], begin):
            ly, lz, ry, rz = left // SIDE, lax.rem(left, SIDE), right // SIDE, lax.rem(right, SIDE)
            product = None
            for comp in range(3):
                term = lax.dot_general(
                    blocks[ly, lz, comp], blocks[ry, rz, comp], (((1,), (1,)), ((), ())),
                    preferred_element_type=jnp.float32,
                )
                product = term if product is None else product + term
            slot = tile if slot >= NEAR else slot
            for row in range(BLOCK // 8):
                for lane in range(2):
                    place_x, place_low, place_core, place_row = row // 8, row // 4 % 2, row // 2 % 2, row % 2
                    part[slot, place_core, place_x, place_low * 4 + place_row * 2 + lane] = product[
                        row * 8:row * 8 + 8, lane * 128:lane * 128 + 128
                    ]

    def swap(number):
        span = pl.ds(starts[number], BATCHES[number])
        return send(part.at[span, other], pair.at[span], ps.at[number], pr.at[number], dev_pair)

    def begin_batch(number):
        compute(starts[number], BATCHES[number])
        return swap(number)

    def add_pair(number, copy):
        begin, size = starts[number], BATCHES[number]
        copy.wait_recv()

        @pl.loop(begin, begin + size)
        def _(slot):
            part[slot, core] = part[slot, core] + pair[slot]

        if begin == NEAR:
            return None
        span = pl.ds(begin, size)
        return (
            send(part.at[span, core, x2, pl.ds(0, 4)], xfirst.at[0, span], xs.at[number, 0], xr.at[number, 0], dev_xp),
            send(part.at[span, core, x2, pl.ds(4, 4)], xfirst.at[1, span], xs.at[number, 1], xr.at[number, 1], dev_xm),
        )

    def add_first(number, copies):
        begin, size = starts[number], BATCHES[number]
        for copy in copies:
            copy.wait_recv()

        @pl.loop(begin, begin + size)
        def _(slot):
            part[slot, core, xp, 0:4] = part[slot, core, xp, 0:4] + xfirst[0, slot]
            part[slot, core, xm, 4:8] = part[slot, core, xm, 4:8] + xfirst[1, slot]

        span = pl.ds(begin, size)
        return (
            send(part.at[span, core, xp], xlast.at[0, span], xs.at[number, 2], xr.at[number, 2], dev_xp),
            send(part.at[span, core, xm], xlast.at[1, span], xs.at[number, 3], xr.at[number, 3], dev_xm),
        )

    def add_last(number, copies):
        begin, size = starts[number], BATCHES[number]
        for copy in copies:
            copy.wait_recv()
        for slot in range(begin, begin + size):
            total[tiles[slot][2]] = part[slot, core, x] + xlast[0, slot] + xlast[1, slot]

    def piece(step):
        target = up(place, step, 8)
        return lax.rem(target, 2) * 4 + target // 2

    flying = {}

    def pass_on(chunk, way, number):
        begin, size = CHUNKS[chunk]
        hops = 4 if chunk % 2 == way else 3
        if number >= hops:
            return
        distance = hops - number
        which = piece(distance if way == 0 else 8 - distance)
        span, here = pl.ds(begin, size), pl.ds(begin - NEAR, size)
        if number > 0:
            flying[chunk, way].wait_recv()
            part[span, core, :, which] = part[span, core, :, which] + zfar[way, number - 1, here]
        flying[chunk, way] = send(
            part.at[span, core, :, which], zfar.at[way, number, here],
            ws.at[chunk, way, number], wr.at[chunk, way, number], dev_zp if way == 0 else dev_zm,
        )

    def pass_some(chunks, first, number):
        for chunk in chunks:
            pass_on(chunk, (chunk + first) % 2, number)

    def pass_all(chunks, number):
        for first in range(2):
            pass_some(chunks, first, number)

    def arrived(chunk):
        for way in range(2):
            flying[chunk, way].wait_recv()
        return (3, 2) if chunk % 2 == 0 else (2, 3)

    def far_sums():
        for chunk in (4, 5):
            begin, size = CHUNKS[chunk]
            above, below = arrived(chunk)
            here = begin - NEAR
            zsum[here:here + size] = (
                part[begin:begin + size, core, :, piece(0)]
                + zfar[0, above, here:here + size] + zfar[1, below, here:here + size]
            )
        first, rest = pl.ds(0, FAR // 2), pl.ds(FAR // 2, FAR // 2)
        return (
            send(zsum.at[first, x2], xfar.at[0, 0, first], fs.at[0], fr.at[0], dev_xp),
            send(zsum.at[rest, x2], xfar.at[0, 1, rest], fs.at[1], fr.at[1], dev_xm),
        )

    def far_cross(copies):
        middle = FAR // 2
        copies[0].wait_recv()
        zsum[0:middle, xp] = zsum[0:middle, xp] + xfar[0, 0, 0:middle]
        copies[1].wait_recv()
        zsum[middle:FAR, xm] = zsum[middle:FAR, xm] + xfar[0, 1, middle:FAR]
        return (
            send(zsum.at[:, xp], xfar.at[1, 0], fs.at[2], fr.at[2], dev_xp),
            send(zsum.at[:, xm], xfar.at[1, 1], fs.at[3], fr.at[3], dev_xm),
        )

    shared = {}

    def share(number, value):
        begin, size = SHARES[number]
        span = pl.ds(y * TILES + begin, size)
        pieces[span] = value
        shared[number] = (
            send(pieces.at[span], pieces.at[span], gs.at[number, 0], gr.at[number, 0], dev_yp),
            send(pieces.at[span], pieces.at[span], gs.at[number, 1], gr.at[number, 1], dev_ym),
        )

    next_by, next_two = (dev_zp, dev_zm), (dev_hp, dev_hm)

    def step_on(chunk, way, kind, distance, peer):
        span = pl.ds(*CHUNKS[chunk])
        which = piece(distance if way == 0 else 8 - distance)
        flying[chunk, way, kind] = send(
            total.at[span, which], zpart.at[way, kind, span], ws.at[chunk, way, kind], wr.at[chunk, way, kind], peer
        )

    def launch(chunks):
        for chunk in chunks:
            way = chunk % 2
            step_on(chunk, way, 0, 4, next_two[way])
        for chunk in chunks:
            for way in range(2):
                step_on(chunk, way, 1, 3, next_by[way])
        for chunk in chunks:
            for way in range(2):
                step_on(chunk, way, 2, 1, next_by[way])

    def meet(chunks):
        for chunk in chunks:
            begin, end = CHUNKS[chunk][0], sum(CHUNKS[chunk])
            for way in (1 - chunk % 2, chunk % 2):
                which = piece(2 if way == 0 else 6)
                flying[chunk, way, 1].wait_recv()
                added = total[begin:end, which] + zpart[way, 1, begin:end]
                if chunk % 2 == way:
                    flying[chunk, way, 0].wait_recv()
                    added = added + zpart[way, 0, begin:end]
                total[begin:end, which] = added
                step_on(chunk, way, 3, 2, next_two[way])

    def share_near(number, chunks):
        parts = []
        for chunk in chunks:
            begin, end = CHUNKS[chunk][0], sum(CHUNKS[chunk])
            value = total[begin:end, piece(0)]
            for kind in (2, 3):
                for way in range(2):
                    flying[chunk, way, kind].wait_recv()
                    value = value + zpart[way, kind, begin:end]
            parts.append(value)
        share(number, jnp.concatenate(parts))

    to_hp[0].wait_recv()
    spread(1, hm, 0)
    to_hm[0].wait_recv()
    near(2)
    local.wait()
    gathered(0)
    pair0 = begin_batch(0)
    to_hp[1].wait_recv()
    spread(1, hm, 1)
    to_hm[1].wait_recv()
    away(0)
    spread(2, hp, 0)
    first0 = add_pair(0, pair0)
    last0 = add_first(0, first0)
    to_hp[2].wait_recv()
    spread(1, hm, 2)
    to_hm[2].wait_recv()
    away(1)
    away(2)
    spread(2, hp, 1)
    spread(2, hp, 2)
    onward(0)
    add_last(0, last0)
    told[0].wait_recv()
    told.append(send(indices.at[hm], indices.at[hm], ts.at[2], tr.at[2], dev_hp))
    gathered(1)
    pair1 = begin_batch(1)
    onward(1)
    first1 = add_pair(1, pair1)
    onward(2)
    gathered(2)
    pair2 = begin_batch(2)
    last1 = add_first(1, first1)
    spread_far(0)
    first2 = add_pair(2, pair2)
    spread_far(1)
    compute(NEAR, 6)
    spread_far(2)
    compute(NEAR + 6, 4)
    pair5 = swap(5)
    last2 = add_first(2, first2)
    add_pair(5, pair5)
    pass_all((4, 5), 0)
    add_last(1, last1)
    told[1].wait_recv()
    told[2].wait_recv()
    listed = pltpu.make_async_copy(indices, wanted, local_sem)
    listed.start()
    gathered(3)
    pair3 = begin_batch(3)
    pair4 = begin_batch(4)
    first3 = add_pair(3, pair3)
    pass_some((4, 5), 0, 1)
    first4 = add_pair(4, pair4)
    pass_some((4, 5), 1, 1)
    last3 = add_first(3, first3)
    pass_some((4, 5), 0, 2)
    last4 = add_first(4, first4)
    pass_some((4, 5), 1, 2)
    add_last(2, last2)
    pass_some((4, 5), 0, 3)
    add_last(3, last3)
    launch((0, 1))
    far = far_sums()
    meet((0, 1))
    add_last(4, last4)
    launch((2, 3))
    far = far_cross(far)
    meet((2, 3))
    for copy in far:
        copy.wait_recv()
    share(0, zsum[:, x] + xfar[1, 0] + xfar[1, 1])
    share_near(1, (0, 1))
    share_near(2, (2, 3))
    last = pl.ds(y * TILES + SHARES[2][0], SHARES[2][1])
    across_y = send(pieces.at[last], pieces.at[last], gs.at[2, 2], gr.at[2, 2], device(y_=up(y, 2)))

    pieces[SIDE * TILES] = jnp.zeros((8, 128), jnp.float32)
    onto = {}
    for chunk, (begin, size) in enumerate(SHARES):
        half = size // 2
        to_yp, to_ym = shared[chunk]
        if chunk == 2:
            to_yp.wait_recv()
            to_ym.wait_recv()
            onto[chunk] = (across_y,)
            continue
        to_yp.wait_recv()
        early = pl.ds(ym * TILES + begin, half)
        on_yp = send(pieces.at[early], pieces.at[early], gs.at[chunk, 2], gr.at[chunk, 2], dev_yp)
        to_ym.wait_recv()
        late = pl.ds(yp * TILES + begin + half, half)
        on_ym = send(pieces.at[late], pieces.at[late], gs.at[chunk, 3], gr.at[chunk, 3], dev_ym)
        onto[chunk] = (on_yp, on_ym)
    for chunk in range(len(SHARES)):
        for copy in onto[chunk]:
            copy.wait_recv()

    listed.wait()

    def choose(number, z):
        for slot in range(SLOTS):
            chosen[number, slot] = pieces[wanted[z, 0, slot]]

    half = SLOTS // 2
    choose(2, h2)
    far_hp = send(chosen.at[2, pl.ds(0, half)], through.at[0], os.at[2], onr.at[2], dev_hp)
    far_hm = send(chosen.at[2, pl.ds(half, half)], through.at[1], os.at[3], onr.at[3], dev_hm)
    choose(0, hp)
    out_hp = send(chosen.at[0], landed.at[0], os.at[0], onr.at[0], dev_hp)
    choose(1, hm)
    out_hm = send(chosen.at[1], landed.at[1], os.at[1], onr.at[1], dev_hm)
    far_hp.wait_recv()
    last_hp = send(through.at[0], landed.at[2, pl.ds(0, half)], os.at[4], onr.at[4], dev_hp)
    far_hm.wait_recv()
    last_hm = send(through.at[1], landed.at[2, pl.ds(half, half)], os.at[5], onr.at[5], dev_hm)

    def put(z, slot, value):
        rows, lanes = pl.multiple_of(z // 2 * 8, 8), pl.multiple_of(lax.rem(z, 2) * 128, 128)
        out_ref[0, slot, pl.ds(rows, 8), pl.ds(lanes, 128)] = value

    for slot in range(SLOTS):
        put(h, slot, pieces[wanted[h, 0, slot]])
    out_hp.wait_recv()
    for slot in range(SLOTS):
        put(hm, slot, landed[0, slot])
    out_hm.wait_recv()
    for slot in range(SLOTS):
        put(hp, slot, landed[1, slot])
    last_hp.wait_recv()
    last_hm.wait_recv()
    for slot in range(SLOTS):
        put(h2, slot, landed[2, slot])
    for copy in started:
        copy.wait_send()


def gram(snapshots, table):
    count = len(BATCHES)
    dma = pltpu.SemaphoreType.DMA
    f32, b16 = jnp.float32, jnp.bfloat16
    return pl.pallas_call(
        kernel,
        out_shape=jax.ShapeDtypeStruct((1, SLOTS, 16, BLOCK), f32),
        in_specs=[pl.BlockSpec(memory_space=pltpu.HBM), pl.BlockSpec(memory_space=pltpu.VMEM)],
        out_specs=pl.BlockSpec(memory_space=pltpu.VMEM),
        scratch_shapes=[
            pltpu.VMEM((4, 4, 3, BLOCK, BLOCK), b16),
            pltpu.VMEM((2, 3, BLOCK // 2, BLOCK), b16),
            pltpu.VMEM((TILES, 2, 4, 8, 8, 128), f32),
            pltpu.VMEM((TILES, 4, 8, 8, 128), f32),
            pltpu.VMEM((2, NEAR, 4, 8, 128), f32),
            pltpu.VMEM((2, NEAR, 8, 8, 128), f32),
            pltpu.VMEM((NEAR, 8, 8, 128), f32),
            pltpu.VMEM((2, 4, NEAR, 8, 128), f32),
            pltpu.VMEM((2, 4, FAR, 4, 8, 128), f32),
            pltpu.VMEM((FAR, 4, 8, 128), f32),
            pltpu.VMEM((2, 2, FAR, 8, 128), f32),
            pltpu.VMEM((SIDE, 8, 128), jnp.int32),
            pltpu.SMEM((SIDE, 8, 128), jnp.int32),
            pltpu.VMEM((SIDE * TILES + 1, 8, 128), f32),
            pltpu.VMEM((3, SLOTS, 8, 128), f32),
            pltpu.VMEM((2, SLOTS // 2, 8, 128), f32),
            pltpu.VMEM((3, SLOTS, 8, 128), f32),
            dma(()), dma((6, 3)), dma((6, 3)), dma((4, 3, 2)), dma((4, 3, 2)), dma((count,)), dma((count,)),
            dma((count, 4)), dma((count, 4)), dma((6, 2, 4)), dma((6, 2, 4)), dma((4,)), dma((4,)),
            dma((3,)), dma((3,)), dma((3, 4)), dma((3, 4)), dma((6,)), dma((6,)),
        ],
        compiler_params=pltpu.CompilerParams(collective_id=0, has_side_effects=True, vmem_limit_bytes=30 * 2**20),
        name="gram_tiles",
    )(snapshots, table)


def per_device(snapshots, tile_table):
    scale = 1.0 / math.sqrt(3 * snapshots.shape[2] * lax.axis_size("space"))
    return gram(snapshots, jnp.transpose(tile_table, (0, 2, 1))) * scale


def solution(mesh):
    in_specs = (P(None, "tm", "space"), P("tm", None, None))
    out_specs = P("tm", None, "space", None)
    return jax.shard_map(
        per_device, mesh=mesh, in_specs=in_specs, out_specs=out_specs, check_vma=False
    )
```

```python
import math

import jax
import jax.numpy as jnp
from jax import lax
from jax.experimental import pallas as pl
from jax.experimental.pallas import tpu as pltpu
from jax.sharding import PartitionSpec as P

MESH = pl.DeviceIdType.MESH
BLOCK = 256
SIDE = 4
SLOTS = 20
TILES = 34
BATCHES = (1, 4, 8, 5, 6, 10)
NEAR, FAR = 24, 10
CHUNKS = ((0, 6), (6, 6), (12, 6), (18, 6), (24, 5), (29, 5))
SHARES = ((24, 10), (0, 12), (12, 12))


def tile_list(h, y):
    z = [lax.rem(h + step, SIDE) for step in range(SIDE)]
    same, near, back = y, lax.rem(y + 1, SIDE), lax.rem(y + 3, SIDE)

    def make(z1, y1, z2, y2, tile):
        first = z1 * SIDE + y1 <= z2 * SIDE + y2
        one, two = y1 * SIDE + z1, y2 * SIDE + z2
        return (jnp.where(first, one, two), jnp.where(first, two, one), tile)

    def own(a, b):
        step = (b - a) % SIDE
        return make(z[a], same, z[b], same, 24 + 4 * step + (lax.rem(z[a], 2) if step == 2 else z[a]))

    def side(a, b):
        step = (b - a) % SIDE
        return make(z[a], same, z[b], near, z[a] + (0, 4, 12, 16)[step])

    def across(a):
        return make(z[a], back, z[(a + 1) % SIDE], near, 8 + z[a])

    def level(a):
        return make(a, back, a, near, 20 + a - half)

    def cross(a):
        low = lax.rem(z[a], 2)
        return make(low, back, low + 2, near, 22 + low)

    half = jnp.where(back >= 2, 2, 0)
    early = jnp.where(z[2] == half, half + 1, half)
    late = 2 * half + 1 - early
    return [
        side(0, 0),
        side(0, 3), side(3, 0), side(3, 3), across(3),
        side(1, 1), side(1, 0), side(0, 1), side(1, 3), side(3, 1), across(0), cross(1), level(early),
        side(2, 2), side(2, 3), side(1, 2), across(1), across(2),
        side(2, 0), side(0, 2), side(2, 1), side(3, 2), cross(0), level(late),
        own(0, 0), own(3, 3), own(3, 0), own(1, 1), own(0, 1), own(1, 3),
        own(2, 2), own(1, 2), own(2, 3), own(0, 2),
    ]


def tile_index(a, b):
    za, ya, zb, yb = a >> 2, a & 3, b >> 2, b & 3
    dy, dz, back = (yb - ya) & 3, (zb - za) & 3, (za - zb) & 3
    own = 24 + jnp.where(dz == 2, 8 + (za & 1), jnp.where(dz == 3, 4 + zb, za + 4 * dz))
    right = za + 4 * dz + jnp.where(dz >= 2, 4, 0)
    left = zb + 4 * back + jnp.where(back >= 2, 4, 0)
    far_y = jnp.where((dz == 3) | ((dz == 0) & (za >= 2)), yb, ya)
    far = jnp.where(dz == 1, 8 + za, jnp.where(dz == 3, 8 + zb, jnp.where(dz == 0, 20 + (za & 1), 22 + za)))
    which_y = jnp.where(dy == 2, (far_y + 1) & 3, jnp.where(dy == 3, yb, ya))
    which = jnp.where(dy == 0, own, jnp.where(dy == 1, right, jnp.where(dy == 3, left, far)))
    return jnp.where(a >= 0, which_y * TILES + which, SIDE * TILES)


def kernel(
    x_ref, table_ref, out_ref, blocks, relay, part, pair, xfirst, xlast, total, zpart, zfar, zsum, xfar,
    indices, wanted, pieces, chosen, through, landed,
    local_sem, zs, zr, ys, yr, ps, pr, xs, xr, ws, wr, fs, fr, ts, tr, gs, gr, os, onr,
):
    tm, space = lax.axis_index("tm"), lax.axis_index("space")
    h, y = tm // SIDE, lax.rem(tm, SIDE)
    x, low, core = space // SIDE, lax.rem(space // 2, 2), lax.rem(space, 2)

    def device(h_=h, y_=y, x_=x, low_=low, core_=core):
        return (h_ * SIDE + y_, x_ * SIDE + low_ * 2 + core_)

    def up(value, step, size=SIDE):
        return lax.rem(value + step, size)

    hp, hm, h2 = up(h, 1), up(h, 3), up(h, 2)
    yp, ym = up(y, 1), up(y, 3)
    xp, xm, x2 = up(x, 1), up(x, 3), up(x, 2)
    other = 1 - core
    place = h * 2 + low
    zp, zm = up(place, 1, 8), up(place, 7, 8)
    dev_hp, dev_hm = device(h_=hp), device(h_=hm)
    dev_yp, dev_ym = device(y_=yp), device(y_=ym)
    dev_xp, dev_xm = device(x_=xp), device(x_=xm)
    dev_zp = device(h_=zp // 2, low_=lax.rem(zp, 2))
    dev_zm = device(h_=zm // 2, low_=lax.rem(zm, 2))
    dev_pair = device(core_=other)

    barrier = pltpu.get_barrier_semaphore()
    peers = (dev_hp, dev_hm, device(h_=h2), device(y_=up(y, 2)), dev_yp, dev_ym, dev_xp, dev_xm, dev_zp, dev_zm, dev_pair)
    for peer in peers:
        pl.semaphore_signal(barrier, inc=1, device_id=peer, device_id_type=MESH)
    pl.semaphore_wait(barrier, len(peers))

    started = []

    def send(src, dst, send_sem, recv_sem, peer):
        copy = pltpu.make_async_remote_copy(
            src_ref=src, dst_ref=dst, send_sem=send_sem, recv_sem=recv_sem, device_id=peer, device_id_type=MESH
        )
        copy.start()
        started.append(copy)
        return copy

    def cells(which):
        return pl.ds(pl.multiple_of(which * BLOCK, BLOCK), BLOCK)

    every = slice(None)
    first_rows, last_rows = pl.ds(0, BLOCK // 2), pl.ds(BLOCK // 2, BLOCK // 2)

    local = pltpu.make_async_copy(x_ref.at[:, :, cells(h)], blocks.at[y, h], local_sem)
    local.start()
    comps = range(3)
    to_hp, to_hm, via_hp, via_hm, on_hp, on_hm, moved = {}, {}, {}, {}, {}, {}, {}

    def near(k):
        to_hp[k] = send(x_ref.at[k, :, cells(hp)], blocks.at[y, h, k], zs.at[0, k], zr.at[0, k], dev_hp)
        to_hm[k] = send(x_ref.at[k, :, cells(hm)], blocks.at[y, h, k], zs.at[1, k], zr.at[1, k], dev_hm)

    def away(k):
        via_hp[k] = send(x_ref.at[k, first_rows, cells(h2)], relay.at[0, k], zs.at[2, k], zr.at[2, k], dev_hp)
        via_hm[k] = send(x_ref.at[k, last_rows, cells(h2)], relay.at[1, k], zs.at[3, k], zr.at[3, k], dev_hm)

    def spread(key, z, k, src=None):
        src = blocks.at[y, z, k] if src is None else src
        for way, peer in enumerate((dev_yp, dev_ym)):
            moved[key, k, way] = send(src, blocks.at[y, z, k], ys.at[key, k, way], yr.at[key, k, way], peer)

    def gathered(key):
        for k in comps:
            for way in range(2):
                moved[key, k, way].wait_recv()

    near(0)
    near(1)
    for k in comps:
        spread(0, h, k, x_ref.at[k, :, cells(h)])
    indices[h] = jnp.zeros((8, 128), jnp.int32)
    indices[h, 0:1, 0:SLOTS] = tile_index(table_ref[0, 0:1, :], table_ref[0, 1:2, :])
    told = [
        send(indices.at[h], indices.at[h], ts.at[number], tr.at[number], peer)
        for number, peer in enumerate((dev_hp, dev_hm))
    ]

    def onward(k):
        via_hp[k].wait_recv()
        on_hp[k] = send(relay.at[0, k], blocks.at[y, hm, k, first_rows], zs.at[4, k], zr.at[4, k], dev_hp)
        via_hm[k].wait_recv()
        on_hm[k] = send(relay.at[1, k], blocks.at[y, hp, k, last_rows], zs.at[5, k], zr.at[5, k], dev_hm)

    def spread_far(k):
        on_hp[k].wait_recv()
        on_hm[k].wait_recv()
        spread(3, h2, k)

    tiles = tile_list(h, y)
    starts = [sum(BATCHES[:number]) for number in range(len(BATCHES))]

    def compute(begin, size):
        for slot, (left, right, tile) in enumerate(tiles[begin:begin + size], begin):
            ly, lz, ry, rz = left // SIDE, lax.rem(left, SIDE), right // SIDE, lax.rem(right, SIDE)
            product = None
            for comp in range(3):
                term = lax.dot_general(
                    blocks[ly, lz, comp], blocks[ry, rz, comp], (((1,), (1,)), ((), ())),
                    preferred_element_type=jnp.float32,
                )
                product = term if product is None else product + term
            slot = tile if slot >= NEAR else slot
            for row in range(BLOCK // 8):
                for lane in range(2):
                    place_x, place_low, place_core, place_row = row // 8, row // 4 % 2, row // 2 % 2, row % 2
                    part[slot, place_core, place_x, place_low * 4 + place_row * 2 + lane] = product[
                        row * 8:row * 8 + 8, lane * 128:lane * 128 + 128
                    ]

    def swap(number):
        span = pl.ds(starts[number], BATCHES[number])
        return send(part.at[span, other], pair.at[span], ps.at[number], pr.at[number], dev_pair)

    def begin_batch(number):
        compute(starts[number], BATCHES[number])
        return swap(number)

    def add_pair(number, copy):
        begin, size = starts[number], BATCHES[number]
        copy.wait_recv()

        @pl.loop(begin, begin + size)
        def _(slot):
            part[slot, core] = part[slot, core] + pair[slot]

        if begin == NEAR:
            return None
        span = pl.ds(begin, size)
        return (
            send(part.at[span, core, x2, pl.ds(0, 4)], xfirst.at[0, span], xs.at[number, 0], xr.at[number, 0], dev_xp),
            send(part.at[span, core, x2, pl.ds(4, 4)], xfirst.at[1, span], xs.at[number, 1], xr.at[number, 1], dev_xm),
        )

    def add_first(number, copies):
        begin, size = starts[number], BATCHES[number]
        for copy in copies:
            copy.wait_recv()

        @pl.loop(begin, begin + size)
        def _(slot):
            part[slot, core, xp, 0:4] = part[slot, core, xp, 0:4] + xfirst[0, slot]
            part[slot, core, xm, 4:8] = part[slot, core, xm, 4:8] + xfirst[1, slot]

        span = pl.ds(begin, size)
        return (
            send(part.at[span, core, xp], xlast.at[0, span], xs.at[number, 2], xr.at[number, 2], dev_xp),
            send(part.at[span, core, xm], xlast.at[1, span], xs.at[number, 3], xr.at[number, 3], dev_xm),
        )

    def add_last(number, copies):
        begin, size = starts[number], BATCHES[number]
        for copy in copies:
            copy.wait_recv()
        for slot in range(begin, begin + size):
            total[tiles[slot][2]] = part[slot, core, x] + xlast[0, slot] + xlast[1, slot]

    def piece(step):
        target = up(place, step, 8)
        return lax.rem(target, 2) * 4 + target // 2

    flying = {}

    def pass_on(chunk, way, number):
        begin, size = CHUNKS[chunk]
        hops = 4 if chunk % 2 == way else 3
        if number >= hops:
            return
        distance = hops - number
        which = piece(distance if way == 0 else 8 - distance)
        span, here = pl.ds(begin, size), pl.ds(begin - NEAR, size)
        if number > 0:
            flying[chunk, way].wait_recv()
            part[span, core, :, which] = part[span, core, :, which] + zfar[way, number - 1, here]
        flying[chunk, way] = send(
            part.at[span, core, :, which], zfar.at[way, number, here],
            ws.at[chunk, way, number], wr.at[chunk, way, number], dev_zp if way == 0 else dev_zm,
        )

    def pass_some(chunks, first, number):
        for chunk in chunks:
            pass_on(chunk, (chunk + first) % 2, number)

    def pass_all(chunks, number):
        for first in range(2):
            pass_some(chunks, first, number)

    def arrived(chunk):
        for way in range(2):
            flying[chunk, way].wait_recv()
        return (3, 2) if chunk % 2 == 0 else (2, 3)

    def far_sums():
        for chunk in (4, 5):
            begin, size = CHUNKS[chunk]
            above, below = arrived(chunk)
            here = begin - NEAR
            zsum[here:here + size] = (
                part[begin:begin + size, core, :, piece(0)]
                + zfar[0, above, here:here + size] + zfar[1, below, here:here + size]
            )
        first, rest = pl.ds(0, FAR // 2), pl.ds(FAR // 2, FAR // 2)
        return (
            send(zsum.at[first, x2], xfar.at[0, 0, first], fs.at[0], fr.at[0], dev_xp),
            send(zsum.at[rest, x2], xfar.at[0, 1, rest], fs.at[1], fr.at[1], dev_xm),
        )

    def far_cross(copies):
        middle = FAR // 2
        copies[0].wait_recv()
        zsum[0:middle, xp] = zsum[0:middle, xp] + xfar[0, 0, 0:middle]
        copies[1].wait_recv()
        zsum[middle:FAR, xm] = zsum[middle:FAR, xm] + xfar[0, 1, middle:FAR]
        return (
            send(zsum.at[:, xp], xfar.at[1, 0], fs.at[2], fr.at[2], dev_xp),
            send(zsum.at[:, xm], xfar.at[1, 1], fs.at[3], fr.at[3], dev_xm),
        )

    shared, across_y = {}, {}

    def share(number, value):
        begin, size = SHARES[number]
        span = pl.ds(y * TILES + begin, size)
        pieces[span] = value
        shared[number] = (
            send(pieces.at[span], pieces.at[span], gs.at[number, 0], gr.at[number, 0], dev_yp),
            send(pieces.at[span], pieces.at[span], gs.at[number, 1], gr.at[number, 1], dev_ym),
        )

    next_by, next_two = (dev_zp, dev_zm), (dev_hp, dev_hm)

    def step_on(chunk, way, kind, distance, peer):
        span = pl.ds(*CHUNKS[chunk])
        which = piece(distance if way == 0 else 8 - distance)
        flying[chunk, way, kind] = send(
            total.at[span, which], zpart.at[way, kind, span], ws.at[chunk, way, kind], wr.at[chunk, way, kind], peer
        )

    def launch(chunks):
        for chunk in chunks:
            way = chunk % 2
            step_on(chunk, way, 0, 4, next_two[way])
        for chunk in chunks:
            for way in range(2):
                step_on(chunk, way, 1, 3, next_by[way])
        for chunk in chunks:
            for way in range(2):
                step_on(chunk, way, 2, 1, next_by[way])

    def meet(chunks):
        for chunk in chunks:
            begin, end = CHUNKS[chunk][0], sum(CHUNKS[chunk])
            for way in (1 - chunk % 2, chunk % 2):
                which = piece(2 if way == 0 else 6)
                flying[chunk, way, 1].wait_recv()
                added = total[begin:end, which] + zpart[way, 1, begin:end]
                if chunk % 2 == way:
                    flying[chunk, way, 0].wait_recv()
                    added = added + zpart[way, 0, begin:end]
                total[begin:end, which] = added
                step_on(chunk, way, 3, 2, next_two[way])

    def share_near(number, chunks):
        parts = []
        for chunk in chunks:
            begin, end = CHUNKS[chunk][0], sum(CHUNKS[chunk])
            value = total[begin:end, piece(0)]
            for kind in (2, 3):
                for way in range(2):
                    flying[chunk, way, kind].wait_recv()
                    value = value + zpart[way, kind, begin:end]
            parts.append(value)
        share(number, jnp.concatenate(parts))
        begin, size = SHARES[number]
        span = pl.ds(y * TILES + begin, size)
        across_y[number] = send(
            pieces.at[span], pieces.at[span], gs.at[number, 2], gr.at[number, 2], device(y_=up(y, 2))
        )

    to_hp[0].wait_recv()
    spread(1, hm, 0)
    to_hm[0].wait_recv()
    near(2)
    local.wait()
    gathered(0)
    pair0 = begin_batch(0)
    to_hp[1].wait_recv()
    spread(1, hm, 1)
    to_hm[1].wait_recv()
    away(0)
    spread(2, hp, 0)
    first0 = add_pair(0, pair0)
    last0 = add_first(0, first0)
    to_hp[2].wait_recv()
    spread(1, hm, 2)
    to_hm[2].wait_recv()
    away(1)
    away(2)
    spread(2, hp, 1)
    spread(2, hp, 2)
    onward(0)
    add_last(0, last0)
    told[0].wait_recv()
    told.append(send(indices.at[hm], indices.at[hm], ts.at[2], tr.at[2], dev_hp))
    gathered(1)
    pair1 = begin_batch(1)
    onward(1)
    first1 = add_pair(1, pair1)
    onward(2)
    gathered(2)
    pair2 = begin_batch(2)
    last1 = add_first(1, first1)
    spread_far(0)
    first2 = add_pair(2, pair2)
    spread_far(1)
    compute(NEAR, 6)
    spread_far(2)
    compute(NEAR + 6, 4)
    pair5 = swap(5)
    last2 = add_first(2, first2)
    add_pair(5, pair5)
    pass_all((4, 5), 0)
    add_last(1, last1)
    told[1].wait_recv()
    told[2].wait_recv()
    listed = pltpu.make_async_copy(indices, wanted, local_sem)
    listed.start()
    gathered(3)
    pair3 = begin_batch(3)
    pair4 = begin_batch(4)
    first3 = add_pair(3, pair3)
    pass_some((4, 5), 0, 1)
    first4 = add_pair(4, pair4)
    pass_some((4, 5), 1, 1)
    last3 = add_first(3, first3)
    pass_some((4, 5), 0, 2)
    last4 = add_first(4, first4)
    pass_some((4, 5), 1, 2)
    add_last(2, last2)
    pass_some((4, 5), 0, 3)
    add_last(3, last3)
    launch((0, 1))
    far = far_sums()
    meet((0, 1))
    add_last(4, last4)
    launch((2, 3))
    far = far_cross(far)
    meet((2, 3))
    for copy in far:
        copy.wait_recv()
    share(0, zsum[:, x] + xfar[1, 0] + xfar[1, 1])
    share_near(1, (0, 1))
    share_near(2, (2, 3))

    pieces[SIDE * TILES] = jnp.zeros((8, 128), jnp.float32)
    onto = {}
    for chunk, (begin, size) in enumerate(SHARES):
        half = size // 2
        to_yp, to_ym = shared[chunk]
        if chunk > 0:
            to_yp.wait_recv()
            to_ym.wait_recv()
            onto[chunk] = (across_y[chunk],)
            continue
        to_yp.wait_recv()
        early = pl.ds(ym * TILES + begin, half)
        on_yp = send(pieces.at[early], pieces.at[early], gs.at[chunk, 2], gr.at[chunk, 2], dev_yp)
        to_ym.wait_recv()
        late = pl.ds(yp * TILES + begin + half, half)
        on_ym = send(pieces.at[late], pieces.at[late], gs.at[chunk, 3], gr.at[chunk, 3], dev_ym)
        onto[chunk] = (on_yp, on_ym)
    for chunk in range(len(SHARES)):
        for copy in onto[chunk]:
            copy.wait_recv()

    listed.wait()

    def choose(number, z):
        for slot in range(SLOTS):
            chosen[number, slot] = pieces[wanted[z, 0, slot]]

    half = SLOTS // 2
    choose(2, h2)
    last_hp = send(chosen.at[2, pl.ds(0, half)], landed.at[2, pl.ds(0, half)], os.at[2], onr.at[2], device(h_=h2))
    last_hm = send(chosen.at[2, pl.ds(half, half)], landed.at[2, pl.ds(half, half)], os.at[3], onr.at[3], device(h_=h2))
    choose(0, hp)
    out_hp = send(chosen.at[0], landed.at[0], os.at[0], onr.at[0], dev_hp)
    choose(1, hm)
    out_hm = send(chosen.at[1], landed.at[1], os.at[1], onr.at[1], dev_hm)

    def put(z, slot, value):
        rows, lanes = pl.multiple_of(z // 2 * 8, 8), pl.multiple_of(lax.rem(z, 2) * 128, 128)
        out_ref[0, slot, pl.ds(rows, 8), pl.ds(lanes, 128)] = value

    for slot in range(SLOTS):
        put(h, slot, pieces[wanted[h, 0, slot]])
    out_hp.wait_recv()
    for slot in range(SLOTS):
        put(hm, slot, landed[0, slot])
    out_hm.wait_recv()
    for slot in range(SLOTS):
        put(hp, slot, landed[1, slot])
    last_hp.wait_recv()
    last_hm.wait_recv()
    for slot in range(SLOTS):
        put(h2, slot, landed[2, slot])
    for copy in started:
        copy.wait_send()


def gram(snapshots, table):
    count = len(BATCHES)
    dma = pltpu.SemaphoreType.DMA
    f32, b16 = jnp.float32, jnp.bfloat16
    return pl.pallas_call(
        kernel,
        out_shape=jax.ShapeDtypeStruct((1, SLOTS, 16, BLOCK), f32),
        in_specs=[pl.BlockSpec(memory_space=pltpu.HBM), pl.BlockSpec(memory_space=pltpu.VMEM)],
        out_specs=pl.BlockSpec(memory_space=pltpu.VMEM),
        scratch_shapes=[
            pltpu.VMEM((4, 4, 3, BLOCK, BLOCK), b16),
            pltpu.VMEM((2, 3, BLOCK // 2, BLOCK), b16),
            pltpu.VMEM((TILES, 2, 4, 8, 8, 128), f32),
            pltpu.VMEM((TILES, 4, 8, 8, 128), f32),
            pltpu.VMEM((2, NEAR, 4, 8, 128), f32),
            pltpu.VMEM((2, NEAR, 8, 8, 128), f32),
            pltpu.VMEM((NEAR, 8, 8, 128), f32),
            pltpu.VMEM((2, 4, NEAR, 8, 128), f32),
            pltpu.VMEM((2, 4, FAR, 4, 8, 128), f32),
            pltpu.VMEM((FAR, 4, 8, 128), f32),
            pltpu.VMEM((2, 2, FAR, 8, 128), f32),
            pltpu.VMEM((SIDE, 8, 128), jnp.int32),
            pltpu.SMEM((SIDE, 8, 128), jnp.int32),
            pltpu.VMEM((SIDE * TILES + 1, 8, 128), f32),
            pltpu.VMEM((3, SLOTS, 8, 128), f32),
            pltpu.VMEM((2, SLOTS // 2, 8, 128), f32),
            pltpu.VMEM((3, SLOTS, 8, 128), f32),
            dma(()), dma((6, 3)), dma((6, 3)), dma((4, 3, 2)), dma((4, 3, 2)), dma((count,)), dma((count,)),
            dma((count, 4)), dma((count, 4)), dma((6, 2, 4)), dma((6, 2, 4)), dma((4,)), dma((4,)),
            dma((3,)), dma((3,)), dma((3, 4)), dma((3, 4)), dma((6,)), dma((6,)),
        ],
        compiler_params=pltpu.CompilerParams(collective_id=0, has_side_effects=True, vmem_limit_bytes=30 * 2**20),
        name="gram_tiles",
    )(snapshots, table)


def per_device(snapshots, tile_table):
    scale = 1.0 / math.sqrt(3 * snapshots.shape[2] * lax.axis_size("space"))
    return gram(snapshots, jnp.transpose(tile_table, (0, 2, 1))) * scale


def solution(mesh):
    in_specs = (P(None, "tm", "space"), P("tm", None, None))
    out_specs = P("tm", None, "space", None)
    return jax.shard_map(
        per_device, mesh=mesh, in_specs=in_specs, out_specs=out_specs, check_vma=False
    )
```

```python
import math

import jax
import jax.numpy as jnp
from jax import lax
from jax.experimental import pallas as pl
from jax.experimental.pallas import tpu as pltpu
from jax.sharding import PartitionSpec as P

MESH = pl.DeviceIdType.MESH
BLOCK = 256
SIDE = 4
SLOTS = 20
TILES = 34
BATCHES = (1, 4, 8, 5, 6, 10)
NEAR, FAR = 24, 10
CHUNKS = ((0, 6), (6, 6), (12, 6), (18, 6), (24, 5), (29, 5))
SHARES = ((24, 10), (0, 12), (12, 12))


def tile_list(h, y):
    z = [lax.rem(h + step, SIDE) for step in range(SIDE)]
    same, near, back = y, lax.rem(y + 1, SIDE), lax.rem(y + 3, SIDE)

    def make(z1, y1, z2, y2, tile):
        first = z1 * SIDE + y1 <= z2 * SIDE + y2
        one, two = y1 * SIDE + z1, y2 * SIDE + z2
        return (jnp.where(first, one, two), jnp.where(first, two, one), tile)

    def own(a, b):
        step = (b - a) % SIDE
        return make(z[a], same, z[b], same, 24 + 4 * step + (lax.rem(z[a], 2) if step == 2 else z[a]))

    def side(a, b):
        step = (b - a) % SIDE
        return make(z[a], same, z[b], near, z[a] + (0, 4, 12, 16)[step])

    def across(a):
        return make(z[a], back, z[(a + 1) % SIDE], near, 8 + z[a])

    def level(a):
        return make(a, back, a, near, 20 + a - half)

    def cross(a):
        low = lax.rem(z[a], 2)
        return make(low, back, low + 2, near, 22 + low)

    half = jnp.where(back >= 2, 2, 0)
    early = jnp.where(z[2] == half, half + 1, half)
    late = 2 * half + 1 - early
    return [
        side(0, 0),
        side(0, 3), side(3, 0), side(3, 3), across(3),
        side(1, 1), side(1, 0), side(0, 1), side(1, 3), side(3, 1), across(0), cross(1), level(early),
        side(2, 2), side(2, 3), side(1, 2), across(1), across(2),
        side(2, 0), side(0, 2), side(2, 1), side(3, 2), cross(0), level(late),
        own(0, 0), own(3, 3), own(3, 0), own(1, 1), own(0, 1), own(1, 3),
        own(2, 2), own(1, 2), own(2, 3), own(0, 2),
    ]


def tile_index(a, b):
    za, ya, zb, yb = a >> 2, a & 3, b >> 2, b & 3
    dy, dz, back = (yb - ya) & 3, (zb - za) & 3, (za - zb) & 3
    own = 24 + jnp.where(dz == 2, 8 + (za & 1), jnp.where(dz == 3, 4 + zb, za + 4 * dz))
    right = za + 4 * dz + jnp.where(dz >= 2, 4, 0)
    left = zb + 4 * back + jnp.where(back >= 2, 4, 0)
    far_y = jnp.where((dz == 3) | ((dz == 0) & (za >= 2)), yb, ya)
    far = jnp.where(dz == 1, 8 + za, jnp.where(dz == 3, 8 + zb, jnp.where(dz == 0, 20 + (za & 1), 22 + za)))
    which_y = jnp.where(dy == 2, (far_y + 1) & 3, jnp.where(dy == 3, yb, ya))
    which = jnp.where(dy == 0, own, jnp.where(dy == 1, right, jnp.where(dy == 3, left, far)))
    return jnp.where(a >= 0, which_y * TILES + which, SIDE * TILES)


def kernel(
    x_ref, table_ref, out_ref, blocks, relay, part, pair, xfirst, xlast, total, zpart, zfar, zsum, xfar,
    indices, wanted, pieces, chosen, through, landed,
    local_sem, zs, zr, ys, yr, ps, pr, xs, xr, ws, wr, fs, fr, ts, tr, gs, gr, os, onr,
):
    tm, space = lax.axis_index("tm"), lax.axis_index("space")
    h, y = tm // SIDE, lax.rem(tm, SIDE)
    x, low, core = space // SIDE, lax.rem(space // 2, 2), lax.rem(space, 2)

    def device(h_=h, y_=y, x_=x, low_=low, core_=core):
        return (h_ * SIDE + y_, x_ * SIDE + low_ * 2 + core_)

    def up(value, step, size=SIDE):
        return lax.rem(value + step, size)

    hp, hm, h2 = up(h, 1), up(h, 3), up(h, 2)
    yp, ym = up(y, 1), up(y, 3)
    xp, xm, x2 = up(x, 1), up(x, 3), up(x, 2)
    other = 1 - core
    place = h * 2 + low
    zp, zm = up(place, 1, 8), up(place, 7, 8)
    dev_hp, dev_hm = device(h_=hp), device(h_=hm)
    dev_yp, dev_ym = device(y_=yp), device(y_=ym)
    dev_xp, dev_xm = device(x_=xp), device(x_=xm)
    dev_zp = device(h_=zp // 2, low_=lax.rem(zp, 2))
    dev_zm = device(h_=zm // 2, low_=lax.rem(zm, 2))
    dev_pair = device(core_=other)

    barrier = pltpu.get_barrier_semaphore()
    peers = (dev_hp, dev_hm, device(h_=h2), device(y_=up(y, 2)), dev_yp, dev_ym, dev_xp, dev_xm, dev_zp, dev_zm, dev_pair)
    for peer in peers:
        pl.semaphore_signal(barrier, inc=1, device_id=peer, device_id_type=MESH)
    pl.semaphore_wait(barrier, len(peers))

    started = []

    def send(src, dst, send_sem, recv_sem, peer):
        copy = pltpu.make_async_remote_copy(
            src_ref=src, dst_ref=dst, send_sem=send_sem, recv_sem=recv_sem, device_id=peer, device_id_type=MESH
        )
        copy.start()
        started.append(copy)
        return copy

    def cells(which):
        return pl.ds(pl.multiple_of(which * BLOCK, BLOCK), BLOCK)

    every = slice(None)
    first_rows, last_rows = pl.ds(0, BLOCK // 2), pl.ds(BLOCK // 2, BLOCK // 2)

    local = pltpu.make_async_copy(x_ref.at[:, :, cells(h)], blocks.at[y, h], local_sem)
    local.start()
    comps = range(3)
    to_hp, to_hm, via_hp, via_hm, on_hp, on_hm, moved = {}, {}, {}, {}, {}, {}, {}

    def near(k):
        to_hp[k] = send(x_ref.at[k, :, cells(hp)], blocks.at[y, h, k], zs.at[0, k], zr.at[0, k], dev_hp)
        to_hm[k] = send(x_ref.at[k, :, cells(hm)], blocks.at[y, h, k], zs.at[1, k], zr.at[1, k], dev_hm)

    def away(k):
        via_hp[k] = send(x_ref.at[k, first_rows, cells(h2)], relay.at[0, k], zs.at[2, k], zr.at[2, k], dev_hp)
        via_hm[k] = send(x_ref.at[k, last_rows, cells(h2)], relay.at[1, k], zs.at[3, k], zr.at[3, k], dev_hm)

    def spread(key, z, k, src=None):
        src = blocks.at[y, z, k] if src is None else src
        for way, peer in enumerate((dev_yp, dev_ym)):
            moved[key, k, way] = send(src, blocks.at[y, z, k], ys.at[key, k, way], yr.at[key, k, way], peer)

    def gathered(key):
        for k in comps:
            for way in range(2):
                moved[key, k, way].wait_recv()

    near(0)
    near(1)
    for k in comps:
        spread(0, h, k, x_ref.at[k, :, cells(h)])
    indices[h] = jnp.zeros((8, 128), jnp.int32)
    indices[h, 0:1, 0:SLOTS] = tile_index(table_ref[0, 0:1, :], table_ref[0, 1:2, :])
    told = [
        send(indices.at[h], indices.at[h], ts.at[number], tr.at[number], peer)
        for number, peer in enumerate((dev_hp, dev_hm))
    ]

    def onward(k):
        via_hp[k].wait_recv()
        on_hp[k] = send(relay.at[0, k], blocks.at[y, hm, k, first_rows], zs.at[4, k], zr.at[4, k], dev_hp)
        via_hm[k].wait_recv()
        on_hm[k] = send(relay.at[1, k], blocks.at[y, hp, k, last_rows], zs.at[5, k], zr.at[5, k], dev_hm)

    def spread_far(k):
        on_hp[k].wait_recv()
        on_hm[k].wait_recv()
        spread(3, h2, k)

    tiles = tile_list(h, y)
    starts = [sum(BATCHES[:number]) for number in range(len(BATCHES))]

    def compute(begin, size):
        for slot, (left, right, tile) in enumerate(tiles[begin:begin + size], begin):
            ly, lz, ry, rz = left // SIDE, lax.rem(left, SIDE), right // SIDE, lax.rem(right, SIDE)
            product = None
            for comp in range(3):
                term = lax.dot_general(
                    blocks[ly, lz, comp], blocks[ry, rz, comp], (((1,), (1,)), ((), ())),
                    preferred_element_type=jnp.float32,
                )
                product = term if product is None else product + term
            slot = tile if slot >= NEAR else slot
            for row in range(BLOCK // 8):
                for lane in range(2):
                    place_x, place_low, place_core, place_row = row // 8, row // 4 % 2, row // 2 % 2, row % 2
                    part[slot, place_core, place_x, place_low * 4 + place_row * 2 + lane] = product[
                        row * 8:row * 8 + 8, lane * 128:lane * 128 + 128
                    ]

    def swap(number):
        span = pl.ds(starts[number], BATCHES[number])
        return send(part.at[span, other], pair.at[span], ps.at[number], pr.at[number], dev_pair)

    def begin_batch(number):
        compute(starts[number], BATCHES[number])
        return swap(number)

    def add_pair(number, copy):
        begin, size = starts[number], BATCHES[number]
        copy.wait_recv()

        @pl.loop(begin, begin + size)
        def _(slot):
            part[slot, core] = part[slot, core] + pair[slot]

        if begin == NEAR:
            return None
        span = pl.ds(begin, size)
        return (
            send(part.at[span, core, x2, pl.ds(0, 4)], xfirst.at[0, span], xs.at[number, 0], xr.at[number, 0], dev_xp),
            send(part.at[span, core, x2, pl.ds(4, 4)], xfirst.at[1, span], xs.at[number, 1], xr.at[number, 1], dev_xm),
        )

    def add_first(number, copies):
        begin, size = starts[number], BATCHES[number]
        for copy in copies:
            copy.wait_recv()

        @pl.loop(begin, begin + size)
        def _(slot):
            part[slot, core, xp, 0:4] = part[slot, core, xp, 0:4] + xfirst[0, slot]
            part[slot, core, xm, 4:8] = part[slot, core, xm, 4:8] + xfirst[1, slot]

        span = pl.ds(begin, size)
        return (
            send(part.at[span, core, xp], xlast.at[0, span], xs.at[number, 2], xr.at[number, 2], dev_xp),
            send(part.at[span, core, xm], xlast.at[1, span], xs.at[number, 3], xr.at[number, 3], dev_xm),
        )

    def add_last(number, copies):
        begin, size = starts[number], BATCHES[number]
        for copy in copies:
            copy.wait_recv()
        for slot in range(begin, begin + size):
            total[tiles[slot][2]] = part[slot, core, x] + xlast[0, slot] + xlast[1, slot]

    def piece(step):
        target = up(place, step, 8)
        return lax.rem(target, 2) * 4 + target // 2

    flying = {}

    def pass_on(chunk, way, number):
        begin, size = CHUNKS[chunk]
        hops = 4 if chunk % 2 == way else 3
        if number >= hops:
            return
        distance = hops - number
        which = piece(distance if way == 0 else 8 - distance)
        span, here = pl.ds(begin, size), pl.ds(begin - NEAR, size)
        if number > 0:
            flying[chunk, way].wait_recv()
            part[span, core, :, which] = part[span, core, :, which] + zfar[way, number - 1, here]
        flying[chunk, way] = send(
            part.at[span, core, :, which], zfar.at[way, number, here],
            ws.at[chunk, way, number], wr.at[chunk, way, number], dev_zp if way == 0 else dev_zm,
        )

    def pass_some(chunks, first, number):
        for chunk in chunks:
            pass_on(chunk, (chunk + first) % 2, number)

    def pass_all(chunks, number):
        for first in range(2):
            pass_some(chunks, first, number)

    def arrived(chunk):
        for way in range(2):
            flying[chunk, way].wait_recv()
        return (3, 2) if chunk % 2 == 0 else (2, 3)

    def far_sums():
        for chunk in (4, 5):
            begin, size = CHUNKS[chunk]
            above, below = arrived(chunk)
            here = begin - NEAR
            zsum[here:here + size] = (
                part[begin:begin + size, core, :, piece(0)]
                + zfar[0, above, here:here + size] + zfar[1, below, here:here + size]
            )
        first, rest = pl.ds(0, FAR // 2), pl.ds(FAR // 2, FAR // 2)
        return (
            send(zsum.at[first, x2], xfar.at[0, 0, first], fs.at[0], fr.at[0], dev_xp),
            send(zsum.at[rest, x2], xfar.at[0, 1, rest], fs.at[1], fr.at[1], dev_xm),
        )

    def far_cross(copies):
        middle = FAR // 2
        copies[0].wait_recv()
        zsum[0:middle, xp] = zsum[0:middle, xp] + xfar[0, 0, 0:middle]
        copies[1].wait_recv()
        zsum[middle:FAR, xm] = zsum[middle:FAR, xm] + xfar[0, 1, middle:FAR]
        return (
            send(zsum.at[:, xp], xfar.at[1, 0], fs.at[2], fr.at[2], dev_xp),
            send(zsum.at[:, xm], xfar.at[1, 1], fs.at[3], fr.at[3], dev_xm),
        )

    shared, across_y = {}, {}

    def share(number, value):
        begin, size = SHARES[number]
        span = pl.ds(y * TILES + begin, size)
        pieces[span] = value
        shared[number] = (
            send(pieces.at[span], pieces.at[span], gs.at[number, 0], gr.at[number, 0], dev_yp),
            send(pieces.at[span], pieces.at[span], gs.at[number, 1], gr.at[number, 1], dev_ym),
        )
        across_y[number] = send(
            pieces.at[span], pieces.at[span], gs.at[number, 2], gr.at[number, 2], device(y_=up(y, 2))
        )

    next_by, next_two = (dev_zp, dev_zm), (dev_hp, dev_hm)

    def step_on(chunk, way, kind, distance, peer):
        span = pl.ds(*CHUNKS[chunk])
        which = piece(distance if way == 0 else 8 - distance)
        flying[chunk, way, kind] = send(
            total.at[span, which], zpart.at[way, kind, span], ws.at[chunk, way, kind], wr.at[chunk, way, kind], peer
        )

    def launch(chunks):
        for chunk in chunks:
            way = chunk % 2
            step_on(chunk, way, 0, 4, next_two[way])
        for chunk in chunks:
            for way in range(2):
                step_on(chunk, way, 1, 3, next_by[way])
        for chunk in chunks:
            for way in range(2):
                step_on(chunk, way, 2, 1, next_by[way])

    def meet(chunks):
        for chunk in chunks:
            begin, end = CHUNKS[chunk][0], sum(CHUNKS[chunk])
            for way in (1 - chunk % 2, chunk % 2):
                which = piece(2 if way == 0 else 6)
                flying[chunk, way, 1].wait_recv()
                added = total[begin:end, which] + zpart[way, 1, begin:end]
                if chunk % 2 == way:
                    flying[chunk, way, 0].wait_recv()
                    added = added + zpart[way, 0, begin:end]
                total[begin:end, which] = added
                step_on(chunk, way, 3, 2, next_two[way])

    def share_near(number, chunks):
        parts = []
        for chunk in chunks:
            begin, end = CHUNKS[chunk][0], sum(CHUNKS[chunk])
            value = total[begin:end, piece(0)]
            for kind in (2, 3):
                for way in range(2):
                    flying[chunk, way, kind].wait_recv()
                    value = value + zpart[way, kind, begin:end]
            parts.append(value)
        share(number, jnp.concatenate(parts))

    to_hp[0].wait_recv()
    spread(1, hm, 0)
    to_hm[0].wait_recv()
    near(2)
    local.wait()
    gathered(0)
    pair0 = begin_batch(0)
    to_hp[1].wait_recv()
    spread(1, hm, 1)
    to_hm[1].wait_recv()
    away(0)
    spread(2, hp, 0)
    first0 = add_pair(0, pair0)
    last0 = add_first(0, first0)
    to_hp[2].wait_recv()
    spread(1, hm, 2)
    to_hm[2].wait_recv()
    away(1)
    away(2)
    spread(2, hp, 1)
    spread(2, hp, 2)
    onward(0)
    add_last(0, last0)
    told[0].wait_recv()
    told.append(send(indices.at[hm], indices.at[hm], ts.at[2], tr.at[2], dev_hp))
    gathered(1)
    pair1 = begin_batch(1)
    onward(1)
    first1 = add_pair(1, pair1)
    onward(2)
    gathered(2)
    pair2 = begin_batch(2)
    last1 = add_first(1, first1)
    spread_far(0)
    first2 = add_pair(2, pair2)
    spread_far(1)
    compute(NEAR, 6)
    spread_far(2)
    compute(NEAR + 6, 4)
    pair5 = swap(5)
    last2 = add_first(2, first2)
    add_pair(5, pair5)
    pass_all((4, 5), 0)
    add_last(1, last1)
    told[1].wait_recv()
    told[2].wait_recv()
    listed = pltpu.make_async_copy(indices, wanted, local_sem)
    listed.start()
    gathered(3)
    pair3 = begin_batch(3)
    pair4 = begin_batch(4)
    first3 = add_pair(3, pair3)
    pass_some((4, 5), 0, 1)
    first4 = add_pair(4, pair4)
    pass_some((4, 5), 1, 1)
    last3 = add_first(3, first3)
    pass_some((4, 5), 0, 2)
    last4 = add_first(4, first4)
    pass_some((4, 5), 1, 2)
    add_last(2, last2)
    pass_some((4, 5), 0, 3)
    add_last(3, last3)
    launch((0, 1))
    far = far_sums()
    meet((0, 1))
    add_last(4, last4)
    launch((2, 3))
    far = far_cross(far)
    meet((2, 3))
    for copy in far:
        copy.wait_recv()
    share(0, zsum[:, x] + xfar[1, 0] + xfar[1, 1])
    share_near(1, (0, 1))
    share_near(2, (2, 3))

    pieces[SIDE * TILES] = jnp.zeros((8, 128), jnp.float32)
    for number in range(len(SHARES)):
        for copy in shared[number] + (across_y[number],):
            copy.wait_recv()
    listed.wait()

    def choose(number, z):
        for slot in range(SLOTS):
            chosen[number, slot] = pieces[wanted[z, 0, slot]]

    half = SLOTS // 2
    choose(2, h2)
    last_hp = send(chosen.at[2, pl.ds(0, half)], landed.at[2, pl.ds(0, half)], os.at[2], onr.at[2], device(h_=h2))
    last_hm = send(chosen.at[2, pl.ds(half, half)], landed.at[2, pl.ds(half, half)], os.at[3], onr.at[3], device(h_=h2))
    choose(0, hp)
    out_hp = send(chosen.at[0], landed.at[0], os.at[0], onr.at[0], dev_hp)
    choose(1, hm)
    out_hm = send(chosen.at[1], landed.at[1], os.at[1], onr.at[1], dev_hm)

    def put(z, slot, value):
        rows, lanes = pl.multiple_of(z // 2 * 8, 8), pl.multiple_of(lax.rem(z, 2) * 128, 128)
        out_ref[0, slot, pl.ds(rows, 8), pl.ds(lanes, 128)] = value

    for slot in range(SLOTS):
        put(h, slot, pieces[wanted[h, 0, slot]])
    out_hp.wait_recv()
    for slot in range(SLOTS):
        put(hm, slot, landed[0, slot])
    out_hm.wait_recv()
    for slot in range(SLOTS):
        put(hp, slot, landed[1, slot])
    last_hp.wait_recv()
    last_hm.wait_recv()
    for slot in range(SLOTS):
        put(h2, slot, landed[2, slot])
    for copy in started:
        copy.wait_send()


def gram(snapshots, table):
    count = len(BATCHES)
    dma = pltpu.SemaphoreType.DMA
    f32, b16 = jnp.float32, jnp.bfloat16
    return pl.pallas_call(
        kernel,
        out_shape=jax.ShapeDtypeStruct((1, SLOTS, 16, BLOCK), f32),
        in_specs=[pl.BlockSpec(memory_space=pltpu.HBM), pl.BlockSpec(memory_space=pltpu.VMEM)],
        out_specs=pl.BlockSpec(memory_space=pltpu.VMEM),
        scratch_shapes=[
            pltpu.VMEM((4, 4, 3, BLOCK, BLOCK), b16),
            pltpu.VMEM((2, 3, BLOCK // 2, BLOCK), b16),
            pltpu.VMEM((TILES, 2, 4, 8, 8, 128), f32),
            pltpu.VMEM((TILES, 4, 8, 8, 128), f32),
            pltpu.VMEM((2, NEAR, 4, 8, 128), f32),
            pltpu.VMEM((2, NEAR, 8, 8, 128), f32),
            pltpu.VMEM((NEAR, 8, 8, 128), f32),
            pltpu.VMEM((2, 4, NEAR, 8, 128), f32),
            pltpu.VMEM((2, 4, FAR, 4, 8, 128), f32),
            pltpu.VMEM((FAR, 4, 8, 128), f32),
            pltpu.VMEM((2, 2, FAR, 8, 128), f32),
            pltpu.VMEM((SIDE, 8, 128), jnp.int32),
            pltpu.SMEM((SIDE, 8, 128), jnp.int32),
            pltpu.VMEM((SIDE * TILES + 1, 8, 128), f32),
            pltpu.VMEM((3, SLOTS, 8, 128), f32),
            pltpu.VMEM((2, SLOTS // 2, 8, 128), f32),
            pltpu.VMEM((3, SLOTS, 8, 128), f32),
            dma(()), dma((6, 3)), dma((6, 3)), dma((4, 3, 2)), dma((4, 3, 2)), dma((count,)), dma((count,)),
            dma((count, 4)), dma((count, 4)), dma((6, 2, 4)), dma((6, 2, 4)), dma((4,)), dma((4,)),
            dma((3,)), dma((3,)), dma((3, 4)), dma((3, 4)), dma((6,)), dma((6,)),
        ],
        compiler_params=pltpu.CompilerParams(collective_id=0, has_side_effects=True, vmem_limit_bytes=30 * 2**20),
        name="gram_tiles",
    )(snapshots, table)


def per_device(snapshots, tile_table):
    scale = 1.0 / math.sqrt(3 * snapshots.shape[2] * lax.axis_size("space"))
    return gram(snapshots, jnp.transpose(tile_table, (0, 2, 1))) * scale


def solution(mesh):
    in_specs = (P(None, "tm", "space"), P("tm", None, None))
    out_specs = P("tm", None, "space", None)
    return jax.shard_map(
        per_device, mesh=mesh, in_specs=in_specs, out_specs=out_specs, check_vma=False
    )
```
